32 devices in a mesh: row: 8 (over z, y), col: 4 (over x, core).
Axes of the slice: x: 2, y: 2, z: 4, core: 2. Of those that a mesh axis runs over, the one named last changes fastest.
Arguments:
- tokens: bfloat16 [16384, 1024], P('row', 'col'), may hold values from -6 to 6
- segments: int32 [16, 1024], P('row'), may hold values from 0 to 7, never falling along the last dimension, each value on 1 to 256 neighbouring positions
- wqkv: bfloat16 [1024, 3072], P('row', 'col'), may hold values from -0.1875 to 0.1875
- bias_qv: bfloat16 [2048], P('col'), may hold values from -3 to 3
- wo: bfloat16 [1024, 1024], P('col', 'row'), may hold values from -1.5 to 1.5
- bias_o: bfloat16 [1024], P('col'), may hold values from -3 to 3
- gain_a: bfloat16 [1024], P('col'), may hold values from 0.099609375 to 1.8984375
- shift_a: bfloat16 [1024], P('col'), may hold values from -3 to 3
- w_in: bfloat16 [1024, 4096], P('row', 'col'), may hold values from -0.1875 to 0.1875
- bias_in: bfloat16 [4096], P('col'), may hold values from -3 to 3
- w_out: bfloat16 [4096, 1024], P('col', 'row'), may hold values from -0.1875 to 0.1875
- bias_out: bfloat16 [1024], P('col'), may hold values from -3 to 3
- gain_b: bfloat16 [1024], P('col'), may hold values from 0.099609375 to 1.8984375
- shift_b: bfloat16 [1024], P('col'), may hold values from -3 to 3
- cotangent: bfloat16 [16384, 1024], P('row', 'col'), may hold values from -6 to 6
Outputs:
- output: bfloat16 [16384, 1024], P('row', 'col')
- grad_tokens: float32 [16384, 1024], P('row', 'col')
- grad_wqkv: float32 [1024, 3072], P('row', 'col')
- grad_bias_qv: float32 [2048], P('col')
- grad_wo: float32 [1024, 1024], P('col', 'row')
- grad_bias_o: float32 [1024], P('col')
- grad_gain_a: float32 [1024], P('col')
- grad_shift_a: float32 [1024], P('col')
- grad_w_in: float32 [1024, 4096], P('row', 'col')
- grad_bias_in: float32 [4096], P('col')
- grad_w_out: float32 [4096, 1024], P('col', 'row')
- grad_bias_out: float32 [1024], P('col')
- grad_gain_b: float32 [1024], P('col')
- grad_shift_b: float32 [1024], P('col')
The draws below stay inside these ranges and needn't reach their ends.
Inputs may be any that keep to these rules, and one draw needn't show every extreme that they name: `segments`: within each sequence the document numbers never fall and each of the 8 documents has 1 to 256 tokens; each sequence has one document of exactly 256 tokens.
All inputs are finite; a program needn't handle non-finite values.
Results may differ from the reference program's by a relative error of at most 0.017.
Values may be sent and summed in bfloat16 or wider, within the bound.
No kernel may reach another device: no remote copies, remote signals or barrier semaphores. Data moves between devices by JAX's collectives and lax.ppermute only.
A program may use at most 128 MiB of HBM per device.

```python
import math
import jax
import jax.numpy as jnp
import numpy as np
from jax import lax

D = 1024
HEADS = 16
DH = 64
FF = 4096
SEQ = 1024
DOCS = 8
SEQS = 16
TOKENS = 16384


def steps_of(key, shape, split, low, top_value):
    level = 1.0
    for position, shards_of in split:
        steps = jax.random.uniform(jax.random.fold_in(jax.random.fold_in(key, 6), position), (shards_of,), jnp.float32, low / len(split), top_value / len(split))
        level = level * jnp.repeat(jnp.exp(steps), shape[position] // shards_of).reshape((-1,) + (1,) * (len(shape) - 1 - position))
    return level


def profile(count, total, limit, skew):
    loads = [(1 << 20) // math.isqrt(grade ** skew) + 1 for grade in range(2, count + 1)]
    surplus, counts = total - limit - (count - 1), [1] * (count - 1)
    while surplus > 0:
        free = [i for i in range(count - 1) if counts[i] < limit]
        mass, budget = sum([loads[i] for i in free]), surplus
        for i in free:
            more = min(limit - counts[i], max(1, budget * loads[i] // mass), surplus)
            counts[i] = counts[i] + more
            surplus = surplus - more
    return np.array([limit] + counts)


def uneven(key, number_of, total, bound, skew):
    if number_of == 2:
        one = jax.random.randint(key, (), max(1, total - bound), min(bound, total - 1) + 1)
        return jnp.stack([one, total - one])
    lengths = jnp.asarray(profile(number_of, total, bound, skew), jnp.int32)
    twos = (number_of - 1) // 2
    giver, receiver = lengths[1:1 + 2 * twos:2], lengths[2:2 + 2 * twos:2]
    margin = jnp.minimum(giver - 1, bound - receiver)
    passed = jax.random.randint(jax.random.fold_in(key, 1), (twos,), 0, 1 << 20) % (margin + 1)
    lengths = lengths.at[1:1 + 2 * twos:2].set(giver - passed).at[2:2 + 2 * twos:2].set(receiver + passed)
    return lengths[jax.random.permutation(jax.random.fold_in(key, 2), number_of)]


def scatter_about(stream_key, shape, spread, bound, shards=(), kind=jnp.bfloat16):
    array = spread * jax.random.normal(stream_key, shape, jnp.float32)
    if shards:
        array = array * steps_of(stream_key, shape, shards, -0.22, 0.18)
    return jnp.clip(array, -bound, bound).astype(kind)


def setup_inputs(seed: int = 0) -> dict:
    key_list = jax.random.split(jax.random.key(seed), 16)
    tokens = scatter_about(key_list[0], (TOKENS, D), 1.0, 6.0, ((0, 8), (1, 4)))
    segments = jax.vmap(lambda own: jnp.searchsorted(jnp.cumsum(uneven(own, DOCS, SEQ, SEQ // 4, 2)), jnp.arange(SEQ), side="right"))(jax.random.split(key_list[1], SEQS)).reshape((SEQS, SEQ)).astype(jnp.int32)
    wqkv = scatter_about(key_list[2], (D, 3 * D), D ** -0.5, 0.1875, ((0, 8), (1, 4)))
    bias_qv = scatter_about(key_list[3], (2 * D,), 0.5, 3.0, ((0, 4),))
    wo = scatter_about(key_list[4], (D, D), (D // 64) ** -0.5, 1.5, ((0, 4), (1, 8)))
    bias_o = scatter_about(key_list[5], (D,), 0.5, 3.0, ((0, 4),))
    gain_a = jnp.clip(1.0 + 0.18 * jax.random.normal(key_list[6], (D,), jnp.float32), 0.099609375, 1.8984375).astype(jnp.bfloat16)
    shift_a = scatter_about(key_list[7], (D,), 0.5, 3.0, ((0, 4),))
    w_in = scatter_about(key_list[8], (D, FF), D ** -0.5, 0.1875, ((0, 8), (1, 4)))
    bias_in = scatter_about(key_list[9], (FF,), 0.5, 3.0, ((0, 4),))
    w_out = scatter_about(key_list[10], (FF, D), (FF // 4) ** -0.5, 0.1875, ((0, 4), (1, 8)))
    bias_out = scatter_about(key_list[11], (D,), 0.5, 3.0, ((0, 4),))
    gain_b = jnp.clip(1.0 + 0.18 * jax.random.normal(key_list[12], (D,), jnp.float32), 0.099609375, 1.8984375).astype(jnp.bfloat16)
    shift_b = scatter_about(key_list[13], (D,), 0.5, 3.0, ((0, 4),))
    cotangent = scatter_about(key_list[14], (TOKENS, D), 1.0, 6.0, ((0, 8), (1, 4)))
    return dict(tokens=tokens, segments=segments, wqkv=wqkv, bias_qv=bias_qv, wo=wo, bias_o=bias_o, gain_a=gain_a, shift_a=shift_a, w_in=w_in, bias_in=bias_in, w_out=w_out, bias_out=bias_out, gain_b=gain_b, shift_b=shift_b, cotangent=cotangent)


@jax.custom_vjp
def low(v):
    return lax.optimization_barrier(v.astype(jnp.bfloat16)).astype(jnp.float32)

@jax.custom_vjp
def low_back(v):
    return v

def low_keep(v):
    return (low(v), None)

def low_pass(kept, grad):
    return (grad,)

def back_keep(v):
    return (v, None)

def back_low(kept, grad):
    return (low(grad),)
low.defvjp(low_keep, low_pass)
low_back.defvjp(back_keep, back_low)
highest = lax.Precision.HIGHEST
NORM_EPS = 1e-06
MASKED = -1000000000.0

def product(left, right):
    return jnp.dot(left, right, precision=highest)

def norm_rows(hidden, gain, shift):
    row_mean = lax.optimization_barrier(jnp.mean(hidden, axis=-1, keepdims=True))
    row_square = lax.optimization_barrier(jnp.mean(hidden * hidden, axis=-1, keepdims=True))
    inv_std = lax.rsqrt(row_square - row_mean * row_mean + NORM_EPS)
    return (hidden - row_mean) * inv_std * gain + shift

def layer_sequence(params, row_data, labels):
    wqkv, bias_qv, wo, bias_o, gain_a, shift_a, w_in, bias_in, w_out, bias_out, gain_b, shift_b = params
    length = row_data.shape[0]
    projected = low_back(product(row_data, wqkv)).reshape(length, HEADS, 3, DH)
    biases = bias_qv.reshape(HEADS, 2, DH)
    queries = low(projected[:, :, 0] + biases[:, 0])
    key_rows = low(projected[:, :, 1])
    value_rows = low(projected[:, :, 2] + biases[:, 1])
    scores = low_back(jnp.einsum('qhd,khd->hqk', queries, key_rows, precision=highest) * (1.0 / math.sqrt(DH)))
    allowed = labels[:, None] == labels[None, :]
    scores = jnp.where(allowed[None], scores, MASKED)
    probabilities = low(jax.nn.softmax(scores, axis=-1))
    context = low(low_back(jnp.einsum('hqk,khd->qhd', probabilities, value_rows, precision=highest))).reshape(length, D)
    hidden_a = row_data + (low_back(product(context, wo)) + bias_o)
    normed_a = norm_rows(hidden_a, gain_a, shift_a)
    inner = low_back(product(low(normed_a), w_in)) + bias_in
    active = low(jax.nn.gelu(inner, approximate=False))
    hidden_b = normed_a + (low_back(product(active, w_out)) + bias_out)
    return norm_rows(hidden_b, gain_b, shift_b)

def reference(tokens, segments, wqkv, bias_qv, wo, bias_o, gain_a, shift_a, w_in, bias_in, w_out, bias_out, gain_b, shift_b, cotangent):
    params = tuple((argument.astype(jnp.float32) for argument in (wqkv, bias_qv, wo, bias_o, gain_a, shift_a, w_in, bias_in, w_out, bias_out, gain_b, shift_b)))
    row_data = tokens.astype(jnp.float32).reshape(-1, SEQ, D)

    def forward(inputs, weights):
        per_sequence = jax.checkpoint(lambda paired: layer_sequence(weights, paired[0], paired[1]))
        return lax.map(per_sequence, (inputs, segments))
    result, pullback = jax.vjp(forward, row_data, params)
    grad_rows, grad_params = pullback(cotangent.astype(jnp.float32).reshape(-1, SEQ, D))
    return (result.reshape(-1, D).astype(jnp.bfloat16), grad_rows.reshape(-1, D), grad_params[0], grad_params[1], grad_params[2], grad_params[3], grad_params[4], grad_params[5], grad_params[6], grad_params[7], grad_params[8], grad_params[9], grad_params[10], grad_params[11])
```

```python
import math

import jax
import jax.numpy as jnp
from jax import lax
from jax.sharding import PartitionSpec as P

DH = 64
NORM_EPS = 1e-06
MASKED = -1000000000.0
block_limit = 512
F32 = jnp.float32
BF16 = jnp.bfloat16


def nn(left, right):
    return lax.dot_general(left, right, (((1,), (0,)), ((), ())), preferred_element_type=F32)


def nt(left, right):
    return lax.dot_general(left, right, (((1,), (1,)), ((), ())), preferred_element_type=F32)


def tn(left, right):
    return lax.dot_general(left, right, (((0,), (0,)), ((), ())), preferred_element_type=F32)


def trade(block, axis, count, mask):
    return lax.ppermute(block, axis, [(i, i ^ mask) for i in range(count)])


def pick(block, bit, dim):
    return lax.dynamic_slice_in_dim(block, bit, 1, dim)


class Stage:
    def __init__(self, axis, count, mask, index, dim):
        self.axis, self.count, self.mask, self.dim = axis, count, mask, dim
        self.bit = (index // mask) % 2

    def trade(self, block):
        return trade(block, self.axis, self.count, self.mask)

    def join(self, mine, other, dim):
        low = self.bit == 0
        return jnp.concatenate(
            (jnp.where(low, mine, other), jnp.where(low, other, mine)), axis=dim
        )

    def gather(self, block):
        return self.join(block, self.trade(block), self.dim)

    def reduce(self, block):
        keep = pick(block, self.bit, self.dim)
        sent = pick(block, 1 - self.bit, self.dim)
        got = self.trade(sent)
        return (keep.astype(F32) + got.astype(F32)).astype(block.dtype)

    def swap(self, block, split, dim):
        keep = pick(block, self.bit, split)
        sent = pick(block, 1 - self.bit, split)
        return self.join(keep, self.trade(sent), dim)


def bits_of(count):
    return [1 << b for b in reversed(range(count.bit_length() - 1))]


def attend(queries, key_rows, value_rows, labels):
    length = queries.shape[0]
    block_rows = min(block_limit, length)
    score_scale = 1.0 / math.sqrt(queries.shape[1])

    def one_block(first_row):
        query_block = lax.dynamic_slice_in_dim(queries, first_row, block_rows, 0)
        label_block = lax.dynamic_slice_in_dim(labels, first_row, block_rows, 0)
        scores = nt(query_block, key_rows) * score_scale
        scores = jnp.where(label_block[:, None] == labels[None, :], scores, MASKED)
        row_max = jnp.max(scores, axis=1, keepdims=True)
        shifted = jnp.exp(scores - row_max)
        row_total = jnp.sum(shifted, axis=1, keepdims=True)
        probabilities = (shifted / row_total).astype(BF16)
        context = nn(probabilities, value_rows)
        return (context, (row_max + jnp.log(row_total))[:, 0])

    starts = jnp.arange(length // block_rows, dtype=jnp.int32) * block_rows
    context, log_total = lax.map(one_block, starts)
    return (context.reshape(length, -1), log_total.reshape(length))


def attend_back(queries, key_rows, value_rows, labels, log_total, grad_context):
    length = queries.shape[0]
    block_rows = min(block_limit, length)
    score_scale = 1.0 / math.sqrt(queries.shape[1])

    def one_block(state_pair, first_row):
        grad_keys, grad_values = state_pair
        query_block = lax.dynamic_slice_in_dim(queries, first_row, block_rows, 0)
        label_block = lax.dynamic_slice_in_dim(labels, first_row, block_rows, 0)
        total_block = lax.dynamic_slice_in_dim(log_total, first_row, block_rows, 0)
        grad_block = lax.dynamic_slice_in_dim(grad_context, first_row, block_rows, 0)
        scores = nt(query_block, key_rows) * score_scale
        scores = jnp.where(label_block[:, None] == labels[None, :], scores, MASKED)
        probabilities = jnp.exp(scores - total_block[:, None])
        grad_prob = nt(grad_block, value_rows)
        row_dot = jnp.sum(probabilities * grad_prob, axis=1, keepdims=True)
        dscore = (probabilities * (grad_prob - row_dot)).astype(BF16)
        grad_query = nn(dscore, key_rows) * score_scale
        grad_keys = grad_keys + tn(dscore, query_block) * score_scale
        grad_values = grad_values + tn(probabilities.astype(BF16), grad_block)
        return ((grad_keys, grad_values), grad_query)

    starts = jnp.arange(length // block_rows, dtype=jnp.int32) * block_rows
    zero_rows = jnp.zeros(key_rows.shape, F32)
    (grad_keys, grad_values), grad_query = lax.scan(one_block, (zero_rows, zero_rows), starts)
    return (grad_query.reshape(queries.shape), grad_keys, grad_values)


attend_heads = jax.vmap(attend, in_axes=(1, 1, 1, None), out_axes=1)
attend_heads_back = jax.vmap(attend_back, in_axes=(1, 1, 1, None, 1, 1), out_axes=1)


def body(
    rows,
    cols,
    tokens,
    segments,
    wqkv,
    bias_qv,
    wo,
    bias_o,
    gain_a,
    shift_a,
    w_in,
    bias_in,
    w_out,
    bias_out,
    gain_b,
    shift_b,
    cotangent,
):
    seqs, length = segments.shape
    ways = cols // seqs
    width = tokens.shape[1]
    model = width * cols
    heads = wqkv.shape[1] // (3 * DH)
    hid = w_in.shape[1]
    part = length // ways
    own_rows = wqkv.shape[0]
    row, col = lax.axis_index("row"), lax.axis_index("col")
    seq, way = col // ways, col % ways
    row_masks, seq_masks, way_masks = bits_of(rows), bits_of(seqs), bits_of(ways)
    ns, nw, nr = len(seq_masks), len(way_masks), len(row_masks)
    by_seq = [Stage("col", cols, mask * ways, col, i) for i, mask in enumerate(seq_masks)]
    by_way = [Stage("col", cols, mask, col, i) for i, mask in enumerate(way_masks)]
    by_row = [Stage("row", rows, mask, row, ns + i) for i, mask in enumerate(row_masks)]
    order_a = by_row + by_seq
    order_b = by_row[:-1] + by_seq + by_row[-1:]

    def gather_weight(shard):
        half = shard.shape[1] // 2
        parts = []
        for order, piece in ((order_a, shard[:, :half]), (order_b, shard[:, half:])):
            block = piece.reshape((1,) * (ns + nr) + piece.shape)
            for stage in order:
                block = stage.gather(block)
            parts.append(block.reshape(seqs, rows * own_rows, half))
        return jnp.concatenate(parts, axis=2)

    def scatter_weight(grads):
        whole = jnp.stack(grads, axis=0)
        half = whole.shape[2] // 2
        parts = []
        for order, piece in ((order_a, whole[:, :, :half]), (order_b, whole[:, :, half:])):
            block = piece.reshape((2,) * (ns + nr) + (own_rows, half))
            for stage in reversed(order):
                block = stage.reduce(block)
            parts.append(block.reshape(own_rows, half))
        return jnp.concatenate(parts, axis=1).astype(F32)

    def gather_ways(block):
        block = block.reshape((1,) * nw + block.shape)
        for stage in by_way:
            block = stage.gather(block)
        return block.reshape(length, model)

    def scatter_ways(partial_terms):
        block = partial_terms.reshape((2,) * nw + (part, model))
        for stage in by_way:
            keep = pick(block, stage.bit, stage.dim)
            sent = pick(block, 1 - stage.bit, stage.dim)
            got = stage.trade(sent.astype(BF16))
            block = keep + got.astype(F32)
        return block.reshape(part, model)

    small = jnp.concatenate(
        [v.reshape(-1, width) for v in (bias_o, gain_a, shift_a, bias_out, gain_b, shift_b, bias_qv, bias_in)]
    )
    small = small.reshape((1,) * (ns + nw) + small.shape)
    for stage in by_seq:
        small = stage.gather(small)
    for i, stage in enumerate(by_way):
        small = stage.join(small, stage.trade(small), ns + i)
    small = small.reshape(cols, -1, width).astype(F32)
    full = [small[:, i].reshape(1, model) for i in range(6)]
    bias_o32, gain_a32, shift_a32, bias_out32, gain_b32, shift_b32 = full
    mine = small.reshape(seqs, ways, -1, width)
    mine = lax.dynamic_slice_in_dim(mine, way, 1, 1)[:, 0]
    nq = bias_qv.shape[0] // width
    bias_qv_all = mine[:, 6 : 6 + nq].reshape(seqs, heads, 2, DH)
    bias_in_all = mine[:, 6 + nq :].reshape(seqs, 1, hid)

    def own_sequence(array):
        block = array.reshape((2,) * ns + (1,) * ns + (length, width))
        for i, stage in enumerate(by_seq):
            block = stage.swap(block, i, ns + i)
        return block.reshape((seqs, length, width))

    def own_part(array):
        block = own_sequence(array)
        block = block.reshape((seqs,) + (1,) * nw + (2,) * nw + (part, width))
        for i, stage in enumerate(by_way):
            block = stage.swap(block, 1 + nw + i, 1 + i)
        block = block.reshape(cols, part, width)
        return jnp.transpose(block, (1, 0, 2)).reshape(part, model)

    def back_to_features(array):
        block = array.reshape((part, seqs) + (2,) * nw + (width,))
        block = jnp.moveaxis(block, 0, -2).reshape((seqs,) + (2,) * nw + (1,) * nw + (part, width))
        for i, stage in enumerate(by_way):
            block = stage.swap(block, 1 + i, 1 + nw + i)
        block = block.reshape((2,) * ns + (1,) * ns + (length, width))
        for i, stage in enumerate(by_seq):
            block = stage.swap(block, i, ns + i)
        return block.reshape(seqs * length, width)

    labels = lax.dynamic_slice_in_dim(segments, seq, 1, 0)[0]

    tokens_x = own_sequence(tokens)
    block = tokens_x.reshape((seqs,) + (1,) * nw + (length, width))
    for i, stage in enumerate(by_way):
        block = stage.join(block, stage.trade(block), 1 + i)
    block = block.reshape(cols, length, width)
    whole_x = jnp.transpose(block, (1, 0, 2)).reshape(length, model)
    cot = own_part(cotangent).astype(F32)

    def by_kind(weight):
        n = weight.shape[0]
        return weight.reshape(n, heads, 3, DH).transpose(0, 2, 1, 3).reshape(n, -1)

    def by_head(weight):
        n = weight.shape[0]
        return weight.reshape(n, 3, heads, DH).transpose(0, 2, 1, 3).reshape(n, -1)

    qkv_all = gather_weight(by_kind(wqkv))
    wo_all = gather_weight(wo.T)
    in_all = gather_weight(w_in)
    out_all = gather_weight(w_out.T)

    queries, key_rows, value_rows = [], [], []
    for j in range(seqs):
        projected = nn(whole_x, qkv_all[j]).reshape(length, 3, heads, DH)
        queries.append((projected[:, 0] + bias_qv_all[j][:, 0]).astype(BF16))
        key_rows.append(projected[:, 1].astype(BF16))
        value_rows.append((projected[:, 2] + bias_qv_all[j][:, 1]).astype(BF16))
    queries = jnp.concatenate(queries, axis=1)
    key_rows = jnp.concatenate(key_rows, axis=1)
    value_rows = jnp.concatenate(value_rows, axis=1)
    context, log_total = attend_heads(queries, key_rows, value_rows, labels)
    context = context.astype(BF16).reshape(length, seqs, heads * DH)
    partial_a = sum(nt(context[:, j], wo_all[j]) for j in range(seqs))
    own_x = lax.dynamic_slice_in_dim(whole_x, way * part, part, 0)
    hidden_a = scatter_ways(partial_a) + own_x.astype(F32) + bias_o32

    def norm(hidden):
        mean = jnp.mean(hidden, axis=1, keepdims=True)
        square = jnp.mean(hidden * hidden, axis=1, keepdims=True)
        inv_std = lax.rsqrt(square - mean * mean + NORM_EPS)
        return (hidden - mean) * inv_std, inv_std

    def norm_back(incoming, centred, inv_std, gain):
        scaled = incoming * gain
        first = jnp.mean(scaled, axis=1, keepdims=True)
        second = jnp.mean(scaled * centred, axis=1, keepdims=True)
        return inv_std * (scaled - first - centred * second)

    centred_a, inv_std_a = norm(hidden_a)
    normed_a = centred_a * gain_a32 + shift_a32
    whole_y = gather_ways(normed_a.astype(BF16))
    gelu = lambda v: jax.nn.gelu(v, approximate=False)
    inner = [nn(whole_y, in_all[j]) + bias_in_all[j] for j in range(seqs)]
    active = [gelu(v).astype(BF16) for v in inner]
    partial_b = sum(nt(active[j], out_all[j]) for j in range(seqs))
    hidden_b = scatter_ways(partial_b) + bias_out32 + normed_a
    centred_b, inv_std_b = norm(hidden_b)
    output = back_to_features((centred_b * gain_b32 + shift_b32).astype(BF16))

    grad_b = norm_back(cot, centred_b, inv_std_b, gain_b32)
    whole_gb = gather_ways(grad_b.astype(BF16))
    grad_inner = [jax.vjp(gelu, inner[j])[1](nn(whole_gb, out_all[j]))[0] for j in range(seqs)]
    grad_inner_low = [v.astype(BF16) for v in grad_inner]
    partial_n = sum(nt(grad_inner_low[j], in_all[j]) for j in range(seqs))
    grad_w_out = scatter_weight([tn(whole_gb, active[j]).astype(BF16) for j in range(seqs)])
    grad_w_in = scatter_weight([tn(whole_y, grad_inner_low[j]).astype(BF16) for j in range(seqs)])
    grad_normed = scatter_ways(partial_n) + grad_b
    grad_a = norm_back(grad_normed, centred_a, inv_std_a, gain_a32)
    whole_ga = gather_ways(grad_a.astype(BF16))
    grad_context = [nn(whole_ga, wo_all[j]).astype(BF16) for j in range(seqs)]
    grad_wo = scatter_weight([tn(whole_ga, context[:, j]).astype(BF16) for j in range(seqs)])
    grad_context = jnp.concatenate(grad_context, axis=1).reshape(length, seqs * heads, DH)
    grad_q, grad_k, grad_v = attend_heads_back(
        queries, key_rows, value_rows, labels, log_total, grad_context
    )
    split = lambda v: v.reshape(length, seqs, heads * DH)
    grad_q, grad_k, grad_v = split(grad_q), split(grad_k), split(grad_v)
    grad_projected = [
        jnp.concatenate((grad_q[:, j], grad_k[:, j], grad_v[:, j]), axis=1).astype(BF16)
        for j in range(seqs)
    ]
    partial_x = sum(nt(grad_projected[j], qkv_all[j]) for j in range(seqs))
    grad_wqkv = scatter_weight([tn(whole_x, grad_projected[j]).astype(BF16) for j in range(seqs)])
    grad_tokens = back_to_features((scatter_ways(partial_x) + grad_a).astype(BF16)).astype(F32)

    per_hidden = jnp.stack(
        [
            jnp.concatenate(
                (
                    jnp.stack(
                        (
                            jnp.sum(grad_q[:, j], axis=0).reshape(heads, DH),
                            jnp.sum(grad_v[:, j], axis=0).reshape(heads, DH),
                        ),
                        axis=1,
                    ).reshape(-1),
                    jnp.sum(grad_inner[j], axis=0),
                )
            )
            for j in range(seqs)
        ]
    )
    per_feature = jnp.stack(
        [
            jnp.sum(v, axis=0)
            for v in (
                grad_a,
                grad_normed * centred_a,
                grad_normed,
                grad_b,
                cot * centred_b,
                cot,
            )
        ]
    )
    block = per_feature.reshape((6, seqs) + (2,) * nw + (width,))
    for i, stage in enumerate(by_way):
        keep = pick(block, stage.bit, 2 + i)
        sent = pick(block, 1 - stage.bit, 2 + i)
        block = keep + stage.trade(sent)
    block = block.reshape(6, seqs, width).transpose(1, 0, 2).reshape(seqs, 6 * width)
    block = jnp.concatenate((per_hidden, block), axis=1).reshape((2,) * ns + (-1,))
    for stage in by_seq:
        block = stage.reduce(block)
    sums = lax.psum(block.reshape(-1), "row")
    nqv = bias_qv.shape[0]
    sum_qv, sum_in = sums[:nqv], sums[nqv : nqv + hid]
    rest = sums[nqv + hid :].reshape(6, width)
    return (
        output,
        grad_tokens,
        by_head(grad_wqkv),
        sum_qv,
        grad_wo.T,
        rest[0],
        rest[1],
        rest[2],
        grad_w_in,
        sum_in,
        grad_w_out.T,
        rest[3],
        rest[4],
        rest[5],
    )


def solution(mesh):
    tile, across, down, flat = P("row", "col"), P("row", None), P("col", "row"), P("col")
    in_specs = (tile, across, tile, flat, down, flat, flat, flat, tile, flat, down, flat, flat, flat, tile)
    out_specs = (tile, tile, tile, flat, down, flat, flat, flat, tile, flat, down, flat, flat, flat)
    rows, cols = mesh.shape["row"], mesh.shape["col"]

    def layer(*args):
        return body(rows, cols, *args)

    return jax.shard_map(layer, mesh=mesh, in_specs=in_specs, out_specs=out_specs, check_vma=False)
```

```python
import functools
import math

import jax
import jax.numpy as jnp
from jax import lax
from jax.experimental import pallas as pl
from jax.experimental.pallas import tpu as pltpu
from jax.sharding import PartitionSpec as P

DH = 64
NORM_EPS = 1e-06
MASKED = -1000000000.0
LONGEST = 256
F32 = jnp.float32
BF16 = jnp.bfloat16


def nn(left, right):
    return lax.dot_general(left, right, (((1,), (0,)), ((), ())), preferred_element_type=F32)


def nt(left, right):
    return lax.dot_general(left, right, (((1,), (1,)), ((), ())), preferred_element_type=F32)


def tn(left, right):
    return lax.dot_general(left, right, (((0,), (0,)), ((), ())), preferred_element_type=F32)


def after(block, *others):
    return lax.optimization_barrier((block,) + others)[0]


def pick(block, bit, dim):
    return lax.dynamic_slice_in_dim(block, bit, 1, dim)


def bits_of(count):
    return [1 << b for b in reversed(range(count.bit_length() - 1))]


class Stage:
    def __init__(self, axis, count, mask, index):
        self.axis, self.pairs = axis, [(i, i ^ mask) for i in range(count)]
        self.bit = (index // mask) % 2

    def trade(self, block):
        return lax.ppermute(block, self.axis, self.pairs)

    def join(self, mine, other, dim):
        low = self.bit == 0
        return jnp.concatenate(
            (jnp.where(low, mine, other), jnp.where(low, other, mine)), axis=dim
        )

    def gather(self, block, dim):
        return self.join(block, self.trade(block), dim)

    def swap(self, block, split, dim):
        keep = pick(block, self.bit, split)
        return self.join(keep, self.trade(pick(block, 1 - self.bit, split)), dim)

    def reduce(self, block, dim):
        got = self.trade(pick(block, 1 - self.bit, dim))
        return add(pick(block, self.bit, dim), got)


def add(mine, other):
    return (mine.astype(F32) + other.astype(F32)).astype(mine.dtype)


def tiles_of(length):
    return min(256, length), min(128, length)


def key_windows(labels):
    rows, step = tiles_of(labels.shape[0])
    first, last = labels[::rows], labels[rows - 1 :: rows]
    start = jnp.sum(labels[None, :] < first[:, None], axis=1)
    stop = jnp.sum(labels[None, :] <= last[:, None], axis=1)
    block = start // step
    return jnp.stack((block, (stop - 1) // step + 1 - block)).astype(jnp.int32)


def for_each_block(windows, length, run):
    rows, step = tiles_of(length)
    reach = -(-(LONGEST - 1) // step)
    most = min(length // step, rows // step + 2 * reach)

    def one(i, carry):
        q0 = pl.multiple_of(i * rows, rows)
        k0 = pl.multiple_of(windows[0, i] * step, step)
        for n in range(1, most + 1):
            pl.when(windows[1, i] == n)(functools.partial(run, q0, k0, rows, n * step))
        return carry

    lax.fori_loop(0, length // rows, one, 0)


def attend_kernel(
    windows, x_ref, w_ref, b_ref, lab_col, lab_row, q_ref, k_ref, v_ref, ctx_ref, lse_ref
):
    length, lanes = q_ref.shape
    rows, _ = tiles_of(length)

    def project(i, carry):
        here = pl.ds(pl.multiple_of(i * rows, rows), rows)
        projected = nn(x_ref[here, :], w_ref[...]) + b_ref[...]
        scale = 1.0 / math.sqrt(DH)
        q_ref[here, :] = (projected[:, :lanes].astype(BF16).astype(F32) * scale).astype(BF16)
        k_ref[here, :] = projected[:, lanes : 2 * lanes].astype(BF16)
        v_ref[here, :] = projected[:, 2 * lanes :].astype(BF16)
        return carry

    lax.fori_loop(0, length // rows, project, 0)

    def run(q0, k0, rows, span):
        q = q_ref[pl.ds(q0, rows), :]
        k = k_ref[pl.ds(k0, span), :]
        v_t = v_ref[pl.ds(k0, span), :].T
        same = lab_col[pl.ds(k0, span), :] == lab_row[:, pl.ds(q0, rows)]
        head = lax.broadcasted_iota(jnp.int32, (span, lanes), 1) // DH
        outs = []
        for h in range(lanes // DH):
            scores = nt(jnp.where(head == h, k, jnp.zeros_like(k)), q)
            scores = jnp.where(same, scores, MASKED)
            top = jnp.max(scores, axis=0, keepdims=True)
            shifted = jnp.exp(scores - top)
            total = jnp.sum(shifted, axis=0, keepdims=True)
            outs.append(nn(v_t[h * DH : (h + 1) * DH, :], shifted.astype(BF16)) / total)
            lse_ref[h : h + 1, pl.ds(q0, rows)] = top + jnp.log(total)
        ctx_ref[pl.ds(q0, rows), :] = jnp.concatenate(outs, axis=0).T.astype(BF16)

    for_each_block(windows, length, run)


def attend_back_kernel(
    windows, ga_ref, wo_ref, q_ref, k_ref, v_ref, lse_ref, lab_col, lab_row, gp_ref, sum_ref,
    do_ref, dk_acc, dv_acc,
):
    length, lanes = q_ref.shape
    tile_rows, _ = tiles_of(length)
    scale = 1.0 / math.sqrt(DH)
    dk_acc[...] = jnp.zeros_like(dk_acc)
    dv_acc[...] = jnp.zeros_like(dv_acc)
    sum_ref[...] = jnp.zeros_like(sum_ref)

    def project(i, carry):
        here = pl.ds(pl.multiple_of(i * tile_rows, tile_rows), tile_rows)
        do_ref[here, :] = nn(ga_ref[here, :], wo_ref[...]).astype(BF16)
        return carry

    lax.fori_loop(0, length // tile_rows, project, 0)

    def run(q0, k0, rows, span):
        q = q_ref[pl.ds(q0, rows), :]
        do = do_ref[pl.ds(q0, rows), :]
        k = k_ref[pl.ds(k0, span), :]
        v = v_ref[pl.ds(k0, span), :]
        k_t = k.T
        same = lab_col[pl.ds(k0, span), :] == lab_row[:, pl.ds(q0, rows)]
        head = lax.broadcasted_iota(jnp.int32, (span, lanes), 1) // DH
        head_q = lax.broadcasted_iota(jnp.int32, (rows, lanes), 1) // DH
        dqs = []
        dk = dv = None
        for h in range(lanes // DH):
            only = lambda a, own: jnp.where(own == h, a, jnp.zeros_like(a))
            scores = jnp.where(same, nt(only(k, head), q), MASKED)
            prob = jnp.exp(scores - lse_ref[h : h + 1, pl.ds(q0, rows)])
            weighted = prob * nt(only(v, head), do)
            row_dot = jnp.sum(weighted, axis=0, keepdims=True)
            dscore = (weighted - prob * row_dot).astype(BF16)
            dv_h = nn(prob.astype(BF16), only(do, head_q))
            dk_h = nn(dscore, only(q, head_q))
            dv = dv_h if dv is None else dv + dv_h
            dk = dk_h if dk is None else dk + dk_h
            dqs.append(nn(k_t[h * DH : (h + 1) * DH, :], dscore))
        dq = jnp.concatenate(dqs, axis=0).T * scale
        gp_ref[pl.ds(q0, rows), :lanes] = dq.astype(BF16)
        sum_ref[0:1, :] += jnp.sum(dq, axis=0, keepdims=True)
        dk_acc[pl.ds(k0, span), :] += dk
        dv_acc[pl.ds(k0, span), :] += dv

    for_each_block(windows, length, run)
    gp_ref[:, lanes : 2 * lanes] = dk_acc[...].astype(BF16)
    gp_ref[:, 2 * lanes :] = dv_acc[...].astype(BF16)
    sum_ref[1:2, :] = jnp.sum(dv_acc[...], axis=0, keepdims=True)


def whole_call(kernel, scalars, operands, outs, scratch, flops, name):
    full = lambda a: pl.BlockSpec(a.shape, lambda i, *_: (0,) * len(a.shape))
    moved = sum(math.prod(a.shape) * a.dtype.itemsize for a in list(operands) + list(outs))
    return pl.pallas_call(
        kernel,
        grid_spec=pltpu.PrefetchScalarGridSpec(
            num_scalar_prefetch=len(scalars),
            grid=(1,),
            in_specs=[full(a) for a in operands],
            out_specs=[full(a) for a in outs],
            scratch_shapes=scratch,
        ),
        out_shape=outs,
        cost_estimate=pl.CostEstimate(flops=flops, transcendentals=0, bytes_accessed=moved),
        name=name,
    )(*scalars, *operands)


def attend(windows, x, weight, bias, lab_col, lab_row):
    length, model = x.shape
    lanes = weight.shape[1] // 3
    rows = jax.ShapeDtypeStruct((length, lanes), BF16)
    outs = [rows, rows, rows, rows, jax.ShapeDtypeStruct((lanes // DH, length), F32)]
    return whole_call(
        attend_kernel, [windows], [x, weight, bias, lab_col, lab_row], outs, [],
        6 * length * model * lanes + 20 * length * 640 * lanes, "attend",
    )


def attend_back(windows, ga, wo, q, k, v, lse, lab_col, lab_row):
    length, lanes = q.shape
    outs = [
        jax.ShapeDtypeStruct((length, 3 * lanes), BF16),
        jax.ShapeDtypeStruct((2, lanes), F32),
    ]
    scratch = [pltpu.VMEM((length, lanes), BF16)] + [pltpu.VMEM((length, lanes), F32)] * 2
    return whole_call(
        attend_back_kernel, [windows], [ga, wo, q, k, v, lse, lab_col, lab_row], outs, scratch,
        2 * length * ga.shape[1] * lanes + 40 * length * 640 * lanes, "attend_back",
    )


def ffn_in_kernel(y_ref, w_ref, b_ref, act_ref, slope_ref):
    inner = nn(y_ref[...], w_ref[...]) + b_ref[...]
    share = 0.5 + 0.5 * lax.erf(inner * math.sqrt(0.5))
    density = jnp.exp(-0.5 * inner * inner) * (1.0 / math.sqrt(2.0 * math.pi))
    act_ref[...] = (inner * share).astype(BF16)
    slope_ref[...] = (share + inner * density).astype(BF16)


def ffn_back_kernel(gb_ref, w_ref, slope_ref, gi_ref, sum_ref):
    grad = nn(gb_ref[...], w_ref[...]) * slope_ref[...].astype(F32)
    gi_ref[...] = grad.astype(BF16)
    sum_ref[...] = jnp.sum(grad, axis=0, keepdims=True)


def by_columns(kernel, rows, weight, extra, outs, flops, name):
    length, model = rows.shape
    wide = weight.shape[1]
    tile = min(256, wide)
    column = lambda a: pl.BlockSpec((a.shape[0], tile), lambda i: (0, i))
    moved = sum(math.prod(a.shape) * a.dtype.itemsize for a in [rows, weight, extra] + list(outs))
    return pl.pallas_call(
        kernel,
        grid=(wide // tile,),
        in_specs=[pl.BlockSpec((length, model), lambda i: (0, 0)), column(weight), column(extra)],
        out_specs=[column(a) for a in outs],
        out_shape=outs,
        cost_estimate=pl.CostEstimate(flops=flops, transcendentals=0, bytes_accessed=moved),
        name=name,
    )(rows, weight, extra)


def ffn_in(y, weight, bias):
    out = jax.ShapeDtypeStruct((y.shape[0], weight.shape[1]), BF16)
    flops = 2 * math.prod(y.shape) * weight.shape[1] * 3
    return by_columns(ffn_in_kernel, y, weight, bias, [out, out], flops, "ffn_in")


def ffn_back(gb, weight, slope):
    outs = [
        jax.ShapeDtypeStruct(slope.shape, BF16),
        jax.ShapeDtypeStruct((1, slope.shape[1]), F32),
    ]
    flops = 2 * math.prod(gb.shape) * weight.shape[1]
    return by_columns(ffn_back_kernel, gb, weight, slope, outs, flops, "ffn_back")


def body(
    rows,
    cols,
    tokens,
    segments,
    wqkv,
    bias_qv,
    wo,
    bias_o,
    gain_a,
    shift_a,
    w_in,
    bias_in,
    w_out,
    bias_out,
    gain_b,
    shift_b,
    cotangent,
):
    seqs, length = segments.shape
    ways = cols // seqs
    width = tokens.shape[1]
    model = width * cols
    heads = wqkv.shape[1] // (3 * DH)
    hid = w_in.shape[1]
    part = length // ways
    own_rows = wqkv.shape[0]
    row, col = lax.axis_index("row"), lax.axis_index("col")
    seq, way = col // ways, col % ways
    by_seq = [Stage("col", cols, mask * ways, col) for mask in bits_of(seqs)]
    by_way = [Stage("col", cols, mask, col) for mask in bits_of(ways)]
    by_row = [Stage("row", rows, mask, row) for mask in bits_of(rows)]
    ns, nw, nr = len(by_seq), len(by_way), len(by_row)
    far, near = by_row[:-1], by_row[-1]

    def gather_far(shard):
        block = shard.reshape((1,) * nr + shard.shape)
        for i, stage in enumerate(far):
            block = stage.gather(block, i)
        return block

    def gather_near_first(block):
        mine = near.gather(block, nr - 1).reshape(model, -1)
        return [mine]

    def gather_seq_last(blocks):
        for stage in by_seq:
            blocks = blocks + [stage.trade(b) for b in blocks]
        return blocks

    def gather_seq_first(block):
        block = block[None]
        for stage in by_seq:
            block = jnp.concatenate((block, stage.trade(block)), axis=0)
        return block

    def gather_near_last(block):
        block = near.gather(block, nr)
        return [block[j].reshape(model, -1) for j in range(seqs)]

    shards = []
    halves = lambda w: w.reshape(own_rows, 2, heads // 2, 3, DH)
    shards.append(halves(wqkv).transpose(0, 1, 3, 2, 4).reshape(own_rows, -1))
    shards.append(wo.T)
    shards.append(w_in)
    shards.append(w_out.T)

    labels = lax.dynamic_slice_in_dim(segments, seq, 1, 0)[0]
    windows = key_windows(labels)
    lab_col, lab_row = labels[:, None], labels[None, :]

    vectors = jnp.concatenate(
        [v.reshape(-1, width) for v in (bias_o, gain_a, shift_a, bias_out, gain_b, shift_b, bias_qv, bias_in)]
    )

    def own_sequence(array):
        block = array.reshape((2,) * ns + (1,) * ns + (length, width))
        for i, stage in enumerate(by_seq):
            block = stage.swap(block, i, ns + i)
        return block.reshape((seqs, length, width))

    tokens_x = own_sequence(tokens)
    block = tokens_x.reshape((seqs,) + (1,) * nw + (length, width))
    for i, stage in enumerate(by_way):
        block = stage.gather(block, 1 + i)
    block = block.reshape(cols, length, width)
    whole_x = jnp.transpose(block, (1, 0, 2)).reshape(length, model)

    pairs = [vectors]
    for stage in by_seq:
        pairs = pairs + [stage.trade(v) for v in pairs]
    block = vectors.reshape((1,) * (ns + nw) + vectors.shape)[..., :6, :]
    for i, stage in enumerate(by_seq):
        block = stage.join(block, pairs[1 << i].reshape((1,) * (ns + nw) + vectors.shape)[..., :6, :], i)
    for i, stage in enumerate(by_way):
        block = stage.gather(block, ns + i)
    full = block.reshape(cols, 6, width).transpose(1, 0, 2).reshape(6, 1, model).astype(F32)
    bias_o32, gain_a32, shift_a32, bias_out32, gain_b32, shift_b32 = (full[i] for i in range(6))
    nq = bias_qv.shape[0] // width

    def qkv_bias(j, half):
        both = pairs[j][6 : 6 + nq].astype(F32).reshape(2, heads // 2, 2, DH)[half]
        q, v = both[:, 0].reshape(1, -1), both[:, 1].reshape(1, -1)
        return jnp.concatenate((q, jnp.zeros_like(q), v), axis=1)

    def in_bias(j, half):
        return pairs[j][6 + nq :].astype(F32).reshape(2, 1, hid // 2)[half]

    gathered = []
    held_far = held_first = None
    for shard in shards:
        if held_far is not None:
            shard = after(shard, held_far)
        block = gather_far(shard)
        held_far = block
        half = block.shape[-1] // 2
        one, two = block[..., :half], block[..., half:]
        if held_first is not None:
            one, two = after(one, *held_first), after(two, *held_first)
        one, two = gather_near_first(one), gather_seq_first(two)
        held_first = (one[0], two)
        one, two = gather_seq_last(one), gather_near_last(two)
        gathered.append([(one[j], two[j]) for j in range(seqs)])
    flat = [[blk for pair in weight for blk in pair] for weight in gathered]
    qkv_all, wo_all, in_all, out_all = flat
    places = [(j, half) for j in range(seqs) for half in range(2)]

    def own_part(array):
        block = own_sequence(array)
        block = block.reshape((seqs,) + (1,) * nw + (2,) * nw + (part, width))
        for i, stage in enumerate(by_way):
            block = stage.swap(block, 1 + nw + i, 1 + i)
        block = block.reshape(cols, part, width)
        return jnp.transpose(block, (1, 0, 2)).reshape(part, model)

    def back_to_features(array):
        block = array.reshape((part, seqs) + (2,) * nw + (width,))
        block = jnp.moveaxis(block, 0, -2).reshape((seqs,) + (2,) * nw + (1,) * nw + (part, width))
        for i, stage in enumerate(by_way):
            block = stage.swap(block, 1 + i, 1 + nw + i)
        block = block.reshape((2,) * ns + (1,) * ns + (length, width))
        for i, stage in enumerate(by_seq):
            block = stage.swap(block, i, ns + i)
        return block.reshape(seqs * length, width)

    def gather_ways(block):
        block = block.reshape((1,) * nw + block.shape)
        for i, stage in enumerate(by_way):
            block = stage.gather(block, i)
        return block.reshape(length, model)

    def scatter_ways(partial_terms):
        block = partial_terms.reshape((2,) * nw + (part, model))
        for i, stage in enumerate(by_way):
            got = stage.trade(pick(block, 1 - stage.bit, i).astype(BF16))
            block = pick(block, stage.bit, i) + got.astype(F32)
        return block.reshape(part, model)

    def scatter_weight(blocks):
        ones, twos = blocks[0::2], blocks[1::2]
        for stage in reversed(by_seq):
            count = len(ones) // 2
            ones = [add(ones[j], stage.trade(ones[count + j])) for j in range(count)]
        one = near.reduce(ones[0].reshape((2,) * nr + (own_rows, -1)), nr - 1)
        two = jnp.stack([b.reshape((2,) * nr + (own_rows, -1)) for b in twos])
        two = near.reduce(two, nr)
        for stage in reversed(by_seq):
            count = two.shape[0] // 2
            two = add(two[:count], stage.trade(two[count:]))
        block = jnp.concatenate((one, two[0]), axis=-1)
        for i, stage in reversed(list(enumerate(far))):
            block = stage.reduce(block, i)
        return block.reshape(own_rows, -1).astype(F32)

    cot = own_part(after(cotangent, held_first[0])).astype(F32)

    kept = [
        attend(windows, whole_x, qkv_all[i], qkv_bias(*places[i]), lab_col, lab_row)
        for i in range(2 * seqs)
    ]
    context = jnp.concatenate([k[3] for k in kept], axis=1)
    partial_a = nt(context, jnp.concatenate(wo_all, axis=1))
    own_x = lax.dynamic_slice_in_dim(whole_x, way * part, part, 0)
    hidden_a = scatter_ways(partial_a) + own_x.astype(F32) + bias_o32

    def norm(hidden):
        mean = jnp.mean(hidden, axis=1, keepdims=True)
        square = jnp.mean(hidden * hidden, axis=1, keepdims=True)
        inv_std = lax.rsqrt(square - mean * mean + NORM_EPS)
        return (hidden - mean) * inv_std, inv_std

    def norm_back(incoming, centred, inv_std, gain):
        scaled = incoming * gain
        first = jnp.mean(scaled, axis=1, keepdims=True)
        second = jnp.mean(scaled * centred, axis=1, keepdims=True)
        return inv_std * (scaled - first - centred * second)

    centred_a, inv_std_a = norm(hidden_a)
    normed_a = centred_a * gain_a32 + shift_a32
    whole_y = gather_ways(normed_a.astype(BF16))
    active, slope = zip(
        *[ffn_in(whole_y, in_all[i], in_bias(*places[i])) for i in range(2 * seqs)]
    )
    partial_b = sum(nt(active[i], out_all[i]) for i in range(2 * seqs))
    hidden_b = scatter_ways(partial_b) + bias_out32 + normed_a
    centred_b, inv_std_b = norm(hidden_b)
    output = back_to_features((centred_b * gain_b32 + shift_b32).astype(BF16))

    grad_b = norm_back(cot, centred_b, inv_std_b, gain_b32)
    whole_gb = gather_ways(grad_b.astype(BF16))
    grad_w_out = scatter_weight([tn(whole_gb, a).astype(BF16) for a in active])
    grad_inner, sum_inner = zip(
        *[ffn_back(whole_gb, out_all[i], slope[i]) for i in range(2 * seqs)]
    )
    partial_n = sum(nt(grad_inner[i], in_all[i]) for i in range(2 * seqs))
    grad_w_in = scatter_weight([tn(whole_y, g).astype(BF16) for g in grad_inner])
    grad_normed = scatter_ways(partial_n) + grad_b
    grad_a = norm_back(grad_normed, centred_a, inv_std_a, gain_a32)
    whole_ga = gather_ways(grad_a.astype(BF16))
    grad_wo = scatter_weight([tn(whole_ga, k[3]).astype(BF16) for k in kept])
    grad_projected, sum_projected = zip(
        *[
            attend_back(windows, whole_ga, wo_all[i], *kept[i][:3], kept[i][4], lab_col, lab_row)
            for i in range(2 * seqs)
        ]
    )
    grad_wqkv = scatter_weight([tn(whole_x, g).astype(BF16) for g in grad_projected])
    partial_x = sum(nt(grad_projected[i], qkv_all[i]) for i in range(2 * seqs))
    grad_tokens = back_to_features((scatter_ways(partial_x) + grad_a).astype(BF16)).astype(F32)

    per_hidden = []
    for j in range(seqs):
        two = [sum_projected[2 * j + h].reshape(2, heads // 2, DH).transpose(1, 0, 2) for h in range(2)]
        sums = [s.reshape(-1) for s in two] + [sum_inner[2 * j + h].reshape(-1) for h in range(2)]
        per_hidden.append(jnp.concatenate(sums))
    per_feature = jnp.stack(
        [
            jnp.sum(v, axis=0)
            for v in (
                grad_a,
                grad_normed * centred_a,
                grad_normed,
                grad_b,
                cot * centred_b,
                cot,
            )
        ]
    )
    block = per_feature.reshape((6, seqs) + (2,) * nw + (width,))
    for i, stage in enumerate(by_way):
        block = stage.reduce(block, 2 + i)
    block = block.reshape((6,) + (2,) * ns + (width,))
    for i, stage in enumerate(by_seq):
        block = stage.reduce(block, 1 + i)
    for stage in reversed(by_seq):
        count = len(per_hidden) // 2
        per_hidden = [per_hidden[j] + stage.trade(per_hidden[count + j]) for j in range(count)]
    sums = jnp.concatenate((per_hidden[0], block.reshape(-1)))
    for stage in by_row:
        sums = sums + stage.trade(sums)
    nqv = bias_qv.shape[0]
    sum_qv, sum_in = sums[:nqv], sums[nqv : nqv + hid]
    rest = sums[nqv + hid :].reshape(6, width)
    by_kind = grad_wqkv.reshape(own_rows, 2, 3, heads // 2, DH)
    return (
        output,
        grad_tokens,
        by_kind.transpose(0, 1, 3, 2, 4).reshape(own_rows, -1),
        sum_qv,
        grad_wo.T,
        rest[0],
        rest[1],
        rest[2],
        grad_w_in,
        sum_in,
        grad_w_out.T,
        rest[3],
        rest[4],
        rest[5],
    )


def solution(mesh):
    tile, across, down, flat = P("row", "col"), P("row", None), P("col", "row"), P("col")
    in_specs = (tile, across, tile, flat, down, flat, flat, flat, tile, flat, down, flat, flat, flat, tile)
    out_specs = (tile, tile, tile, flat, down, flat, flat, flat, tile, flat, down, flat, flat, flat)
    rows, cols = mesh.shape["row"], mesh.shape["col"]

    def layer(*args):
        return body(rows, cols, *args)

    return jax.shard_map(layer, mesh=mesh, in_specs=in_specs, out_specs=out_specs, check_vma=False)
```

```python
import functools
import math

import jax
import jax.numpy as jnp
from jax import lax
from jax.experimental import pallas as pl
from jax.experimental.pallas import tpu as pltpu
from jax.sharding import PartitionSpec as P

DH = 64
NORM_EPS = 1e-06
MASKED = -1000000000.0
LONGEST = 256
F32 = jnp.float32
BF16 = jnp.bfloat16


def nn(left, right):
    return lax.dot_general(left, right, (((1,), (0,)), ((), ())), preferred_element_type=F32)


def nt(left, right):
    return lax.dot_general(left, right, (((1,), (1,)), ((), ())), preferred_element_type=F32)


def tn(left, right):
    return lax.dot_general(left, right, (((0,), (0,)), ((), ())), preferred_element_type=F32)


def after(block, *others):
    return lax.optimization_barrier((block,) + others)[0]


def pick(block, bit, dim):
    return lax.dynamic_slice_in_dim(block, bit, 1, dim)


def bits_of(count):
    return [1 << b for b in reversed(range(count.bit_length() - 1))]


class Stage:
    def __init__(self, axis, count, mask, index):
        self.axis, self.pairs = axis, [(i, i ^ mask) for i in range(count)]
        self.bit = (index // mask) % 2

    def trade(self, block):
        return lax.ppermute(block, self.axis, self.pairs)

    def join(self, mine, other, dim):
        low = self.bit == 0
        return jnp.concatenate(
            (jnp.where(low, mine, other), jnp.where(low, other, mine)), axis=dim
        )

    def gather(self, block, dim):
        return self.join(block, self.trade(block), dim)

    def swap(self, block, split, dim):
        keep = pick(block, self.bit, split)
        return self.join(keep, self.trade(pick(block, 1 - self.bit, split)), dim)

    def reduce(self, block, dim):
        got = self.trade(pick(block, 1 - self.bit, dim))
        return add(pick(block, self.bit, dim), got)


def add(mine, other):
    return (mine.astype(F32) + other.astype(F32)).astype(mine.dtype)


def tiles_of(length):
    return min(256, length), min(128, length)


def key_windows(labels):
    rows, step = tiles_of(labels.shape[0])
    first, last = labels[::rows], labels[rows - 1 :: rows]
    start = jnp.sum(labels[None, :] < first[:, None], axis=1)
    stop = jnp.sum(labels[None, :] <= last[:, None], axis=1)
    block = start // step
    return jnp.stack((block, (stop - 1) // step + 1 - block)).astype(jnp.int32)


def for_each_block(windows, length, run):
    rows, step = tiles_of(length)
    reach = -(-(LONGEST - 1) // step)
    most = min(length // step, rows // step + 2 * reach)

    def one(i, carry):
        q0 = pl.multiple_of(i * rows, rows)
        k0 = pl.multiple_of(windows[0, i] * step, step)
        for n in range(1, most + 1):
            pl.when(windows[1, i] == n)(functools.partial(run, q0, k0, rows, n * step))
        return carry

    lax.fori_loop(0, length // rows, one, 0)


def attend_kernel(windows, q_ref, k_ref, v_ref, lab_col, lab_row, ctx_ref, lse_ref):
    length, lanes = q_ref.shape[1:]

    def run(q0, k0, rows, span):
        q = q_ref[0, pl.ds(q0, rows), :]
        k = k_ref[0, pl.ds(k0, span), :]
        v_t = v_ref[0, pl.ds(k0, span), :].T
        same = lab_col[pl.ds(k0, span), :] == lab_row[:, pl.ds(q0, rows)]
        head = lax.broadcasted_iota(jnp.int32, (span, lanes), 1) // DH
        outs = []
        for h in range(lanes // DH):
            scores = nt(jnp.where(head == h, k, jnp.zeros_like(k)), q)
            scores = jnp.where(same, scores, MASKED)
            top = jnp.max(scores, axis=0, keepdims=True)
            shifted = jnp.exp(scores - top)
            total = jnp.sum(shifted, axis=0, keepdims=True)
            outs.append(nn(v_t[h * DH : (h + 1) * DH, :], shifted.astype(BF16)) / total)
            lse_ref[0, h : h + 1, pl.ds(q0, rows)] = top + jnp.log(total)
        ctx_ref[0, pl.ds(q0, rows), :] = jnp.concatenate(outs, axis=0).T.astype(BF16)

    for_each_block(windows, length, run)


def attend_back_kernel(
    windows, q_ref, k_ref, v_ref, do_ref, lse_ref, lab_col, lab_row, gp_ref, sum_ref, dk_acc, dv_acc
):
    length, lanes = q_ref.shape[1:]
    scale = 1.0 / math.sqrt(DH)
    dk_acc[...] = jnp.zeros_like(dk_acc)
    dv_acc[...] = jnp.zeros_like(dv_acc)
    sum_ref[...] = jnp.zeros_like(sum_ref)

    def run(q0, k0, rows, span):
        q = q_ref[0, pl.ds(q0, rows), :]
        do = do_ref[0, pl.ds(q0, rows), :]
        k = k_ref[0, pl.ds(k0, span), :]
        v = v_ref[0, pl.ds(k0, span), :]
        k_t = k.T
        same = lab_col[pl.ds(k0, span), :] == lab_row[:, pl.ds(q0, rows)]
        head = lax.broadcasted_iota(jnp.int32, (span, lanes), 1) // DH
        head_q = lax.broadcasted_iota(jnp.int32, (rows, lanes), 1) // DH
        dqs = []
        dk = dv = None
        for h in range(lanes // DH):
            only = lambda a, own: jnp.where(own == h, a, jnp.zeros_like(a))
            scores = jnp.where(same, nt(only(k, head), q), MASKED)
            prob = jnp.exp(scores - lse_ref[0, h : h + 1, pl.ds(q0, rows)])
            weighted = prob * nt(only(v, head), do)
            row_dot = jnp.sum(weighted, axis=0, keepdims=True)
            dscore = (weighted - prob * row_dot).astype(BF16)
            dv_h = nn(prob.astype(BF16), only(do, head_q))
            dk_h = nn(dscore, only(q, head_q))
            dv = dv_h if dv is None else dv + dv_h
            dk = dk_h if dk is None else dk + dk_h
            dqs.append(nn(k_t[h * DH : (h + 1) * DH, :], dscore))
        dq = jnp.concatenate(dqs, axis=0).T * scale
        gp_ref[0, pl.ds(q0, rows), :lanes] = dq.astype(BF16)
        sum_ref[0, 0:1, :] += jnp.sum(dq, axis=0, keepdims=True)
        dk_acc[pl.ds(k0, span), :] += dk
        dv_acc[pl.ds(k0, span), :] += dv

    for_each_block(windows, length, run)
    gp_ref[0, :, lanes : 2 * lanes] = dk_acc[...].astype(BF16)
    gp_ref[0, :, 2 * lanes :] = dv_acc[...].astype(BF16)
    sum_ref[0, 1:2, :] = jnp.sum(dv_acc[...], axis=0, keepdims=True)


def struct(shape, dtype):
    return jax.ShapeDtypeStruct(shape, dtype)


def fixed(a):
    return pl.BlockSpec(a.shape, lambda i, *_: (0,) * len(a.shape))


def slab(a):
    return pl.BlockSpec((1,) + a.shape[1:], lambda i, *_: (i,) + (0,) * (len(a.shape) - 1))


def launch(kernel, grid, scalars, operands, specs, outs, out_specs, scratch, flops, name, aliases=None):
    moved = sum(math.prod(a.shape) * a.dtype.itemsize for a in list(operands) + list(outs))
    return pl.pallas_call(
        kernel,
        grid_spec=pltpu.PrefetchScalarGridSpec(
            num_scalar_prefetch=len(scalars),
            grid=(grid,),
            in_specs=specs,
            out_specs=out_specs,
            scratch_shapes=scratch,
        ),
        out_shape=outs,
        input_output_aliases=aliases or {},
        cost_estimate=pl.CostEstimate(flops=flops, transcendentals=0, bytes_accessed=moved),
        name=name,
    )(*scalars, *operands)


def attend(windows, q, k, v, lab_col, lab_row):
    slabs, length, lanes = q.shape
    operands = [q, k, v, lab_col, lab_row]
    specs = [slab(q)] * 3 + [fixed(lab_col), fixed(lab_row)]
    outs = [struct(q.shape, BF16), struct((slabs, lanes // DH, length), F32)]
    return launch(
        attend_kernel, slabs, [windows], operands, specs, outs, [slab(a) for a in outs], [],
        40 * slabs * length * 640 * lanes, "attend",
    )


def attend_back(windows, q, k, v, do, lse, lab_col, lab_row):
    slabs, length, lanes = q.shape
    operands = [q, k, v, do, lse, lab_col, lab_row]
    specs = [slab(a) for a in operands[:5]] + [fixed(lab_col), fixed(lab_row)]
    outs = [struct((slabs, length, 3 * lanes), BF16), struct((slabs, 2, lanes), F32)]
    return launch(
        attend_back_kernel, slabs, [windows], operands, specs, outs, [slab(a) for a in outs],
        [pltpu.VMEM((length, lanes), F32)] * 2, 60 * slabs * length * 640 * lanes, "attend_back",
    )


def row_tile(length):
    return min(256, length)


def tall(a, tile):
    if len(a.shape) == 2:
        return pl.BlockSpec((tile, a.shape[1]), lambda i, *_: (i, 0))
    return pl.BlockSpec((a.shape[0], tile, a.shape[2]), lambda i, *_: (0, i, 0))


def tall_from(a, tile, per):
    if len(a.shape) == 2:
        return pl.BlockSpec((tile, a.shape[1]), lambda i, at: (at[0] * per + i, 0))
    return pl.BlockSpec((a.shape[0], tile, a.shape[2]), lambda i, at: (0, at[0] * per + i, 0))


def project_kernel(x_ref, b_ref, *refs):
    count = b_ref.shape[0]
    weights, (q_ref, k_ref, v_ref) = refs[:count], refs[count:]
    lanes = q_ref.shape[2]
    scale = 1.0 / math.sqrt(DH)
    x = x_ref[...]
    for i in range(count):
        projected = nn(x, weights[i][...]) + b_ref[i]
        q_ref[i] = (projected[:, :lanes].astype(BF16).astype(F32) * scale).astype(BF16)
        k_ref[i] = projected[:, lanes : 2 * lanes].astype(BF16)
        v_ref[i] = projected[:, 2 * lanes :].astype(BF16)


def project(x, weights, bias):
    length, model = x.shape
    lanes = weights[0].shape[1] // 3
    tile = row_tile(length)
    outs = [struct((len(weights), length, lanes), BF16)] * 3
    return launch(
        project_kernel, length // tile, [], [x, bias] + weights,
        [tall(x, tile), fixed(bias)] + [fixed(w) for w in weights], outs,
        [tall(a, tile) for a in outs], [], 6 * length * model * lanes * len(weights), "project",
    )


def context_out_kernel(at, ctx_ref, *refs):
    weights, out_ref = refs[:-1], refs[-1]
    lanes = ctx_ref.shape[2]
    left = jnp.concatenate([ctx_ref[i] for i in range(len(weights))], axis=1)
    right = jnp.concatenate([w[:, w.shape[1] - lanes :] for w in weights], axis=1)
    out_ref[...] = nt(left, right).astype(out_ref.dtype)


def context_out(at, ctx, weights, part, dtype):
    tile = row_tile(part)
    model = weights[0].shape[0]
    out = struct((part, model), dtype)
    return launch(
        context_out_kernel, part // tile, [at], [ctx] + weights,
        [tall_from(ctx, tile, part // tile)] + [fixed(w) for w in weights], [out], [tall(out, tile)], [],
        2 * part * model * ctx.shape[0] * ctx.shape[2], "context_out",
    )[0]


def context_back_kernel(ga_ref, *refs):
    weights, out_ref = refs[:-1], refs[-1]
    lanes = out_ref.shape[2]
    right = jnp.concatenate([w[:, w.shape[1] - lanes :] for w in weights], axis=1)
    grad = nn(ga_ref[...], right).astype(BF16)
    for i in range(len(weights)):
        out_ref[i] = grad[:, i * lanes : (i + 1) * lanes]


def context_back(ga, weights, lanes):
    tile = row_tile(ga.shape[0])
    out = struct((len(weights), ga.shape[0], lanes), BF16)
    return launch(
        context_back_kernel, ga.shape[0] // tile, [], [ga] + weights,
        [tall(ga, tile)] + [fixed(w) for w in weights], [out], [tall(out, tile)], [],
        2 * math.prod(ga.shape) * lanes * len(weights), "context_back",
    )[0]


def ffn_in_kernel(y_ref, b_ref, *refs):
    count = b_ref.shape[0]
    wide = b_ref.shape[2]
    weights, (act_ref, slope_ref) = refs[:count], refs[-2:]
    y = y_ref[...]
    for i in range(count):
        inner = nn(y, weights[i][:, :wide]) + b_ref[i]
        share = 0.5 + 0.5 * lax.erf(inner * math.sqrt(0.5))
        density = jnp.exp(-0.5 * inner * inner) * (1.0 / math.sqrt(2.0 * math.pi))
        act_ref[i] = (inner * share).astype(BF16)
        slope_ref[i] = (share + inner * density).astype(BF16)


def place(a, tile, first):
    return pl.BlockSpec((a.shape[0], tile, a.shape[2]), lambda i, *_: (0, first + i, 0))


def ffn_in(y, bias, weights, ways, place_at, earlier):
    part, model = y.shape
    tile = row_tile(part)
    first = place_at * (part // tile)
    wide = bias.shape[2]
    count = len(weights)
    out = struct((count, part * ways, wide), BF16)
    anywhere = [pl.BlockSpec(memory_space=pl.ANY)] * len(earlier)
    return launch(
        ffn_in_kernel, part // tile, [], [y, bias] + weights + earlier,
        [tall(y, tile), fixed(bias)] + [fixed(w) for w in weights] + anywhere,
        [out, out], [place(out, tile, first)] * 2, [],
        6 * part * model * wide * count, "ffn_in",
        {2 + count + i: i for i in range(len(earlier))},
    )


def ffn_out_kernel(act_ref, *refs):
    weights, out_ref = refs[:-1], refs[-1]
    total = nt(act_ref[0], weights[0][...])
    for i in range(1, len(weights)):
        total += nt(act_ref[i], weights[i][...])
    out_ref[...] = total.astype(out_ref.dtype)


def ffn_out(act, weights, part, place_at, dtype):
    tile = row_tile(part)
    model = weights[0].shape[0]
    out = struct((part, model), dtype)
    return launch(
        ffn_out_kernel, part // tile, [], [act] + weights,
        [place(act, tile, place_at * (part // tile))] + [fixed(w) for w in weights],
        [out], [tall(out, tile)], [], 2 * part * model * act.shape[0] * act.shape[2], "ffn_out",
    )[0]


def ffn_back_kernel(gb_ref, slope_ref, *refs):
    count = slope_ref.shape[0]
    wide = slope_ref.shape[2]
    outs, ins = refs[:count], refs[count : 2 * count]
    gi_ref, sum_ref, out_ref = refs[-3:]
    gb = gb_ref[...]
    total = None
    sums = []
    for i in range(count):
        grad = nn(gb, outs[i][...]) * slope_ref[i].astype(F32)
        low = grad.astype(BF16)
        gi_ref[i] = low
        sums.append(jnp.sum(grad, axis=0, keepdims=True))
        term = nt(low, ins[i][:, :wide])
        total = term if total is None else total + term
    out_ref[...] = total.astype(out_ref.dtype)

    @pl.when(pl.program_id(0) == 0)
    def _():
        sum_ref[...] = jnp.zeros_like(sum_ref)

    for i in range(count):
        sum_ref[i] += sums[i]


def ffn_back(gb, slope, outs_w, ins_w, place_at, earlier, dtype):
    part, model = gb.shape
    tile = row_tile(part)
    first = place_at * (part // tile)
    count, _, wide = slope.shape
    anywhere = [pl.BlockSpec(memory_space=pl.ANY)] * len(earlier)
    outs = [struct(slope.shape, BF16), struct((count, 1, wide), F32), struct((part, model), dtype)]
    return launch(
        ffn_back_kernel, part // tile, [], [gb, slope] + outs_w + ins_w + earlier,
        [tall(gb, tile), place(slope, tile, first)] + [fixed(w) for w in outs_w + ins_w] + anywhere,
        outs, [place(outs[0], tile, first), fixed(outs[1]), tall(outs[2], tile)], [],
        4 * part * model * wide * count, "ffn_back",
        {2 + 2 * count + i: i for i in range(len(earlier))},
    )


def inputs_back_kernel(at, gp_ref, *refs):
    weights, out_ref = refs[:-1], refs[-1]
    total = nt(gp_ref[0], weights[0][...])
    for i in range(1, len(weights)):
        total += nt(gp_ref[i], weights[i][...])
    out_ref[...] = total.astype(out_ref.dtype)


def inputs_back(at, gp, weights, part, dtype):
    tile = row_tile(part)
    model = weights[0].shape[0]
    out = struct((part, model), dtype)
    return launch(
        inputs_back_kernel, part // tile, [at], [gp] + weights,
        [tall_from(gp, tile, part // tile)] + [fixed(w) for w in weights], [out], [tall(out, tile)], [],
        2 * part * model * gp.shape[0] * gp.shape[2], "inputs_back",
    )[0]


def weight_grad(left, right):
    length, model = left.shape
    count, _, wide = right.shape
    out = struct((count, model, wide), BF16)

    def kernel(left_ref, right_ref, out_ref, left_t):
        @pl.when(pl.program_id(0) == 0)
        def _():
            left_t[...] = left_ref[...].T

        out_ref[0] = nn(left_t[...], right_ref[0]).astype(BF16)

    stack = launch(
        kernel, count, [], [left, right], [fixed(left), slab(right)], [out], [slab(out)],
        [pltpu.VMEM((model, length), BF16)], 2 * length * model * wide * count, "weight_grad",
    )[0]
    return [stack[i] for i in range(count)]


def norm_rows(hidden):
    mean = jnp.mean(hidden, axis=1, keepdims=True)
    square = jnp.mean(hidden * hidden, axis=1, keepdims=True)
    inv_std = lax.rsqrt(square - mean * mean + NORM_EPS)
    return (hidden - mean) * inv_std, inv_std


def norm_rows_back(incoming, centred, inv_std, gain):
    scaled = incoming * gain
    first = jnp.mean(scaled, axis=1, keepdims=True)
    second = jnp.mean(scaled * centred, axis=1, keepdims=True)
    return inv_std * (scaled - first - centred * second)


def add_sums(sum_ref, terms):
    @pl.when(pl.program_id(0) == 0)
    def _():
        sum_ref[...] = jnp.zeros_like(sum_ref)

    for i, term in enumerate(terms):
        sum_ref[i : i + 1, :] += jnp.sum(term, axis=0, keepdims=True)


def norm_a_kernel(at, mine_ref, got_ref, x_ref, vec_ref, centred_ref, inv_ref, y_ref):
    hidden = mine_ref[...] + got_ref[...].astype(F32) + x_ref[...].astype(F32) + vec_ref[0]
    centred, inv_std = norm_rows(hidden)
    centred_ref[...] = centred
    inv_ref[...] = inv_std
    y_ref[...] = (centred * vec_ref[1] + vec_ref[2]).astype(BF16)


def norm_a(at, mine, got, x, vec):
    part, model = mine.shape
    tile = row_tile(part)
    outs = [struct((part, model), F32), struct((part, 1), F32), struct((part, model), BF16)]
    return launch(
        norm_a_kernel, part // tile, [at], [mine, got, x, vec],
        [tall(mine, tile), tall(got, tile), tall_from(x, tile, part // tile), fixed(vec)],
        outs, [tall(a, tile) for a in outs], [], 20 * part * model, "norm_a",
    )


def norm_b_kernel(mine_ref, got_ref, centred_a_ref, cot_ref, vec_ref, out_ref, grad_ref, low_ref, sum_ref):
    normed = centred_a_ref[...] * vec_ref[1] + vec_ref[2]
    hidden = mine_ref[...] + got_ref[...].astype(F32) + vec_ref[3] + normed
    centred, inv_std = norm_rows(hidden)
    out_ref[...] = (centred * vec_ref[4] + vec_ref[5]).astype(BF16)
    incoming = cot_ref[...].astype(F32)
    grad = norm_rows_back(incoming, centred, inv_std, vec_ref[4])
    grad_ref[...] = grad
    low_ref[...] = grad.astype(BF16)
    add_sums(sum_ref, (grad, incoming * centred, incoming))


def norm_b(mine, got, centred_a, cot, vec):
    part, model = mine.shape
    tile = row_tile(part)
    outs = [struct((part, model), BF16), struct((part, model), F32), struct((part, model), BF16), struct((3, model), F32)]
    return launch(
        norm_b_kernel, part // tile, [], [mine, got, centred_a, cot, vec],
        [tall(a, tile) for a in (mine, got, centred_a, cot)] + [fixed(vec)],
        outs, [tall(a, tile) for a in outs[:3]] + [fixed(outs[3])], [], 40 * part * model, "norm_b",
    )


def norm_a_back_kernel(mine_ref, got_ref, gb_ref, centred_ref, inv_ref, vec_ref, grad_ref, low_ref, sum_ref):
    incoming = mine_ref[...] + got_ref[...].astype(F32) + gb_ref[...]
    centred = centred_ref[...]
    grad = norm_rows_back(incoming, centred, inv_ref[...], vec_ref[1])
    grad_ref[...] = grad
    low_ref[...] = grad.astype(BF16)
    add_sums(sum_ref, (grad, incoming * centred, incoming))


def norm_a_back(mine, got, gb, centred, inv, vec):
    part, model = mine.shape
    tile = row_tile(part)
    outs = [struct((part, model), F32), struct((part, model), BF16), struct((3, model), F32)]
    return launch(
        norm_a_back_kernel, part // tile, [], [mine, got, gb, centred, inv, vec],
        [tall(a, tile) for a in (mine, got, gb, centred, inv)] + [fixed(vec)],
        outs, [tall(a, tile) for a in outs[:2]] + [fixed(outs[2])], [], 30 * part * model, "norm_a_back",
    )


def body(
    rows,
    cols,
    tokens,
    segments,
    wqkv,
    bias_qv,
    wo,
    bias_o,
    gain_a,
    shift_a,
    w_in,
    bias_in,
    w_out,
    bias_out,
    gain_b,
    shift_b,
    cotangent,
):
    seqs, length = segments.shape
    ways = cols // seqs
    width = tokens.shape[1]
    model = width * cols
    heads = wqkv.shape[1] // (3 * DH)
    lanes = heads * DH // 2
    hid = w_in.shape[1]
    part = length // ways
    own_rows = wqkv.shape[0]
    row, col = lax.axis_index("row"), lax.axis_index("col")
    seq, way = col // ways, col % ways
    by_seq = [Stage("col", cols, mask * ways, col) for mask in bits_of(seqs)]
    by_way = [Stage("col", cols, mask, col) for mask in bits_of(ways)]
    by_row = [Stage("row", rows, mask, row) for mask in bits_of(rows)]
    ns, nw, nr = len(by_seq), len(by_way), len(by_row)
    far, near = by_row[:-1], by_row[-1]
    parts = range(ways)
    at = [((way ^ p) * jnp.ones((1,), jnp.int32)).astype(jnp.int32) for p in parts]

    def gather_far(one, two):
        halves = [h.reshape((1,) * nr + h.shape) for h in (one, two)]
        for i, stage in enumerate(far):
            both = jnp.stack(halves)
            got = stage.trade(both)
            halves = [stage.join(both[h], got[h], i) for h in range(2)]
        return halves

    def gather_near(block):
        return near.gather(block, nr - 1).reshape(model, -1)

    def gather_last(one, two):
        ones, twos = [gather_near(one)], [two]
        for stage in by_seq:
            twos = twos + [stage.trade(b) for b in twos]
        two = after(two, ones[0])
        twos = [gather_near(b) for b in [two] + twos[1:]]
        for stage in by_seq:
            ones = ones + [stage.trade(b) for b in ones]
        return [b for j in range(seqs) for b in (ones[j], twos[j])]

    def halves_of(weight):
        half = weight.shape[1] // 2
        return weight[:, :half], weight[:, half:]

    by_kind = wqkv.reshape(own_rows, 2, heads // 2, 3, DH).transpose(1, 0, 3, 2, 4)
    by_kind = by_kind.reshape(2, own_rows, -1)
    far_qkv = gather_far(by_kind[0], by_kind[1])

    labels = lax.dynamic_slice_in_dim(segments, seq, 1, 0)[0]
    windows = key_windows(labels)
    lab_col, lab_row = labels[:, None], labels[None, :]

    def exchange(array, split, whole):
        blocks = [array]
        for stage in split + whole:
            both = blocks[0] if len(blocks) == 1 else jnp.concatenate(blocks, axis=1)
            if stage in split:
                both = both.reshape(2, both.shape[0] // 2, both.shape[1])
                mine, sent = pick(both, stage.bit, 0)[0], pick(both, 1 - stage.bit, 0)[0]
            else:
                mine = sent = both
            got = stage.trade(sent)
            low = stage.bit == 0
            blocks = [
                half
                for i in range(len(blocks))
                for a, b in [(mine[:, i * width : (i + 1) * width], got[:, i * width : (i + 1) * width])]
                for half in (jnp.where(low, a, b), jnp.where(low, b, a))
            ]
        return jnp.concatenate(blocks, axis=1)

    def to_features(array):
        blocks = [array]
        for stage in by_seq + by_way:
            half = blocks[0].shape[1] // 2
            both = blocks[0] if len(blocks) == 1 else jnp.concatenate(blocks, axis=0)
            mine = lax.dynamic_slice_in_dim(both, stage.bit * half, half, 1)
            got = stage.trade(lax.dynamic_slice_in_dim(both, (1 - stage.bit) * half, half, 1))
            low = stage.bit == 0
            count = array.shape[0]
            blocks = [
                half_rows
                for i in range(len(blocks))
                for a, b in [(mine[i * count : (i + 1) * count], got[i * count : (i + 1) * count])]
                for half_rows in (jnp.where(low, a, b), jnp.where(low, b, a))
            ]
        return jnp.concatenate(blocks, axis=0)

    whole_x = exchange(after(tokens, far_qkv[0]), by_seq, by_way)
    vectors = jnp.concatenate(
        [v.reshape(-1, width) for v in (bias_o, gain_a, shift_a, bias_out, gain_b, shift_b, bias_qv, bias_in)]
    )
    vectors = after(vectors, far_qkv[0])
    pairs = [vectors]
    for stage in by_seq:
        pairs = pairs + [stage.trade(v) for v in pairs]
    blocks = [vectors[:6]]
    for i, stage in enumerate(by_seq):
        got = jnp.concatenate([p[:6] for p in pairs[1 << i : 2 << i]], axis=1)
        low = stage.bit == 0
        both = jnp.concatenate(blocks, axis=1)
        blocks = [
            half
            for k in range(len(blocks))
            for a, b in [(both[:, k * width : (k + 1) * width], got[:, k * width : (k + 1) * width])]
            for half in (jnp.where(low, a, b), jnp.where(low, b, a))
        ]
    for stage in by_way:
        both = jnp.concatenate(blocks, axis=1)
        got = stage.trade(both)
        low = stage.bit == 0
        blocks = [
            half
            for k in range(len(blocks))
            for a, b in [(both[:, k * width : (k + 1) * width], got[:, k * width : (k + 1) * width])]
            for half in (jnp.where(low, a, b), jnp.where(low, b, a))
        ]
    vec = jnp.concatenate(blocks, axis=1).astype(F32)[:, None, :]
    nq = bias_qv.shape[0] // width
    q_biases, in_biases = [], []
    for j in range(seqs):
        both = pairs[j][6 : 6 + nq].astype(F32).reshape(2, heads // 2, 2, DH)
        both = both.transpose(0, 2, 1, 3).reshape(2, 2, lanes)
        q_biases.append(jnp.concatenate((both[:, :1], jnp.zeros_like(both[:, :1]), both[:, 1:]), axis=1))
        in_biases.append(pairs[j][6 + nq :].astype(F32).reshape(2, 1, hid // 2))
    q_bias = jnp.concatenate(q_biases, axis=0).reshape(2 * seqs, 1, 3 * lanes)
    in_bias = jnp.concatenate(in_biases, axis=0)

    qkv_all = gather_last(*far_qkv)
    wo_t, out_t = halves_of(wo.T), halves_of(w_out.T)
    both_in = [jnp.concatenate((a, b), axis=1) for a, b in zip(halves_of(w_in), wo_t)]
    far_in = gather_far(*[after(b, *far_qkv) for b in both_in])
    far_out = gather_far(*[after(b, *far_in) for b in out_t])
    in_all = gather_last(*[after(b, qkv_all[0], qkv_all[3]) for b in far_in])
    out_all = gather_last(*[after(b, in_all[0], in_all[3]) for b in far_out])
    cot = exchange(after(cotangent, qkv_all[2]), by_seq + by_way, [])

    def gather_parts(own):
        blocks = {0: own}
        for mask, stage in zip(bits_of(ways), by_way):
            for p in list(blocks):
                blocks[p ^ mask] = stage.trade(blocks[p])
        return [blocks[p] for p in parts]

    def scatter_parts(make):
        terms = {p: make(p, F32 if p == 0 else BF16) for p in reversed(parts)}
        for mask, stage in list(zip(bits_of(ways), by_way))[:-1]:
            for p in [q for q in terms if q & mask]:
                got = stage.trade(terms.pop(p))
                terms[p ^ mask] = add(terms[p ^ mask], got)
        return terms[0], by_way[-1].trade(terms[1])

    def whole_rows(blocks):
        blocks = list(blocks)
        for mask, stage in zip(reversed(bits_of(ways)), reversed(by_way)):
            low = stage.bit == 0
            for p in parts:
                if not p & mask:
                    a, b = blocks[p], blocks[p | mask]
                    blocks[p], blocks[p | mask] = jnp.where(low, a, b), jnp.where(low, b, a)
        return jnp.concatenate(blocks, axis=0)

    def scatter_first(blocks):
        ones, twos = blocks[0::2], blocks[1::2]
        fold = lambda b: near.reduce(b.reshape((2,) * nr + (own_rows, -1)), nr - 1)
        for stage in reversed(by_seq):
            count = len(ones) // 2
            ones = [add(ones[j], stage.trade(ones[count + j])) for j in range(count)]
        twos = [fold(b) for b in reversed(twos)][::-1]
        for stage in reversed(by_seq):
            count = len(twos) // 2
            twos = [add(twos[j], stage.trade(twos[count + j])) for j in range(count)]
        return fold(ones[0]), twos[0]

    def scatter_far(one, two):
        for i, stage in reversed(list(enumerate(far))):
            halves = (one, two)
            sent = jnp.stack([pick(b, 1 - stage.bit, i) for b in halves])
            got = stage.trade(sent)
            one, two = [add(pick(b, stage.bit, i), got[h]) for h, b in enumerate(halves)]
        return one.reshape(own_rows, -1).astype(F32), two.reshape(own_rows, -1).astype(F32)

    q, k, v = project(whole_x, qkv_all, q_bias)
    context, lse = attend(windows, q, k, v, lab_col, lab_row)
    mine, got = scatter_parts(lambda p, dtype: context_out(at[p], context, in_all, part, dtype))
    centred_a, inv_a, y = norm_a(at[0], mine, got, whole_x, vec)
    y_parts = gather_parts(y)
    earlier = []
    for p in parts:
        earlier = ffn_in(y_parts[p], in_bias, in_all, ways, p, list(earlier))
    active, slope = earlier
    mine, got = scatter_parts(lambda p, dtype: ffn_out(active, out_all, part, p, dtype))
    output, grad_b, gb, sums_b = norm_b(mine, got, centred_a, cot, vec)

    gb_parts = gather_parts(gb)
    output = to_features(after(output, gb_parts[-1]))
    terms, sum_in, earlier = {}, 0.0, []
    for p in parts:
        grad_inner, sums, terms[p] = ffn_back(
            gb_parts[p], slope, out_all, in_all, p, earlier, F32 if p == 0 else BF16
        )
        earlier = [grad_inner]
        sum_in = sum_in + sums
    mine, got = scatter_parts(lambda p, dtype: terms[p])
    grad_w_out = weight_grad(jnp.concatenate(gb_parts, axis=0), active)
    grad_w_in = weight_grad(jnp.concatenate(y_parts, axis=0), grad_inner)
    first_out = scatter_first(grad_w_out)
    grad_a, ga, sums_a = norm_a_back(mine, got, grad_b, centred_a, inv_a, vec)
    whole_ga = whole_rows(gather_parts(ga))
    grad_context = context_back(whole_ga, in_all, lanes)
    first_in = scatter_first([after(b, *first_out) for b in grad_w_in])
    out_halves = scatter_far(*first_out)
    grad_projected, sum_projected = attend_back(windows, q, k, v, grad_context, lse, lab_col, lab_row)
    in_halves = scatter_far(*first_in)
    grad_wo = weight_grad(whole_ga, context)
    grad_wqkv = weight_grad(whole_x, grad_projected)
    last = scatter_first([jnp.concatenate(two, axis=1) for two in zip(grad_wqkv, grad_wo)])
    mine, got = scatter_parts(lambda p, dtype: inputs_back(at[p], grad_projected, qkv_all, part, dtype))
    grad_tokens = to_features((mine + got.astype(F32) + grad_a).astype(BF16)).astype(F32)
    qkv_halves = scatter_far(*last)

    per_hidden = []
    for j in range(seqs):
        two = sum_projected[2 * j : 2 * j + 2].reshape(2, 2, heads // 2, DH).transpose(0, 2, 1, 3)
        per_hidden.append(jnp.concatenate((two.reshape(-1), sum_in[2 * j : 2 * j + 2].reshape(-1))))
    block = jnp.concatenate((sums_a, sums_b), axis=0)
    for stage in by_seq + by_way:
        half = block.shape[1] // 2
        got = stage.trade(lax.dynamic_slice_in_dim(block, (1 - stage.bit) * half, half, 1))
        block = lax.dynamic_slice_in_dim(block, stage.bit * half, half, 1) + got
    for stage in reversed(by_seq):
        count = len(per_hidden) // 2
        per_hidden = [per_hidden[j] + stage.trade(per_hidden[count + j]) for j in range(count)]
    sums = jnp.concatenate((per_hidden[0], block.reshape(-1)))
    for stage in by_row:
        sums = sums + stage.trade(sums)
    nqv = bias_qv.shape[0]
    sum_qv, sum_in = sums[:nqv], sums[nqv : nqv + hid]
    rest = sums[nqv + hid :].reshape(6, width)
    split = 3 * lanes
    grad_qkv = jnp.stack([h[:, :split] for h in qkv_halves])
    grad_qkv = grad_qkv.reshape(2, own_rows, 3, heads // 2, DH).transpose(1, 0, 3, 2, 4)
    return (
        output,
        grad_tokens,
        grad_qkv.reshape(own_rows, -1),
        sum_qv,
        jnp.concatenate([h[:, split:] for h in qkv_halves], axis=1).T,
        rest[0],
        rest[1],
        rest[2],
        jnp.concatenate(in_halves, axis=1),
        sum_in,
        jnp.concatenate(out_halves, axis=1).T,
        rest[3],
        rest[4],
        rest[5],
    )


def solution(mesh):
    tile, across, down, flat = P("row", "col"), P("row", None), P("col", "row"), P("col")
    in_specs = (tile, across, tile, flat, down, flat, flat, flat, tile, flat, down, flat, flat, flat, tile)
    out_specs = (tile, tile, tile, flat, down, flat, flat, flat, tile, flat, down, flat, flat, flat)
    rows, cols = mesh.shape["row"], mesh.shape["col"]

    def layer(*args):
        return body(rows, cols, *args)

    return jax.shard_map(layer, mesh=mesh, in_specs=in_specs, out_specs=out_specs, check_vma=False)
```

```python
import functools
import math

import jax
import jax.numpy as jnp
from jax import lax
from jax.experimental import pallas as pl
from jax.experimental.pallas import tpu as pltpu
from jax.sharding import PartitionSpec as P

DH = 64
NORM_EPS = 1e-06
MASKED = -1000000000.0
LONGEST = 256
COL = ("seq", "way")
F32 = jnp.float32
BF16 = jnp.bfloat16


def nn(left, right):
    return lax.dot_general(left, right, (((1,), (0,)), ((), ())), preferred_element_type=F32)


def nt(left, right):
    return lax.dot_general(left, right, (((1,), (1,)), ((), ())), preferred_element_type=F32)


def tn(left, right):
    return lax.dot_general(left, right, (((0,), (0,)), ((), ())), preferred_element_type=F32)


def after(block, *others):
    return lax.optimization_barrier((block,) + others)[0]


def pick(block, bit, dim):
    return lax.dynamic_slice_in_dim(block, bit, 1, dim)


def bits_of(count):
    return [1 << b for b in reversed(range(count.bit_length() - 1))]


class Stage:
    def __init__(self, axis, count, mask, index):
        self.axis, self.pairs = axis, [(i, i ^ mask) for i in range(count)]
        self.bit = (index // mask) % 2

    def trade(self, block):
        return lax.ppermute(block, self.axis, self.pairs)

    def join(self, mine, other, dim):
        low = self.bit == 0
        return jnp.concatenate(
            (jnp.where(low, mine, other), jnp.where(low, other, mine)), axis=dim
        )

    def gather(self, block, dim):
        return self.join(block, self.trade(block), dim)

    def swap(self, block, split, dim):
        keep = pick(block, self.bit, split)
        return self.join(keep, self.trade(pick(block, 1 - self.bit, split)), dim)

    def reduce(self, block, dim):
        got = self.trade(pick(block, 1 - self.bit, dim))
        return add(pick(block, self.bit, dim), got)


def add(mine, other):
    return (mine.astype(F32) + other.astype(F32)).astype(mine.dtype)


def tiles_of(length):
    return min(256, length), min(128, length)


def key_windows(labels):
    rows, step = tiles_of(labels.shape[0])
    first, last = labels[::rows], labels[rows - 1 :: rows]
    start = jnp.sum(labels[None, :] < first[:, None], axis=1)
    stop = jnp.sum(labels[None, :] <= last[:, None], axis=1)
    block = start // step
    return jnp.stack((block, (stop - 1) // step + 1 - block)).astype(jnp.int32)


def for_each_block(windows, length, run):
    rows, step = tiles_of(length)
    reach = -(-(LONGEST - 1) // step)
    most = min(length // step, rows // step + 2 * reach)

    def one(i, carry):
        q0 = pl.multiple_of(i * rows, rows)
        k0 = pl.multiple_of(windows[0, i] * step, step)
        for n in range(1, most + 1):
            pl.when(windows[1, i] == n)(functools.partial(run, q0, k0, rows, n * step))
        return carry

    lax.fori_loop(0, length // rows, one, 0)


def attend_kernel(windows, q_ref, k_ref, v_ref, lab_col, lab_row, ctx_ref, lse_ref):
    length, lanes = q_ref.shape[1:]

    def run(q0, k0, rows, span):
        q = q_ref[0, pl.ds(q0, rows), :]
        k = k_ref[0, pl.ds(k0, span), :]
        v_t = v_ref[0, pl.ds(k0, span), :].T
        same = lab_col[pl.ds(k0, span), :] == lab_row[:, pl.ds(q0, rows)]
        head = lax.broadcasted_iota(jnp.int32, (span, lanes), 1) // DH
        outs = []
        for h in range(lanes // DH):
            scores = nt(jnp.where(head == h, k, jnp.zeros_like(k)), q)
            scores = jnp.where(same, scores, MASKED)
            top = jnp.max(scores, axis=0, keepdims=True)
            shifted = jnp.exp(scores - top)
            total = jnp.sum(shifted, axis=0, keepdims=True)
            outs.append(nn(v_t[h * DH : (h + 1) * DH, :], shifted.astype(BF16)) / total)
            lse_ref[0, h : h + 1, pl.ds(q0, rows)] = top + jnp.log(total)
        ctx_ref[0, pl.ds(q0, rows), :] = jnp.concatenate(outs, axis=0).T.astype(BF16)

    for_each_block(windows, length, run)


def attend_back_kernel(
    windows, q_ref, k_ref, v_ref, do_ref, lse_ref, lab_col, lab_row, gp_ref, sum_ref, dk_acc, dv_acc
):
    length, lanes = q_ref.shape[1:]
    scale = 1.0 / math.sqrt(DH)
    dk_acc[...] = jnp.zeros_like(dk_acc)
    dv_acc[...] = jnp.zeros_like(dv_acc)
    sum_ref[...] = jnp.zeros_like(sum_ref)

    def run(q0, k0, rows, span):
        q = q_ref[0, pl.ds(q0, rows), :]
        do = do_ref[0, pl.ds(q0, rows), :]
        k = k_ref[0, pl.ds(k0, span), :]
        v = v_ref[0, pl.ds(k0, span), :]
        k_t = k.T
        same = lab_col[pl.ds(k0, span), :] == lab_row[:, pl.ds(q0, rows)]
        head = lax.broadcasted_iota(jnp.int32, (span, lanes), 1) // DH
        head_q = lax.broadcasted_iota(jnp.int32, (rows, lanes), 1) // DH
        dqs = []
        dk = dv = None
        for h in range(lanes // DH):
            only = lambda a, own: jnp.where(own == h, a, jnp.zeros_like(a))
            scores = jnp.where(same, nt(only(k, head), q), MASKED)
            prob = jnp.exp(scores - lse_ref[0, h : h + 1, pl.ds(q0, rows)])
            weighted = prob * nt(only(v, head), do)
            row_dot = jnp.sum(weighted, axis=0, keepdims=True)
            dscore = (weighted - prob * row_dot).astype(BF16)
            dv_h = nn(prob.astype(BF16), only(do, head_q))
            dk_h = nn(dscore, only(q, head_q))
            dv = dv_h if dv is None else dv + dv_h
            dk = dk_h if dk is None else dk + dk_h
            dqs.append(nn(k_t[h * DH : (h + 1) * DH, :], dscore))
        dq = jnp.concatenate(dqs, axis=0).T * scale
        gp_ref[0, pl.ds(q0, rows), :lanes] = dq.astype(BF16)
        sum_ref[0, 0:1, :] += jnp.sum(dq, axis=0, keepdims=True)
        dk_acc[pl.ds(k0, span), :] += dk
        dv_acc[pl.ds(k0, span), :] += dv

    for_each_block(windows, length, run)
    gp_ref[0, :, lanes : 2 * lanes] = dk_acc[...].astype(BF16)
    gp_ref[0, :, 2 * lanes :] = dv_acc[...].astype(BF16)
    sum_ref[0, 1:2, :] = jnp.sum(dv_acc[...], axis=0, keepdims=True)


def struct(shape, dtype):
    return jax.ShapeDtypeStruct(shape, dtype)


def fixed(a):
    return pl.BlockSpec(a.shape, lambda i, *_: (0,) * len(a.shape))


def slab(a):
    return pl.BlockSpec((1,) + a.shape[1:], lambda i, *_: (i,) + (0,) * (len(a.shape) - 1))


def launch(kernel, grid, scalars, operands, specs, outs, out_specs, scratch, flops, name, aliases=None):
    moved = sum(math.prod(a.shape) * a.dtype.itemsize for a in list(operands) + list(outs))
    return pl.pallas_call(
        kernel,
        grid_spec=pltpu.PrefetchScalarGridSpec(
            num_scalar_prefetch=len(scalars),
            grid=(grid,),
            in_specs=specs,
            out_specs=out_specs,
            scratch_shapes=scratch,
        ),
        out_shape=outs,
        input_output_aliases=aliases or {},
        cost_estimate=pl.CostEstimate(flops=flops, transcendentals=0, bytes_accessed=moved),
        name=name,
    )(*scalars, *operands)


def attend(windows, q, k, v, lab_col, lab_row):
    slabs, length, lanes = q.shape
    operands = [q, k, v, lab_col, lab_row]
    specs = [slab(q)] * 3 + [fixed(lab_col), fixed(lab_row)]
    outs = [struct(q.shape, BF16), struct((slabs, lanes // DH, length), F32)]
    return launch(
        attend_kernel, slabs, [windows], operands, specs, outs, [slab(a) for a in outs], [],
        40 * slabs * length * 640 * lanes, "attend",
    )


def attend_back(windows, q, k, v, do, lse, lab_col, lab_row):
    slabs, length, lanes = q.shape
    operands = [q, k, v, do, lse, lab_col, lab_row]
    specs = [slab(a) for a in operands[:5]] + [fixed(lab_col), fixed(lab_row)]
    outs = [struct((slabs, length, 3 * lanes), BF16), struct((slabs, 2, lanes), F32)]
    return launch(
        attend_back_kernel, slabs, [windows], operands, specs, outs, [slab(a) for a in outs],
        [pltpu.VMEM((length, lanes), F32)] * 2, 60 * slabs * length * 640 * lanes, "attend_back",
    )


def row_tile(length):
    return min(256, length)


def tall(a, tile):
    if len(a.shape) == 2:
        return pl.BlockSpec((tile, a.shape[1]), lambda i, *_: (i, 0))
    return pl.BlockSpec((a.shape[0], tile, a.shape[2]), lambda i, *_: (0, i, 0))


def tall_from(a, tile, per):
    if len(a.shape) == 2:
        return pl.BlockSpec((tile, a.shape[1]), lambda i, at: (at[0] * per + i, 0))
    return pl.BlockSpec((a.shape[0], tile, a.shape[2]), lambda i, at: (0, at[0] * per + i, 0))


class Slab:
    def __init__(self, array, width, block, order):
        self.array, self.width = array, width
        shape = (array.shape[0], 1, array.shape[2], width)
        self.spec = pl.BlockSpec(shape, lambda i, at: (0, at[1 + order], 0, block))


def arrays(slabs):
    return [w.array for w in slabs]


def specs_of(slabs):
    return [w.spec for w in slabs]


def rows_of(slab):
    return slab.array.shape[0] * slab.array.shape[2]


def flat(ref):
    return ref[:, 0].reshape(ref.shape[0] * ref.shape[2], ref.shape[3])


def project_kernel(x_ref, b_ref, *refs):
    count = b_ref.shape[0]
    weights, (q_ref, k_ref, v_ref) = refs[:count], refs[count:]
    lanes = q_ref.shape[2]
    scale = 1.0 / math.sqrt(DH)
    x = x_ref[...]
    for i in range(count):
        projected = nn(x, weights[i][...]) + b_ref[i]
        q_ref[i] = (projected[:, :lanes].astype(BF16).astype(F32) * scale).astype(BF16)
        k_ref[i] = projected[:, lanes : 2 * lanes].astype(BF16)
        v_ref[i] = projected[:, 2 * lanes :].astype(BF16)


def project(x, weights, bias):
    length, model = x.shape
    lanes = weights[0].shape[1] // 3
    tile = row_tile(length)
    outs = [struct((len(weights), length, lanes), BF16)] * 3
    return launch(
        project_kernel, length // tile, [], [x, bias] + weights,
        [tall(x, tile), fixed(bias)] + [fixed(w) for w in weights], outs,
        [tall(a, tile) for a in outs], [], 6 * length * model * lanes * len(weights), "project",
    )


def context_out_kernel(at, ctx_ref, *refs):
    weights, out_ref = refs[:-1], refs[-1]
    left = jnp.concatenate([ctx_ref[i] for i in range(ctx_ref.shape[0])], axis=1)
    right = jnp.concatenate([flat(w) for w in weights], axis=1)
    out_ref[...] = nt(left, right).astype(out_ref.dtype)


def context_out(at, ctx, weights, part, dtype):
    tile = row_tile(part)
    model = rows_of(weights[0])
    out = struct((part, model), dtype)
    return launch(
        context_out_kernel, part // tile, [at], [ctx] + arrays(weights),
        [tall_from(ctx, tile, part // tile)] + specs_of(weights), [out], [tall(out, tile)], [],
        2 * part * model * ctx.shape[0] * ctx.shape[2], "context_out",
    )[0]


def context_back_kernel(at, ga_ref, *refs):
    weights, out_ref = refs[:-1], refs[-1]
    lanes = out_ref.shape[2]
    right = jnp.concatenate([flat(w) for w in weights], axis=1)
    grad = nn(ga_ref[...], right).astype(BF16)
    for i in range(out_ref.shape[0]):
        out_ref[i] = grad[:, i * lanes : (i + 1) * lanes]


def context_back(at, ga, weights):
    lanes = weights[0].width // 2
    tile = row_tile(ga.shape[0])
    count = 2 * len(weights)
    out = struct((count, ga.shape[0], lanes), BF16)
    return launch(
        context_back_kernel, ga.shape[0] // tile, [at], [ga] + arrays(weights),
        [tall(ga, tile)] + specs_of(weights), [out], [tall(out, tile)], [],
        2 * math.prod(ga.shape) * lanes * count, "context_back",
    )[0]


def ffn_in_kernel(at, y_ref, b_ref, *refs):
    count = b_ref.shape[0]
    weights, (act_ref, slope_ref) = refs[:count], refs[-2:]
    y = y_ref[...]
    for i in range(count):
        inner = nn(y, flat(weights[i])) + b_ref[i]
        share = 0.5 + 0.5 * lax.erf(inner * math.sqrt(0.5))
        density = jnp.exp(-0.5 * inner * inner) * (1.0 / math.sqrt(2.0 * math.pi))
        act_ref[i] = (inner * share).astype(BF16)
        slope_ref[i] = (share + inner * density).astype(BF16)


def place(a, tile, first):
    return pl.BlockSpec((a.shape[0], tile, a.shape[2]), lambda i, *_: (0, first + i, 0))


def ffn_in(at, y, bias, weights, ways, place_at, earlier):
    part, model = y.shape
    tile = row_tile(part)
    first = place_at * (part // tile)
    wide = bias.shape[2]
    count = len(weights)
    out = struct((count, part * ways, wide), BF16)
    anywhere = [pl.BlockSpec(memory_space=pl.ANY)] * len(earlier)
    return launch(
        ffn_in_kernel, part // tile, [at], [y, bias] + arrays(weights) + earlier,
        [tall(y, tile), fixed(bias)] + specs_of(weights) + anywhere,
        [out, out], [place(out, tile, first)] * 2, [],
        6 * part * model * wide * count, "ffn_in",
        {3 + count + i: i for i in range(len(earlier))},
    )


def ffn_out_kernel(at, act_ref, *refs):
    weights, out_ref = refs[:-1], refs[-1]
    total = nt(act_ref[0], flat(weights[0]))
    for i in range(1, len(weights)):
        total += nt(act_ref[i], flat(weights[i]))
    out_ref[...] = total.astype(out_ref.dtype)


def ffn_out(at, act, weights, part, place_at, dtype):
    tile = row_tile(part)
    model = rows_of(weights[0])
    out = struct((part, model), dtype)
    return launch(
        ffn_out_kernel, part // tile, [at], [act] + arrays(weights),
        [place(act, tile, place_at * (part // tile))] + specs_of(weights),
        [out], [tall(out, tile)], [], 2 * part * model * act.shape[0] * act.shape[2], "ffn_out",
    )[0]


def ffn_back_kernel(at, gb_ref, slope_ref, *refs):
    count = slope_ref.shape[0]
    outs, ins = refs[:count], refs[count : 2 * count]
    gi_ref, sum_ref, out_ref = refs[-3:]
    gb = gb_ref[...]
    total = None
    sums = []
    for i in range(count):
        grad = nn(gb, flat(outs[i])) * slope_ref[i].astype(F32)
        low = grad.astype(BF16)
        gi_ref[i] = low
        sums.append(jnp.sum(grad, axis=0, keepdims=True))
        term = nt(low, flat(ins[i]))
        total = term if total is None else total + term
    out_ref[...] = total.astype(out_ref.dtype)

    @pl.when(pl.program_id(0) == 0)
    def _():
        sum_ref[...] = jnp.zeros_like(sum_ref)

    for i in range(count):
        sum_ref[i] += sums[i]


def ffn_back(at, gb, slope, outs_w, ins_w, place_at, earlier, dtype):
    part, model = gb.shape
    tile = row_tile(part)
    first = place_at * (part // tile)
    count, _, wide = slope.shape
    anywhere = [pl.BlockSpec(memory_space=pl.ANY)] * len(earlier)
    outs = [struct(slope.shape, BF16), struct((count, 1, wide), F32), struct((part, model), dtype)]
    return launch(
        ffn_back_kernel, part // tile, [at], [gb, slope] + arrays(outs_w + ins_w) + earlier,
        [tall(gb, tile), place(slope, tile, first)] + specs_of(outs_w + ins_w) + anywhere,
        outs, [place(outs[0], tile, first), fixed(outs[1]), tall(outs[2], tile)], [],
        4 * part * model * wide * count, "ffn_back",
        {3 + 2 * count + i: i for i in range(len(earlier))},
    )


def inputs_back_kernel(at, gp_ref, *refs):
    weights, out_ref = refs[:-1], refs[-1]
    total = nt(gp_ref[0], weights[0][...])
    for i in range(1, len(weights)):
        total += nt(gp_ref[i], weights[i][...])
    out_ref[...] = total.astype(out_ref.dtype)


def inputs_back(at, gp, weights, part, dtype):
    tile = row_tile(part)
    model = weights[0].shape[0]
    out = struct((part, model), dtype)
    return launch(
        inputs_back_kernel, part // tile, [at], [gp] + weights,
        [tall_from(gp, tile, part // tile)] + [fixed(w) for w in weights], [out], [tall(out, tile)], [],
        2 * part * model * gp.shape[0] * gp.shape[2], "inputs_back",
    )[0]


def transpose_into(left_t, lefts):
    first = 0
    for left in lefts:
        left_t[:, first : first + left.shape[0]] = left[...].T
        first += left.shape[0]


def weight_grad(lefts, right):
    count, length, wide = right.shape
    model = lefts[0].shape[1]
    out = struct((model, wide), BF16)
    parts = len(lefts)

    def kernel(*refs):
        right_ref, outs = refs[parts], refs[parts + 1 : parts + 1 + count]
        left_t, slots, sems = refs[-3:]
        copies = [pltpu.make_async_copy(slots.at[k % 2], outs[k], sems.at[k % 2]) for k in range(count)]

        def step(k):
            if k == 0:
                transpose_into(left_t, refs[:parts])
            if k > 1:
                copies[k - 2].wait()
            slots[k % 2] = nn(left_t[...], right_ref[0]).astype(BF16)
            copies[k].start()
            if k == count - 1:
                for last in copies[max(k - 1, 0) :]:
                    last.wait()

        for k in range(count):
            pl.when(pl.program_id(0) == k)(functools.partial(step, k))

    return launch(
        kernel, count, [], list(lefts) + [right], [fixed(a) for a in lefts] + [slab(right)], [out] * count,
        [pl.BlockSpec(memory_space=pl.ANY)] * count,
        [pltpu.VMEM((model, length), BF16), pltpu.VMEM((2, model, wide), BF16), pltpu.SemaphoreType.DMA((2,))],
        2 * length * model * wide * count, "weight_grad",
    )


def weight_grad_shards(at, lefts, right, rows, seqs):
    count, length, wide = right.shape
    model = lefts[0].shape[1]
    halves = count // seqs
    out = struct((rows, seqs, model // rows, wide * halves), BF16)
    parts = len(lefts)

    def kernel(at_ref, *refs):
        right_ref, out_ref, left_t = refs[parts:]

        @pl.when(pl.program_id(0) == 0)
        def _():
            transpose_into(left_t, refs[:parts])

        made = nn(left_t[...], right_ref[0]).astype(BF16)
        out_ref[:, 0] = made.reshape(out_ref.shape[0], out_ref.shape[2], wide)

    spec = pl.BlockSpec((rows, 1, model // rows, wide), lambda i, at: (0, at[1 + i // halves], 0, i % halves))
    return launch(
        kernel, count, [at], list(lefts) + [right], [fixed(a) for a in lefts] + [slab(right)], [out], [spec],
        [pltpu.VMEM((model, length), BF16)], 2 * length * model * wide * count, "weight_grad_shards",
    )[0]


def norm_rows(hidden):
    mean = jnp.mean(hidden, axis=1, keepdims=True)
    square = jnp.mean(hidden * hidden, axis=1, keepdims=True)
    inv_std = lax.rsqrt(square - mean * mean + NORM_EPS)
    return (hidden - mean) * inv_std, inv_std


def norm_rows_back(incoming, centred, inv_std, gain):
    scaled = incoming * gain
    first = jnp.mean(scaled, axis=1, keepdims=True)
    second = jnp.mean(scaled * centred, axis=1, keepdims=True)
    return inv_std * (scaled - first - centred * second)


def add_sums(sum_ref, terms):
    @pl.when(pl.program_id(0) == 0)
    def _():
        sum_ref[...] = jnp.zeros_like(sum_ref)

    for i, term in enumerate(terms):
        sum_ref[i : i + 1, :] += jnp.sum(term, axis=0, keepdims=True)


def norm_a_kernel(at, mine_ref, got_ref, x_ref, vec_ref, centred_ref, inv_ref, y_ref):
    hidden = mine_ref[...] + got_ref[...].astype(F32) + x_ref[...].astype(F32) + vec_ref[0]
    centred, inv_std = norm_rows(hidden)
    centred_ref[...] = centred
    inv_ref[...] = inv_std
    y_ref[...] = (centred * vec_ref[1] + vec_ref[2]).astype(BF16)


def norm_a(at, mine, got, x, vec):
    part, model = mine.shape
    tile = row_tile(part)
    outs = [struct((part, model), F32), struct((part, 1), F32), struct((part, model), BF16)]
    return launch(
        norm_a_kernel, part // tile, [at], [mine, got, x, vec],
        [tall(mine, tile), tall(got, tile), tall_from(x, tile, part // tile), fixed(vec)],
        outs, [tall(a, tile) for a in outs], [], 20 * part * model, "norm_a",
    )


def norm_b_kernel(mine_ref, got_ref, centred_a_ref, cot_ref, vec_ref, out_ref, grad_ref, low_ref, sum_ref):
    normed = centred_a_ref[...] * vec_ref[1] + vec_ref[2]
    hidden = mine_ref[...] + got_ref[...].astype(F32) + vec_ref[3] + normed
    centred, inv_std = norm_rows(hidden)
    out_ref[...] = (centred * vec_ref[4] + vec_ref[5]).astype(BF16)
    incoming = cot_ref[...].astype(F32)
    grad = norm_rows_back(incoming, centred, inv_std, vec_ref[4])
    grad_ref[...] = grad
    low_ref[...] = grad.astype(BF16)
    add_sums(sum_ref, (grad, incoming * centred, incoming))


def norm_b(mine, got, centred_a, cot, vec):
    part, model = mine.shape
    tile = row_tile(part)
    outs = [struct((part, model), BF16), struct((part, model), F32), struct((part, model), BF16), struct((3, model), F32)]
    return launch(
        norm_b_kernel, part // tile, [], [mine, got, centred_a, cot, vec],
        [tall(a, tile) for a in (mine, got, centred_a, cot)] + [fixed(vec)],
        outs, [tall(a, tile) for a in outs[:3]] + [fixed(outs[3])], [], 40 * part * model, "norm_b",
    )


def norm_a_back_kernel(mine_ref, got_ref, gb_ref, centred_ref, inv_ref, vec_ref, grad_ref, low_ref, sum_ref):
    incoming = mine_ref[...] + got_ref[...].astype(F32) + gb_ref[...]
    centred = centred_ref[...]
    grad = norm_rows_back(incoming, centred, inv_ref[...], vec_ref[1])
    grad_ref[...] = grad
    low_ref[...] = grad.astype(BF16)
    add_sums(sum_ref, (grad, incoming * centred, incoming))


def norm_a_back(mine, got, gb, centred, inv, vec):
    part, model = mine.shape
    tile = row_tile(part)
    outs = [struct((part, model), F32), struct((part, model), BF16), struct((3, model), F32)]
    return launch(
        norm_a_back_kernel, part // tile, [], [mine, got, gb, centred, inv, vec],
        [tall(a, tile) for a in (mine, got, gb, centred, inv)] + [fixed(vec)],
        outs, [tall(a, tile) for a in outs[:2]] + [fixed(outs[2])], [], 30 * part * model, "norm_a_back",
    )


def body(
    rows,
    cols,
    tokens,
    segments,
    wqkv,
    bias_qv,
    wo,
    bias_o,
    gain_a,
    shift_a,
    w_in,
    bias_in,
    w_out,
    bias_out,
    gain_b,
    shift_b,
    cotangent,
):
    seqs, length = segments.shape
    ways = cols // seqs
    width = tokens.shape[1]
    model = width * cols
    heads = wqkv.shape[1] // (3 * DH)
    lanes = heads * DH // 2
    hid = w_in.shape[1]
    part = length // ways
    own_rows = wqkv.shape[0]
    row, col = lax.axis_index("row"), lax.axis_index(COL)
    seq, way = col // ways, col % ways
    by_seq = [Stage(COL, cols, mask * ways, col) for mask in bits_of(seqs)]
    by_way = [Stage(COL, cols, mask, col) for mask in bits_of(ways)]
    by_row = [Stage("row", rows, mask, row) for mask in bits_of(rows)]
    ns, nw, nr = len(by_seq), len(by_way), len(by_row)
    far, near = by_row[:-1], by_row[-1]
    parts = range(ways)
    orders = [0]
    for mask in bits_of(seqs):
        orders = orders + [o ^ mask for o in orders]
    at = [jnp.stack([way ^ p] + [seq ^ o for o in orders]).astype(jnp.int32) for p in parts]

    def gather_far(one, two):
        halves = [h.reshape((1,) * nr + h.shape) for h in (one, two)]
        for i, stage in enumerate(far):
            both = jnp.stack(halves)
            got = stage.trade(both)
            halves = [stage.join(both[h], got[h], i) for h in range(2)]
        return halves

    def gather_near(block):
        return near.gather(block, nr - 1).reshape(model, -1)

    def gather_last(one, two):
        ones, twos = [gather_near(one)], [two]
        for stage in by_seq:
            twos = twos + [stage.trade(b) for b in twos]
        two = after(two, ones[0])
        twos = [gather_near(b) for b in [two] + twos[1:]]
        for stage in by_seq:
            ones = ones + [stage.trade(b) for b in ones]
        return [b for j in range(seqs) for b in (ones[j], twos[j])]

    def halves_of(weight):
        half = weight.shape[1] // 2
        return weight[:, :half], weight[:, half:]

    by_kind = wqkv.reshape(own_rows, 2, heads // 2, 3, DH).transpose(1, 0, 3, 2, 4)
    by_kind = by_kind.reshape(2, own_rows, -1)
    far_qkv = gather_far(by_kind[0], by_kind[1])

    labels = lax.dynamic_slice_in_dim(segments, seq, 1, 0)[0]
    windows = key_windows(labels)
    lab_col, lab_row = labels[:, None], labels[None, :]

    def exchange(array, split, whole):
        blocks = [array]
        for stage in split + whole:
            both = blocks[0] if len(blocks) == 1 else jnp.concatenate(blocks, axis=1)
            if stage in split:
                both = both.reshape(2, both.shape[0] // 2, both.shape[1])
                mine, sent = pick(both, stage.bit, 0)[0], pick(both, 1 - stage.bit, 0)[0]
            else:
                mine = sent = both
            got = stage.trade(sent)
            low = stage.bit == 0
            blocks = [
                half
                for i in range(len(blocks))
                for a, b in [(mine[:, i * width : (i + 1) * width], got[:, i * width : (i + 1) * width])]
                for half in (jnp.where(low, a, b), jnp.where(low, b, a))
            ]
        return jnp.concatenate(blocks, axis=1)

    def to_features(array):
        blocks = [array]
        for stage in by_seq + by_way:
            half = blocks[0].shape[1] // 2
            both = blocks[0] if len(blocks) == 1 else jnp.concatenate(blocks, axis=0)
            mine = lax.dynamic_slice_in_dim(both, stage.bit * half, half, 1)
            got = stage.trade(lax.dynamic_slice_in_dim(both, (1 - stage.bit) * half, half, 1))
            low = stage.bit == 0
            count = array.shape[0]
            blocks = [
                half_rows
                for i in range(len(blocks))
                for a, b in [(mine[i * count : (i + 1) * count], got[i * count : (i + 1) * count])]
                for half_rows in (jnp.where(low, a, b), jnp.where(low, b, a))
            ]
        return jnp.concatenate(blocks, axis=0)

    whole_x = exchange(after(tokens, far_qkv[0]), by_seq, by_way)
    vectors = jnp.concatenate(
        [v.reshape(-1, width) for v in (bias_o, gain_a, shift_a, bias_out, gain_b, shift_b, bias_qv, bias_in)]
    )
    vectors = after(vectors, far_qkv[0])
    pairs = [vectors]
    for stage in by_seq:
        pairs = pairs + [stage.trade(v) for v in pairs]
    blocks = [vectors[:6]]
    for i, stage in enumerate(by_seq):
        got = jnp.concatenate([p[:6] for p in pairs[1 << i : 2 << i]], axis=1)
        low = stage.bit == 0
        both = jnp.concatenate(blocks, axis=1)
        blocks = [
            half
            for k in range(len(blocks))
            for a, b in [(both[:, k * width : (k + 1) * width], got[:, k * width : (k + 1) * width])]
            for half in (jnp.where(low, a, b), jnp.where(low, b, a))
        ]
    for stage in by_way:
        both = jnp.concatenate(blocks, axis=1)
        got = stage.trade(both)
        low = stage.bit == 0
        blocks = [
            half
            for k in range(len(blocks))
            for a, b in [(both[:, k * width : (k + 1) * width], got[:, k * width : (k + 1) * width])]
            for half in (jnp.where(low, a, b), jnp.where(low, b, a))
        ]
    vec = jnp.concatenate(blocks, axis=1).astype(F32)[:, None, :]
    nq = bias_qv.shape[0] // width
    q_biases, in_biases = [], []
    for j in range(seqs):
        both = pairs[j][6 : 6 + nq].astype(F32).reshape(2, heads // 2, 2, DH)
        both = both.transpose(0, 2, 1, 3).reshape(2, 2, lanes)
        q_biases.append(jnp.concatenate((both[:, :1], jnp.zeros_like(both[:, :1]), both[:, 1:]), axis=1))
        in_biases.append(pairs[j][6 + nq :].astype(F32).reshape(2, 1, hid // 2))
    q_bias = jnp.concatenate(q_biases, axis=0).reshape(2 * seqs, 1, 3 * lanes)
    in_bias = jnp.concatenate(in_biases, axis=0)

    qkv_all = gather_last(*far_qkv)
    everyone = ("row", "seq")

    def shards(weight):
        whole = lax.all_gather(weight, everyone, axis=0, tiled=True)
        return whole.reshape(rows, seqs, own_rows, weight.shape[1])

    whole_in = shards(jnp.concatenate((w_in, wo.T), axis=1))
    whole_out = shards(w_out.T)
    pairs_of = [(j, h) for j in range(seqs) for h in range(2)]
    in_all = [Slab(whole_in, hid // 2, h, j) for j, h in pairs_of]
    wo_all = [Slab(whole_in, 2 * lanes, hid // (2 * lanes), j) for j in range(seqs)]
    out_all = [Slab(whole_out, hid // 2, h, j) for j, h in pairs_of]
    cot = exchange(after(cotangent, qkv_all[2]), by_seq + by_way, [])

    def gather_parts(own):
        blocks = {0: own}
        for mask, stage in zip(bits_of(ways), by_way):
            for p in list(blocks):
                blocks[p ^ mask] = stage.trade(blocks[p])
        return [blocks[p] for p in parts]

    def scatter_parts(make):
        terms = {p: make(p, F32 if p == 0 else BF16) for p in reversed(parts)}
        for mask, stage in list(zip(bits_of(ways), by_way))[:-1]:
            for p in [q for q in terms if q & mask]:
                got = stage.trade(terms.pop(p))
                terms[p ^ mask] = add(terms[p ^ mask], got)
        return terms[0], by_way[-1].trade(terms[1])

    def whole_rows(blocks):
        blocks = list(blocks)
        for mask, stage in zip(reversed(bits_of(ways)), reversed(by_way)):
            low = stage.bit == 0
            for p in parts:
                if not p & mask:
                    a, b = blocks[p], blocks[p | mask]
                    blocks[p], blocks[p | mask] = jnp.where(low, a, b), jnp.where(low, b, a)
        return jnp.concatenate(blocks, axis=0)

    def scatter_first(blocks):
        ones, twos = blocks[0::2], blocks[1::2]
        fold = lambda b: near.reduce(b.reshape((2,) * nr + (own_rows, -1)), nr - 1)
        for stage in reversed(by_seq):
            count = len(ones) // 2
            ones = [add(ones[j], stage.trade(ones[count + j])) for j in range(count)]
        twos = [fold(b) for b in reversed(twos)][::-1]
        for stage in reversed(by_seq):
            count = len(twos) // 2
            twos = [add(twos[j], stage.trade(twos[count + j])) for j in range(count)]
        return fold(ones[0]), twos[0]

    def scatter_far(one, two):
        for i, stage in reversed(list(enumerate(far))):
            halves = (one, two)
            sent = jnp.stack([pick(b, 1 - stage.bit, i) for b in halves])
            got = stage.trade(sent)
            one, two = [add(pick(b, stage.bit, i), got[h]) for h, b in enumerate(halves)]
        return one.reshape(own_rows, -1).astype(F32), two.reshape(own_rows, -1).astype(F32)

    q, k, v = project(whole_x, qkv_all, q_bias)
    context, lse = attend(windows, q, k, v, lab_col, lab_row)
    mine, got = scatter_parts(lambda p, dtype: context_out(at[p], context, wo_all, part, dtype))
    centred_a, inv_a, y = norm_a(at[0], mine, got, whole_x, vec)
    y_parts = gather_parts(y)
    earlier = []
    for p in parts:
        earlier = ffn_in(at[0], y_parts[p], in_bias, in_all, ways, p, list(earlier))
    active, slope = earlier
    mine, got = scatter_parts(lambda p, dtype: ffn_out(at[0], active, out_all, part, p, dtype))
    output, grad_b, gb, sums_b = norm_b(mine, got, centred_a, cot, vec)

    gb_parts = gather_parts(gb)
    output = to_features(after(output, gb_parts[-1]))
    grad_w_out = weight_grad_shards(at[0], gb_parts, active, rows, seqs)
    out_sum = lax.psum_scatter(
        grad_w_out.reshape(rows * seqs * own_rows, hid), everyone, scatter_dimension=0, tiled=True
    )
    terms, sum_in, earlier = {}, 0.0, []
    for p in parts:
        grad_inner, sums, terms[p] = ffn_back(
            at[0], after(gb_parts[p], grad_w_out), slope, out_all, in_all, p, earlier, F32 if p == 0 else BF16
        )
        earlier = [grad_inner]
        sum_in = sum_in + sums
    mine, got = scatter_parts(lambda p, dtype: terms[p])
    grad_w_in = weight_grad(y_parts, grad_inner)
    grad_a, ga, sums_a = norm_a_back(mine, got, grad_b, centred_a, inv_a, vec)
    whole_ga = whole_rows(gather_parts(ga))
    grad_context = context_back(at[0], whole_ga, wo_all)
    first_in = scatter_first(grad_w_in)
    grad_projected, sum_projected = attend_back(windows, q, k, v, grad_context, lse, lab_col, lab_row)
    in_halves = scatter_far(*first_in)
    grad_wo = weight_grad([whole_ga], context)
    grad_wqkv = weight_grad([whole_x], grad_projected)
    last = scatter_first([jnp.concatenate(two, axis=1) for two in zip(grad_wqkv, grad_wo)])
    mine, got = scatter_parts(lambda p, dtype: inputs_back(at[p], grad_projected, qkv_all, part, dtype))
    grad_tokens = to_features((mine + got.astype(F32) + grad_a).astype(BF16)).astype(F32)
    qkv_halves = scatter_far(*last)

    per_hidden = []
    for j in range(seqs):
        two = sum_projected[2 * j : 2 * j + 2].reshape(2, 2, heads // 2, DH).transpose(0, 2, 1, 3)
        per_hidden.append(jnp.concatenate((two.reshape(-1), sum_in[2 * j : 2 * j + 2].reshape(-1))))
    block = jnp.concatenate((sums_a, sums_b), axis=0)
    for stage in by_seq + by_way:
        half = block.shape[1] // 2
        got = stage.trade(lax.dynamic_slice_in_dim(block, (1 - stage.bit) * half, half, 1))
        block = lax.dynamic_slice_in_dim(block, stage.bit * half, half, 1) + got
    for stage in reversed(by_seq):
        count = len(per_hidden) // 2
        per_hidden = [per_hidden[j] + stage.trade(per_hidden[count + j]) for j in range(count)]
    sums = jnp.concatenate((per_hidden[0], block.reshape(-1)))
    for stage in by_row:
        sums = sums + stage.trade(sums)
    nqv = bias_qv.shape[0]
    sum_qv, sum_in = sums[:nqv], sums[nqv : nqv + hid]
    rest = sums[nqv + hid :].reshape(6, width)
    split = 3 * lanes
    grad_qkv = jnp.stack([h[:, :split] for h in qkv_halves])
    grad_qkv = grad_qkv.reshape(2, own_rows, 3, heads // 2, DH).transpose(1, 0, 3, 2, 4)
    return (
        output,
        grad_tokens,
        grad_qkv.reshape(own_rows, -1),
        sum_qv,
        jnp.concatenate([h[:, split:] for h in qkv_halves], axis=1).T,
        rest[0],
        rest[1],
        rest[2],
        jnp.concatenate(in_halves, axis=1),
        sum_in,
        out_sum.astype(F32).T,
        rest[3],
        rest[4],
        rest[5],
    )


def solution(mesh):
    rows, cols = mesh.shape["row"], mesh.shape["col"]
    tile, across, down, flat_col = P("row", COL), P("row", None), P(COL, "row"), P(COL)
    in_specs = (
        tile, across, tile, flat_col, down, flat_col, flat_col, flat_col,
        tile, flat_col, down, flat_col, flat_col, flat_col, tile,
    )
    out_specs = (
        tile, tile, tile, flat_col, down, flat_col, flat_col, flat_col,
        tile, flat_col, down, flat_col, flat_col, flat_col,
    )

    def run(*args):
        seqs = args[1].shape[0] // rows
        fine = jax.sharding.Mesh(mesh.devices.reshape(rows, seqs, cols // seqs), ("row",) + COL)

        def layer(*local):
            return body(rows, cols, *local)

        return jax.shard_map(layer, mesh=fine, in_specs=in_specs, out_specs=out_specs, check_vma=False)(*args)

    return run
```

```python
import functools
import math

import jax
import jax.numpy as jnp
from jax import lax
from jax.experimental import pallas as pl
from jax.experimental.pallas import tpu as pltpu
from jax.sharding import PartitionSpec as P

DH = 64
NORM_EPS = 1e-06
MASKED = -1000000000.0
LONGEST = 256
COL = ("seq", "way")
SHARE = 1
F32 = jnp.float32
BF16 = jnp.bfloat16


def nn(left, right):
    return lax.dot_general(left, right, (((1,), (0,)), ((), ())), preferred_element_type=F32)


def nt(left, right):
    return lax.dot_general(left, right, (((1,), (1,)), ((), ())), preferred_element_type=F32)


def tn(left, right):
    return lax.dot_general(left, right, (((0,), (0,)), ((), ())), preferred_element_type=F32)


def after(block, *others):
    return lax.optimization_barrier((block,) + others)[0]


def pick(block, bit, dim):
    return lax.dynamic_slice_in_dim(block, bit, 1, dim)


def bits_of(count):
    return [1 << b for b in reversed(range(count.bit_length() - 1))]


class Stage:
    def __init__(self, axis, count, mask, index):
        self.axis, self.pairs = axis, [(i, i ^ mask) for i in range(count)]
        self.bit = (index // mask) % 2

    def trade(self, block):
        return lax.ppermute(block, self.axis, self.pairs)

    def join(self, mine, other, dim):
        low = self.bit == 0
        return jnp.concatenate(
            (jnp.where(low, mine, other), jnp.where(low, other, mine)), axis=dim
        )

    def gather(self, block, dim):
        return self.join(block, self.trade(block), dim)

    def swap(self, block, split, dim):
        keep = pick(block, self.bit, split)
        return self.join(keep, self.trade(pick(block, 1 - self.bit, split)), dim)

    def reduce(self, block, dim):
        got = self.trade(pick(block, 1 - self.bit, dim))
        return add(pick(block, self.bit, dim), got)


def add_three(mine, one, two):
    return (mine.astype(F32) + one.astype(F32) + two.astype(F32)).astype(mine.dtype)


def add(mine, other):
    return (mine.astype(F32) + other.astype(F32)).astype(mine.dtype)


def tiles_of(length):
    return min(256, length), min(128, length)


def key_windows(labels):
    rows, step = tiles_of(labels.shape[0])
    first, last = labels[::rows], labels[rows - 1 :: rows]
    start = jnp.sum(labels[None, :] < first[:, None], axis=1)
    stop = jnp.sum(labels[None, :] <= last[:, None], axis=1)
    block = start // step
    return jnp.stack((block, (stop - 1) // step + 1 - block)).astype(jnp.int32)


def for_each_block(windows, length, run):
    rows, step = tiles_of(length)
    reach = -(-(LONGEST - 1) // step)
    most = min(length // step, rows // step + 2 * reach)

    def one(i, carry):
        q0 = pl.multiple_of(i * rows, rows)
        k0 = pl.multiple_of(windows[0, i] * step, step)
        for n in range(1, most + 1):
            pl.when(windows[1, i] == n)(functools.partial(run, q0, k0, rows, n * step))
        return carry

    lax.fori_loop(0, length // rows, one, 0)


def attend_kernel(windows, q_ref, k_ref, v_ref, lab_col, lab_row, ctx_ref, lse_ref):
    length, lanes = q_ref.shape[1:]

    def run(q0, k0, rows, span):
        q = q_ref[0, pl.ds(q0, rows), :]
        k = k_ref[0, pl.ds(k0, span), :]
        v_t = v_ref[0, pl.ds(k0, span), :].T
        same = lab_col[pl.ds(k0, span), :] == lab_row[:, pl.ds(q0, rows)]
        head = lax.broadcasted_iota(jnp.int32, (span, lanes), 1) // DH
        outs = []
        for h in range(lanes // DH):
            scores = nt(jnp.where(head == h, k, jnp.zeros_like(k)), q)
            scores = jnp.where(same, scores, MASKED)
            top = jnp.max(scores, axis=0, keepdims=True)
            shifted = jnp.exp(scores - top)
            total = jnp.sum(shifted, axis=0, keepdims=True)
            outs.append(nn(v_t[h * DH : (h + 1) * DH, :], shifted.astype(BF16)) / total)
            lse_ref[0, h : h + 1, pl.ds(q0, rows)] = top + jnp.log(total)
        ctx_ref[0, pl.ds(q0, rows), :] = jnp.concatenate(outs, axis=0).T.astype(BF16)

    for_each_block(windows, length, run)


def attend_back_kernel(
    windows, q_ref, k_ref, v_ref, do_ref, lse_ref, lab_col, lab_row, gp_ref, sum_ref, dk_acc, dv_acc
):
    length, lanes = q_ref.shape[1:]
    scale = 1.0 / math.sqrt(DH)
    dk_acc[...] = jnp.zeros_like(dk_acc)
    dv_acc[...] = jnp.zeros_like(dv_acc)
    sum_ref[...] = jnp.zeros_like(sum_ref)

    def run(q0, k0, rows, span):
        q = q_ref[0, pl.ds(q0, rows), :]
        do = do_ref[0, pl.ds(q0, rows), :]
        k = k_ref[0, pl.ds(k0, span), :]
        v = v_ref[0, pl.ds(k0, span), :]
        k_t = k.T
        same = lab_col[pl.ds(k0, span), :] == lab_row[:, pl.ds(q0, rows)]
        head = lax.broadcasted_iota(jnp.int32, (span, lanes), 1) // DH
        head_q = lax.broadcasted_iota(jnp.int32, (rows, lanes), 1) // DH
        dqs = []
        dk = dv = None
        for h in range(lanes // DH):
            only = lambda a, own: jnp.where(own == h, a, jnp.zeros_like(a))
            scores = jnp.where(same, nt(only(k, head), q), MASKED)
            prob = jnp.exp(scores - lse_ref[0, h : h + 1, pl.ds(q0, rows)])
            weighted = prob * nt(only(v, head), do)
            row_dot = jnp.sum(weighted, axis=0, keepdims=True)
            dscore = (weighted - prob * row_dot).astype(BF16)
            dv_h = nn(prob.astype(BF16), only(do, head_q))
            dk_h = nn(dscore, only(q, head_q))
            dv = dv_h if dv is None else dv + dv_h
            dk = dk_h if dk is None else dk + dk_h
            dqs.append(nn(k_t[h * DH : (h + 1) * DH, :], dscore))
        dq = jnp.concatenate(dqs, axis=0).T * scale
        gp_ref[0, pl.ds(q0, rows), :lanes] = dq.astype(BF16)
        sum_ref[0, 0:1, :] += jnp.sum(dq, axis=0, keepdims=True)
        dk_acc[pl.ds(k0, span), :] += dk
        dv_acc[pl.ds(k0, span), :] += dv

    for_each_block(windows, length, run)
    gp_ref[0, :, lanes : 2 * lanes] = dk_acc[...].astype(BF16)
    gp_ref[0, :, 2 * lanes :] = dv_acc[...].astype(BF16)
    sum_ref[0, 1:2, :] = jnp.sum(dv_acc[...], axis=0, keepdims=True)


def struct(shape, dtype):
    return jax.ShapeDtypeStruct(shape, dtype)


def fixed(a):
    return pl.BlockSpec(a.shape, lambda i, *_: (0,) * len(a.shape))


def slab(a):
    return pl.BlockSpec((1,) + a.shape[1:], lambda i, *_: (i,) + (0,) * (len(a.shape) - 1))


def launch(kernel, grid, scalars, operands, specs, outs, out_specs, scratch, flops, name, aliases=None):
    moved = sum(math.prod(a.shape) * a.dtype.itemsize for a in list(operands) + list(outs))
    return pl.pallas_call(
        kernel,
        grid_spec=pltpu.PrefetchScalarGridSpec(
            num_scalar_prefetch=len(scalars),
            grid=(grid,),
            in_specs=specs,
            out_specs=out_specs,
            scratch_shapes=scratch,
        ),
        out_shape=outs,
        input_output_aliases=aliases or {},
        cost_estimate=pl.CostEstimate(flops=flops // SHARE, transcendentals=0, bytes_accessed=moved // SHARE),
        name=name,
    )(*scalars, *operands)


def slab_from(a, first):
    return pl.BlockSpec((1,) + a.shape[1:], lambda i, *_: (first + i,) + (0,) * (len(a.shape) - 1))


def attend(windows, q, k, v, lab_col, lab_row, first, slabs):
    _, length, lanes = q.shape
    operands = [q, k, v, lab_col, lab_row]
    specs = [slab_from(q, first)] * 3 + [fixed(lab_col), fixed(lab_row)]
    outs = [struct((slabs,) + q.shape[1:], BF16), struct((slabs, lanes // DH, length), F32)]
    return launch(
        attend_kernel, slabs, [windows], operands, specs, outs, [slab(a) for a in outs], [],
        40 * slabs * length * 640 * lanes, "attend",
    )


def attend_back(windows, q, k, v, do, lse, lab_col, lab_row, first, slabs):
    _, length, lanes = q.shape
    operands = [q, k, v, do, lse, lab_col, lab_row]
    specs = [slab_from(a, first) for a in operands[:4]] + [slab(lse), fixed(lab_col), fixed(lab_row)]
    outs = [struct((slabs, length, 3 * lanes), BF16), struct((slabs, 2, lanes), F32)]
    return launch(
        attend_back_kernel, slabs, [windows], operands, specs, outs, [slab(a) for a in outs],
        [pltpu.VMEM((length, lanes), F32)] * 2, 60 * slabs * length * 640 * lanes, "attend_back",
    )


def row_tile(length):
    return min(256, length)


def tall(a, tile):
    if len(a.shape) == 2:
        return pl.BlockSpec((tile, a.shape[1]), lambda i, *_: (i, 0))
    return pl.BlockSpec((a.shape[0], tile, a.shape[2]), lambda i, *_: (0, i, 0))


def tall_from(a, tile, per):
    if len(a.shape) == 2:
        return pl.BlockSpec((tile, a.shape[1]), lambda i, at: (at[0] * per + i, 0))
    return pl.BlockSpec((a.shape[0], tile, a.shape[2]), lambda i, at: (0, at[0] * per + i, 0))


class Slab:
    def __init__(self, array, width, block, order):
        self.array, self.width = array, width
        shape = (array.shape[0], 1, array.shape[2], width)
        self.spec = pl.BlockSpec(shape, lambda i, at: (0, at[1 + order], 0, block))


class Whole:
    def __init__(self, array, width, block):
        self.array, self.width = array, width
        self.spec = pl.BlockSpec((array.shape[0], width), lambda i, *_: (0, block))


def arrays(slabs):
    return [w.array for w in slabs]


def specs_of(slabs):
    return [w.spec for w in slabs]


def rows_of(slab):
    shape = slab.array.shape
    return shape[0] if len(shape) == 2 else shape[0] * shape[2]


def flat(ref):
    if len(ref.shape) == 2:
        return ref[...]
    return ref[:, 0].reshape(ref.shape[0] * ref.shape[2], ref.shape[3])


def project_kernel(x_ref, b_ref, *refs):
    count = b_ref.shape[0]
    weights, (q_ref, k_ref, v_ref) = refs[:count], refs[count:]
    lanes = q_ref.shape[2]
    scale = 1.0 / math.sqrt(DH)
    x = x_ref[...]
    for i in range(count):
        projected = nn(x, weights[i][...]) + b_ref[i]
        q_ref[i] = (projected[:, :lanes].astype(BF16).astype(F32) * scale).astype(BF16)
        k_ref[i] = projected[:, lanes : 2 * lanes].astype(BF16)
        v_ref[i] = projected[:, 2 * lanes :].astype(BF16)


def project(x, weights, bias):
    length, model = x.shape
    lanes = weights[0].shape[1] // 3
    tile = row_tile(length)
    outs = [struct((len(weights), length, lanes), BF16)] * 3
    return launch(
        project_kernel, length // tile, [], [x, bias] + weights,
        [tall(x, tile), fixed(bias)] + [fixed(w) for w in weights], outs,
        [tall(a, tile) for a in outs], [], 6 * length * model * lanes * len(weights), "project",
    )


def context_out(at, stacks, weights, part, dtype):
    tile = row_tile(part)
    model = rows_of(weights[0])
    per, _, lanes = stacks[0].shape
    out = struct((part, model), dtype)

    def kernel(at_ref, *refs):
        left = jnp.concatenate([ctx[i] for ctx in refs[: len(stacks)] for i in range(per)], axis=1)
        right = jnp.concatenate([flat(w)[:, w.shape[-1] - lanes :] for w in refs[len(stacks) : -1]], axis=1)
        refs[-1][...] = nt(left, right).astype(refs[-1].dtype)

    return launch(
        kernel, part // tile, [at], list(stacks) + arrays(weights),
        [tall_from(a, tile, part // tile) for a in stacks] + specs_of(weights), [out], [tall(out, tile)], [],
        2 * part * model * lanes * len(weights), "context_out",
    )[0]


def context_back_kernel(at, ga_ref, *refs):
    weights, out_ref = refs[:-1], refs[-1]
    lanes = out_ref.shape[2]
    right = jnp.concatenate([flat(w)[:, w.shape[-1] - lanes :] for w in weights], axis=1)
    grad = nn(ga_ref[...], right).astype(BF16)
    for i in range(out_ref.shape[0]):
        out_ref[i] = grad[:, i * lanes : (i + 1) * lanes]


def context_back(at, ga, weights, lanes):
    tile = row_tile(ga.shape[0])
    count = len(weights)
    out = struct((count, ga.shape[0], lanes), BF16)
    return launch(
        context_back_kernel, ga.shape[0] // tile, [at], [ga] + arrays(weights),
        [tall(ga, tile)] + specs_of(weights), [out], [tall(out, tile)], [],
        2 * math.prod(ga.shape) * lanes * count, "context_back",
    )[0]


def ffn_in_kernel(at, y_ref, b_ref, *refs):
    count = b_ref.shape[0]
    weights, (act_ref, slope_ref) = refs[:count], refs[-2:]
    y = y_ref[...]
    for i in range(count):
        inner = nn(y, flat(weights[i])) + b_ref[i]
        share = 0.5 + 0.5 * lax.erf(inner * math.sqrt(0.5))
        density = jnp.exp(-0.5 * inner * inner) * (1.0 / math.sqrt(2.0 * math.pi))
        act_ref[i] = (inner * share).astype(BF16)
        slope_ref[i] = (share + inner * density).astype(BF16)


def place(a, tile, first):
    return pl.BlockSpec((a.shape[0], tile, a.shape[2]), lambda i, *_: (0, first + i, 0))


def ffn_in(at, y, bias, weights, ways, place_at, earlier):
    part, model = y.shape
    tile = row_tile(part)
    first = place_at * (part // tile)
    wide = bias.shape[2]
    count = len(weights)
    out = struct((count, part * ways, wide), BF16)
    anywhere = [pl.BlockSpec(memory_space=pl.ANY)] * len(earlier)
    return launch(
        ffn_in_kernel, part // tile, [at], [y, bias] + arrays(weights) + earlier,
        [tall(y, tile), fixed(bias)] + specs_of(weights) + anywhere,
        [out, out], [place(out, tile, first)] * 2, [],
        6 * part * model * wide * count, "ffn_in",
        {3 + count + i: i for i in range(len(earlier))},
    )


def ffn_out_kernel(at, act_ref, *refs):
    weights, out_ref = refs[:-1], refs[-1]
    total = nt(act_ref[0], flat(weights[0]))
    for i in range(1, len(weights)):
        total += nt(act_ref[i], flat(weights[i]))
    out_ref[...] = total.astype(out_ref.dtype)


def ffn_out(at, act, weights, part, place_at, dtype):
    tile = row_tile(part)
    model = rows_of(weights[0])
    out = struct((part, model), dtype)
    return launch(
        ffn_out_kernel, part // tile, [at], [act] + arrays(weights),
        [place(act, tile, place_at * (part // tile))] + specs_of(weights),
        [out], [tall(out, tile)], [], 2 * part * model * act.shape[0] * act.shape[2], "ffn_out",
    )[0]


def ffn_back_kernel(at, gb_ref, slope_ref, *refs):
    count = slope_ref.shape[0]
    outs, ins = refs[:count], refs[count : 2 * count]
    gi_ref, sum_ref, out_ref = refs[-3:]
    gb = gb_ref[...]
    total = None
    sums = []
    for i in range(count):
        grad = nn(gb, flat(outs[i])) * slope_ref[i].astype(F32)
        low = grad.astype(BF16)
        gi_ref[i] = low
        sums.append(jnp.sum(grad, axis=0, keepdims=True))
        term = nt(low, flat(ins[i]))
        total = term if total is None else total + term
    out_ref[...] = total.astype(out_ref.dtype)

    @pl.when(pl.program_id(0) == 0)
    def _():
        sum_ref[...] = jnp.zeros_like(sum_ref)

    for i in range(count):
        sum_ref[i] += sums[i]


def ffn_back(at, gb, slope, outs_w, ins_w, place_at, earlier, dtype):
    part, model = gb.shape
    tile = row_tile(part)
    first = place_at * (part // tile)
    count, _, wide = slope.shape
    anywhere = [pl.BlockSpec(memory_space=pl.ANY)] * len(earlier)
    outs = [struct(slope.shape, BF16), struct((count, 1, wide), F32), struct((part, model), dtype)]
    return launch(
        ffn_back_kernel, part // tile, [at], [gb, slope] + arrays(outs_w + ins_w) + earlier,
        [tall(gb, tile), place(slope, tile, first)] + specs_of(outs_w + ins_w) + anywhere,
        outs, [place(outs[0], tile, first), fixed(outs[1]), tall(outs[2], tile)], [],
        4 * part * model * wide * count, "ffn_back",
        {3 + 2 * count + i: i for i in range(len(earlier))},
    )


def inputs_back(at, stacks, weights, part, dtype):
    tile = row_tile(part)
    model = weights[0].shape[0]
    out = struct((part, model), dtype)
    per = stacks[0].shape[0]

    def kernel(at_ref, *refs):
        grads, rest, out_ref = refs[: len(stacks)], refs[len(stacks) : -1], refs[-1]
        total = None
        for i, weight in enumerate(rest):
            term = nt(grads[i // per][i % per], weight[...])
            total = term if total is None else total + term
        out_ref[...] = total.astype(out_ref.dtype)

    return launch(
        kernel, part // tile, [at], list(stacks) + weights,
        [tall_from(a, tile, part // tile) for a in stacks] + [fixed(w) for w in weights], [out], [tall(out, tile)], [],
        2 * part * model * weights[0].shape[1] * len(weights), "inputs_back",
    )[0]


def transpose_into(left_t, lefts):
    first = 0
    for left in lefts:
        left_t[:, pl.ds(first, left.shape[0])] = left[...].T
        first += left.shape[0]


def weight_grad(pairs):
    count = pairs[0][1].shape[0]
    length, model = pairs[0][1].shape[1], pairs[0][0][0].shape[1]
    wides = [right.shape[2] for _, right, _ in pairs]
    out = struct((model, sum(wides)), BF16)
    lefts = [left for group, _, _ in pairs for left in group]
    rights = [right for _, right, _ in pairs]
    many = len(pairs)

    def kernel(*refs):
        left_refs, refs = refs[: len(lefts)], refs[len(lefts) :]
        right_refs, outs = refs[:many], refs[many : many + count]
        left_t, slots, sems = refs[many + count :]
        copies = [pltpu.make_async_copy(slots.at[k % 2], outs[k], sems.at[k % 2]) for k in range(count)]

        def step(k):
            if k == 0:
                first = 0
                for n, (group, _, _) in enumerate(pairs):
                    transpose_into(left_t.at[n], left_refs[first : first + len(group)])
                    first += len(group)
            if k > 1:
                copies[k - 2].wait()
            column = 0
            for n, wide in enumerate(wides):
                slots[k % 2, :, column : column + wide] = nn(left_t[n], right_refs[n][0]).astype(BF16)
                column += wide
            copies[k].start()
            if k == count - 1:
                for last in copies[max(k - 1, 0) :]:
                    last.wait()

        for k in range(count):
            pl.when(pl.program_id(0) == k)(functools.partial(step, k))

    return launch(
        kernel, count, [], lefts + rights, [fixed(a) for a in lefts] + [slab_from(a, f) for _, a, f in pairs],
        [out] * count, [pl.BlockSpec(memory_space=pl.ANY)] * count,
        [
            pltpu.VMEM((many, model, length), BF16),
            pltpu.VMEM((2,) + out.shape, BF16),
            pltpu.SemaphoreType.DMA((2,)),
        ],
        2 * length * model * sum(wides) * count, "weight_grad",
    )


def weight_grad_shards(at, lefts, right, ring, near, seqs):
    count, length, wide = right.shape
    model = lefts[0].shape[1]
    halves = count // seqs
    own = model // (ring * near)
    out = struct((near, seqs, own, wide * halves), BF16)
    parts = len(lefts)
    block = near * own

    def kernel(at_ref, *refs):
        right_ref, outs, left_t = refs[parts], refs[parts + 1 : -1], refs[-1]

        @pl.when(pl.program_id(0) == 0)
        def _():
            transpose_into(left_t, refs[:parts])

        for k in range(ring):
            first = pl.multiple_of(((at_ref[1 + seqs] + k) % ring) * block, block)
            made = nn(left_t[pl.ds(first, block), :], right_ref[0]).astype(BF16)
            outs[k][:, 0] = made.reshape(near, own, wide)

    spec = pl.BlockSpec((near, 1, own, wide), lambda i, at: (0, at[1 + i // halves], 0, i % halves))
    return launch(
        kernel, count, [at], list(lefts) + [right], [fixed(a) for a in lefts] + [slab(right)], [out] * ring,
        [spec] * ring, [pltpu.VMEM((model, length), BF16)], 2 * length * model * wide * count, "weight_grad_shards",
    )


def assemble(place, pieces):
    ring = len(pieces)
    each = [p if isinstance(p, list) else [p] for p in pieces]
    shape = pieces[0].shape[1:]
    out = struct((ring,) + shape, BF16)
    operands = [a for p in each for a in p]

    def kernel(place_ref, *refs):
        sources, outs, sems = list(refs[: len(operands)]), refs[len(operands) : -1], refs[-1]
        copies = []
        for k, p in enumerate(each):
            spot = (place_ref[0] + k) % ring
            own = [sources.pop(0) for _ in p]
            for h in range(2):
                source = own[h] if len(own) == 2 else own[0].at[h]
                copies.append(pltpu.make_async_copy(source, outs[h].at[spot], sems.at[2 * k + h]))
        for copy in copies:
            copy.start()
        for copy in copies:
            copy.wait()

    anywhere = pl.BlockSpec(memory_space=pl.ANY)
    return launch(
        kernel, 1, [place], operands, [anywhere] * len(operands), [out] * 2, [fixed(out)] * 2,
        [pltpu.SemaphoreType.DMA((2 * ring,))], 0, "assemble",
    )


def norm_rows(hidden):
    mean = jnp.mean(hidden, axis=1, keepdims=True)
    square = jnp.mean(hidden * hidden, axis=1, keepdims=True)
    inv_std = lax.rsqrt(square - mean * mean + NORM_EPS)
    return (hidden - mean) * inv_std, inv_std


def norm_rows_back(incoming, centred, inv_std, gain):
    scaled = incoming * gain
    first = jnp.mean(scaled, axis=1, keepdims=True)
    second = jnp.mean(scaled * centred, axis=1, keepdims=True)
    return inv_std * (scaled - first - centred * second)


def add_sums(sum_ref, terms):
    @pl.when(pl.program_id(0) == 0)
    def _():
        sum_ref[...] = jnp.zeros_like(sum_ref)

    for i, term in enumerate(terms):
        sum_ref[i : i + 1, :] += jnp.sum(term, axis=0, keepdims=True)


def norm_a_kernel(at, mine_ref, got_ref, x_ref, vec_ref, centred_ref, inv_ref, y_ref):
    hidden = mine_ref[...] + got_ref[...].astype(F32) + x_ref[...].astype(F32) + vec_ref[0]
    centred, inv_std = norm_rows(hidden)
    centred_ref[...] = centred
    inv_ref[...] = inv_std
    y_ref[...] = (centred * vec_ref[1] + vec_ref[2]).astype(BF16)


def norm_a(at, mine, got, x, vec):
    part, model = mine.shape
    tile = row_tile(part)
    outs = [struct((part, model), F32), struct((part, 1), F32), struct((part, model), BF16)]
    return launch(
        norm_a_kernel, part // tile, [at], [mine, got, x, vec],
        [tall(mine, tile), tall(got, tile), tall_from(x, tile, part // tile), fixed(vec)],
        outs, [tall(a, tile) for a in outs], [], 20 * part * model, "norm_a",
    )


def norm_b_kernel(mine_ref, got_ref, centred_a_ref, cot_ref, vec_ref, out_ref, grad_ref, low_ref, sum_ref):
    normed = centred_a_ref[...] * vec_ref[1] + vec_ref[2]
    hidden = mine_ref[...] + got_ref[...].astype(F32) + vec_ref[3] + normed
    centred, inv_std = norm_rows(hidden)
    out_ref[...] = (centred * vec_ref[4] + vec_ref[5]).astype(BF16)
    incoming = cot_ref[...].astype(F32)
    grad = norm_rows_back(incoming, centred, inv_std, vec_ref[4])
    grad_ref[...] = grad
    low_ref[...] = grad.astype(BF16)
    add_sums(sum_ref, (grad, incoming * centred, incoming))


def norm_b(mine, got, centred_a, cot, vec):
    part, model = mine.shape
    tile = row_tile(part)
    outs = [struct((part, model), BF16), struct((part, model), F32), struct((part, model), BF16), struct((3, model), F32)]
    return launch(
        norm_b_kernel, part // tile, [], [mine, got, centred_a, cot, vec],
        [tall(a, tile) for a in (mine, got, centred_a, cot)] + [fixed(vec)],
        outs, [tall(a, tile) for a in outs[:3]] + [fixed(outs[3])], [], 40 * part * model, "norm_b",
    )


def norm_a_back_kernel(mine_ref, got_ref, gb_ref, centred_ref, inv_ref, vec_ref, grad_ref, low_ref, sum_ref):
    incoming = mine_ref[...] + got_ref[...].astype(F32) + gb_ref[...]
    centred = centred_ref[...]
    grad = norm_rows_back(incoming, centred, inv_ref[...], vec_ref[1])
    grad_ref[...] = grad
    low_ref[...] = grad.astype(BF16)
    add_sums(sum_ref, (grad, incoming * centred, incoming))


def norm_a_back(mine, got, gb, centred, inv, vec):
    part, model = mine.shape
    tile = row_tile(part)
    outs = [struct((part, model), F32), struct((part, model), BF16), struct((3, model), F32)]
    return launch(
        norm_a_back_kernel, part // tile, [], [mine, got, gb, centred, inv, vec],
        [tall(a, tile) for a in (mine, got, gb, centred, inv)] + [fixed(vec)],
        outs, [tall(a, tile) for a in outs[:2]] + [fixed(outs[2])], [], 30 * part * model, "norm_a_back",
    )


def body(
    rows,
    cols,
    tokens,
    segments,
    wqkv,
    bias_qv,
    wo,
    bias_o,
    gain_a,
    shift_a,
    w_in,
    bias_in,
    w_out,
    bias_out,
    gain_b,
    shift_b,
    cotangent,
):
    seqs, length = segments.shape
    ways = cols // seqs
    width = tokens.shape[1]
    model = width * cols
    heads = wqkv.shape[1] // (3 * DH)
    lanes = heads * DH // 2
    hid = w_in.shape[1]
    part = length // ways
    own_rows = wqkv.shape[0]
    row, col = lax.axis_index("row"), lax.axis_index(COL)
    seq, way = col // ways, col % ways
    by_seq = [Stage(COL, cols, mask * ways, col) for mask in bits_of(seqs)]
    by_way = [Stage(COL, cols, mask, col) for mask in bits_of(ways)]
    by_row = [Stage("row", rows, mask, row) for mask in bits_of(rows)]
    ns, nw, nr = len(by_seq), len(by_way), len(by_row)
    outer, near = by_row[:-1], by_row[-1]
    parts = range(ways)
    orders = [0]
    for mask in bits_of(seqs):
        orders = orders + [o ^ mask for o in orders]
    ring = rows // 2
    place = row // 2
    at = [jnp.stack([way ^ p] + [seq ^ o for o in orders] + [place]).astype(jnp.int32) for p in parts]
    here = place.reshape(1).astype(jnp.int32)

    def turn(block, step):
        return lax.ppermute(block, "row", [(i, (i + 2 * step) % rows) for i in range(rows)])

    def turn_first(piece):
        return turn(piece, 1), turn(piece, -1)

    def turn_rest(piece, got):
        plus, minus = got
        pieces = {0: piece, ring - 1: plus, 1: minus}
        for k in range(2, ring // 2):
            plus, minus = turn(plus, 1), turn(minus, -1)
            pieces[ring - k], pieces[k] = plus, minus
        pieces[ring // 2] = [turn(plus[0], 1), turn(minus[1], -1)]
        return [pieces[k] for k in range(ring)]

    def held(block, mark):
        return after(block, *mark) if mark else block

    def spread(halves):
        one, two = [h[None, None] for h in halves]
        return one, two, near.trade(one), by_seq[0].trade(two)

    def spread_rest(one, two, one_got, two_got):
        one, two = near.join(one, one_got, 0), by_seq[0].join(two, two_got, 1)
        return one, two, by_seq[0].trade(one), near.trade(two)

    def spread_end(one, two, one_got, two_got):
        return jnp.stack((by_seq[0].join(one, one_got, 1), near.join(two, two_got, 0)))

    def whole_shards(pieces):
        return [g.reshape((rows,) + g.shape[2:]) for g in assemble(here, pieces)]

    def last_first(one, two):
        twos = [two]
        for stage in by_seq:
            twos = twos + [stage.trade(b) for b in twos]
        return near.trade(one), twos[1:]

    def last_rest(one, two, one_got, two_got):
        def whole(block, got):
            return near.join(block, got, nr - 1).reshape(model, -1)

        twos = [two] + two_got
        twos_got = [near.trade(b) for b in twos]
        ones = [whole(one, one_got)]
        for stage in by_seq:
            ones = ones + [stage.trade(b) for b in ones]
        return ones, twos, twos_got

    def last_end(ones, twos, twos_got):
        twos = [near.join(b, g, nr - 1).reshape(model, -1) for b, g in zip(twos, twos_got)]
        return [b for j in range(seqs) for b in (ones[j], twos[j])]

    def halves_of(weight):
        half = weight.shape[1] // 2
        return weight[:, :half], weight[:, half:]

    by_kind = wqkv.reshape(own_rows, 2, heads // 2, 3, DH).transpose(1, 0, 3, 2, 4)
    by_kind = by_kind.reshape(2, own_rows, -1)
    def by_bits(pieces):
        return [b.reshape((2,) * (nr - 1) + (1,) + b.shape[1:]) for b in assemble(here, pieces)]

    wo_t = halves_of(wo.T)
    qkv_got = turn_first(by_kind)
    in_piece = jnp.stack([jnp.concatenate((a, b), axis=1) for a, b in zip(halves_of(w_in), wo_t)])
    qkv_pieces = turn_rest(by_kind, qkv_got)
    in_got = turn_first(after(in_piece, *qkv_got))
    out_shards = spread(halves_of(w_out.T))
    out_first = out_shards[2:]
    out_shards = spread_rest(*out_shards)
    far_qkv = by_bits(qkv_pieces)

    labels = lax.dynamic_slice_in_dim(segments, seq, 1, 0)[0]
    windows = key_windows(labels)
    lab_col, lab_row = labels[:, None], labels[None, :]

    def exchange(array, split, whole, mark=()):
        blocks = [array]
        for stage in split + whole:
            both = blocks[0] if len(blocks) == 1 else jnp.concatenate(blocks, axis=1)
            if stage in split:
                both = both.reshape(2, both.shape[0] // 2, both.shape[1])
                mine, sent = pick(both, stage.bit, 0)[0], pick(both, 1 - stage.bit, 0)[0]
            else:
                mine = sent = both
            got = held(stage.trade(sent), mark)
            low = stage.bit == 0
            blocks = [
                half
                for i in range(len(blocks))
                for a, b in [(mine[:, i * width : (i + 1) * width], got[:, i * width : (i + 1) * width])]
                for half in (jnp.where(low, a, b), jnp.where(low, b, a))
            ]
        return jnp.concatenate(blocks, axis=1)

    def to_features(array):
        blocks = [array]
        for stage in by_seq + by_way:
            half = blocks[0].shape[1] // 2
            both = blocks[0] if len(blocks) == 1 else jnp.concatenate(blocks, axis=0)
            mine = lax.dynamic_slice_in_dim(both, stage.bit * half, half, 1)
            got = stage.trade(lax.dynamic_slice_in_dim(both, (1 - stage.bit) * half, half, 1))
            low = stage.bit == 0
            count = array.shape[0]
            blocks = [
                half_rows
                for i in range(len(blocks))
                for a, b in [(mine[i * count : (i + 1) * count], got[i * count : (i + 1) * count])]
                for half_rows in (jnp.where(low, a, b), jnp.where(low, b, a))
            ]
        return jnp.concatenate(blocks, axis=0)

    def widen(array, whole):
        for stage in whole:
            got = stage.trade(array)
            low = stage.bit == 0
            array = jnp.concatenate(
                [
                    half
                    for i in range(array.shape[1] // width)
                    for a, b in [(array[:, i * width : (i + 1) * width], got[:, i * width : (i + 1) * width])]
                    for half in (jnp.where(low, a, b), jnp.where(low, b, a))
                ],
                axis=1,
            )
        return array

    half_x = exchange(after(tokens, *out_first), by_seq, [])
    vectors = jnp.concatenate(
        [v.reshape(-1, width) for v in (bias_o, gain_a, shift_a, bias_out, gain_b, shift_b, bias_qv, bias_in)]
    )
    vectors = after(vectors, half_x)
    whole_x = widen(half_x, by_way)
    pairs = [vectors]
    for stage in by_seq:
        pairs = pairs + [stage.trade(v) for v in pairs]
    blocks = [vectors[:6]]
    for i, stage in enumerate(by_seq):
        got = jnp.concatenate([p[:6] for p in pairs[1 << i : 2 << i]], axis=1)
        low = stage.bit == 0
        both = jnp.concatenate(blocks, axis=1)
        blocks = [
            half
            for k in range(len(blocks))
            for a, b in [(both[:, k * width : (k + 1) * width], got[:, k * width : (k + 1) * width])]
            for half in (jnp.where(low, a, b), jnp.where(low, b, a))
        ]
    for stage in by_way:
        both = jnp.concatenate(blocks, axis=1)
        got = stage.trade(both)
        low = stage.bit == 0
        blocks = [
            half
            for k in range(len(blocks))
            for a, b in [(both[:, k * width : (k + 1) * width], got[:, k * width : (k + 1) * width])]
            for half in (jnp.where(low, a, b), jnp.where(low, b, a))
        ]
    vec = jnp.concatenate(blocks, axis=1).astype(F32)[:, None, :]
    nq = bias_qv.shape[0] // width
    q_biases, in_biases = [], []
    for j in range(seqs):
        both = pairs[j][6 : 6 + nq].astype(F32).reshape(2, heads // 2, 2, DH)
        both = both.transpose(0, 2, 1, 3).reshape(2, 2, lanes)
        q_biases.append(jnp.concatenate((both[:, :1], jnp.zeros_like(both[:, :1]), both[:, 1:]), axis=1))
        in_biases.append(pairs[j][6 + nq :].astype(F32).reshape(2, 1, hid // 2))
    q_bias = jnp.concatenate(q_biases, axis=0).reshape(2 * seqs, 1, 3 * lanes)
    in_bias = jnp.concatenate(in_biases, axis=0)

    qkv_first = last_first(*far_qkv)
    qkv_rest = last_rest(*far_qkv, *qkv_first)
    in_pieces = turn_rest(in_piece, [after(g, *far_qkv) for g in in_got])
    far_in = by_bits(in_pieces)
    in_first = last_first(*[after(b, qkv_rest[0][0], *qkv_first[1]) for b in far_in])
    qkv_all = last_end(*qkv_rest)
    out_piece = spread_end(*out_shards[:2], *[after(b, *far_qkv) for b in out_shards[2:]])
    out_got = turn_first(after(out_piece, *far_in))
    pairs_of = [(j, h) for j in range(seqs) for h in range(2)]

    def gather_parts(own):
        blocks = {0: own}
        for mask, stage in zip(bits_of(ways), by_way):
            for p in list(blocks):
                blocks[p ^ mask] = stage.trade(blocks[p])
        return [blocks[p] for p in parts]

    def scatter_parts(make):
        terms = {p: make(p, F32 if p == 0 else BF16) for p in reversed(parts)}
        for mask, stage in list(zip(bits_of(ways), by_way))[:-1]:
            for p in [q for q in terms if q & mask]:
                got = stage.trade(terms.pop(p))
                terms[p ^ mask] = add(terms[p ^ mask], got)
        return terms[0], by_way[-1].trade(terms[1])

    def whole_rows(blocks):
        blocks = list(blocks)
        for mask, stage in zip(reversed(bits_of(ways)), reversed(by_way)):
            low = stage.bit == 0
            for p in parts:
                if not p & mask:
                    a, b = blocks[p], blocks[p | mask]
                    blocks[p], blocks[p | mask] = jnp.where(low, a, b), jnp.where(low, b, a)
        return jnp.concatenate(blocks, axis=0)

    def fold_start(block):
        block = block.reshape((2,) * nr + (own_rows, -1))
        return block, near.trade(pick(block, 1 - near.bit, nr - 1))

    def fold_end(block, got):
        return add(pick(block, near.bit, nr - 1), got)

    def across_start(blocks):
        count = len(blocks) // 2
        return blocks[:count], [by_seq[-1].trade(b) for b in blocks[count:]]

    def across_end(mine, gots):
        blocks = [add(m, g) for m, g in zip(mine, gots)]
        for stage in list(reversed(by_seq))[1:]:
            count = len(blocks) // 2
            blocks = [add(blocks[j], stage.trade(blocks[count + j])) for j in range(count)]
        return blocks[0]

    def scatter_far(one, two, marks=()):
        for n, (i, stage) in enumerate(reversed(list(enumerate(outer)))):
            halves = (one, two)
            sent = jnp.stack([pick(b, 1 - stage.bit, i) for b in halves])
            got = held(stage.trade(sent), marks[n] if n < len(marks) else ())
            one, two = [add(pick(b, stage.bit, i), got[h]) for h, b in enumerate(halves)]
        return one.reshape(own_rows, -1).astype(F32), two.reshape(own_rows, -1).astype(F32)

    q, k, v = project(whole_x, qkv_all, q_bias)
    contexts, lses, ready = [], [], [in_first[0], *in_first[1]]
    for j in range(seqs):
        context, lse = attend(windows, after(q, *contexts, *ready) if j else q, k, v, lab_col, lab_row, 2 * j, 2)
        contexts, lses = contexts + [context], lses + [lse]
        if j == 0:
            in_first = after(in_first[0], context), [after(b, context) for b in in_first[1]]
            in_rest = last_rest(*far_in, *in_first)
    contexts = [after(c, *contexts, *out_got) for c in contexts]
    out_pieces = turn_rest(out_piece, [after(g, contexts[-1]) for g in out_got])
    in_blocks = last_end(*in_rest)
    in_all = [Whole(b, hid // 2, 0) for b in in_blocks]
    aligned = lanes % 128 == 0
    wo_all = [Whole(b, lanes, hid // 2 // lanes) if aligned else Whole(b, b.shape[1], 0) for b in in_blocks]
    mine, got = scatter_parts(lambda p, dtype: context_out(at[p], contexts, wo_all, part, dtype))
    centred_a, inv_a, y = norm_a(at[0], mine, got, whole_x, vec)
    y_parts = gather_parts(y)
    earlier = []
    for p in parts:
        earlier = ffn_in(at[0], y_parts[p], in_bias, in_all, ways, p, list(earlier))
    active, slope = earlier
    whole_out = whole_shards([after(p, active) if not isinstance(p, list) else [after(b, active) for b in p] for p in out_pieces])
    out_all = [Slab(whole_out[h], hid // 2, 0, j) for j, h in pairs_of]
    cot = exchange(after(cotangent, contexts[-1]), by_seq + by_way, [], (active,))
    mine, got = scatter_parts(lambda p, dtype: ffn_out(at[0], active, out_all, part, p, dtype))
    output, grad_b, gb, sums_b = norm_b(mine, got, centred_a, cot, vec)

    gb_parts = gather_parts(gb)
    output = to_features(after(output, gb_parts[-1]))
    chunks = weight_grad_shards(at[0], gb_parts, active, ring, 2, seqs)
    plus, minus = turn(chunks[ring // 2][0], 1), turn(chunks[ring // 2][1], -1)
    tie = (chunks[0],)
    terms, sum_in, earlier = {}, 0.0, []
    for p in parts:
        grad_inner, sums, terms[p] = ffn_back(
            at[0], after(gb_parts[p], *tie), slope, out_all, in_all, p, earlier, F32 if p == 0 else BF16
        )
        earlier = [grad_inner]
        if p == parts[-1]:
            firsts = plus, minus
            plus, minus = after(plus, grad_inner), after(minus, grad_inner)
            for far in reversed(range(1, ring // 2)):
                up, down = chunks[far], chunks[ring - far]
                if far == ring // 2 - 1:
                    up = jnp.stack((add(up[0], plus), up[1]))
                    down = jnp.stack((down[0], add(down[1], minus)))
                else:
                    up, down = add(up, plus), add(down, minus)
                tie = (up, down)
                plus, minus = turn(up, 1), turn(down, -1)
        sum_in = sum_in + sums
    mine, got = scatter_parts(lambda p, dtype: terms[p])
    grad_w_in = weight_grad([(y_parts, after(grad_inner, *firsts), 0)])
    grad_a, ga, sums_a = norm_a_back(mine, got, after(grad_b, grad_w_in[0]), centred_a, inv_a, vec)
    whole_ga = whole_rows(gather_parts(ga))
    grad_context = context_back(at[0], whole_ga, wo_all, lanes)
    ones_mine, ones_got = across_start(grad_w_in[0::2])
    twos_in = [fold_start(b) for b in grad_w_in[1::2]]
    gots = ones_got + [g for _, g in twos_in] + [plus, minus]
    stacks, sums_p, made, later = {}, [], {}, []
    ready = grad_context
    for j in reversed(range(seqs)):
        projected, sums = attend_back(
            windows, q, k, v, after(grad_context, ready), lses[j], lab_col, lab_row, 2 * j, 2
        )
        if j == seqs - 1:
            projected = after(projected, *gots)
        made[j] = weight_grad([([whole_x], projected, 0), ([whole_ga], contexts[j], 0)])
        ready = made[j][0]
        stacks[j], sums_p = projected, [sums] + sums_p
        if j == seqs - 1:
            ones_got, twos_got = [held(g, (projected,)) for g in ones_got], [held(g, (projected,)) for _, g in twos_in]
            one_in = fold_start(across_end(ones_mine, ones_got))
            two_in = across_start([fold_end(b, g) for (b, _), g in zip(twos_in, twos_got)])
            later = [one_in[1]] + two_in[1]
            out_sum = add_three(chunks[0], after(plus, projected), after(minus, projected))
            out_sum = near.reduce(after(out_sum, ready), 0)
    sum_projected = jnp.concatenate(sums_p, axis=0)
    for stage in reversed(by_seq):
        out_sum = stage.reduce(after(out_sum, ready), 1)
    halves_in = fold_end(one_in[0], held(one_in[1], (ready,))), across_end(two_in[0], [held(g, (ready,)) for g in two_in[1]])
    ones_mine, ones_got = across_start([made[j][0] for j in range(seqs)])
    twos_last = [fold_start(made[j][1]) for j in range(seqs)]
    gots = ones_got + [g for _, g in twos_last]
    stacks = [after(stacks[j], ready, *later) for j in range(seqs)]
    term = {1: inputs_back(at[1], stacks, qkv_all, part, BF16)} if ways == 2 else {}
    tied = [after(a, *gots[:1], *term.values()) for a in stacks]
    mine, got = scatter_parts(
        lambda p, dtype: term[p] if p in term else inputs_back(at[p], tied, qkv_all, part, dtype)
    )
    ones_got, twos_got = [held(g, tuple(term.values())) for g in ones_got], [g for _, g in twos_last]
    one_last = fold_start(across_end(ones_mine, ones_got))
    two_last = across_start([fold_end(b, g) for (b, _), g in zip(twos_last, twos_got)])
    in_halves = scatter_far(*halves_in, [(mine,)])
    grad_tokens = to_features((after(mine, one_last[1]) + got.astype(F32) + grad_a).astype(BF16)).astype(F32)
    qkv_halves = scatter_far(fold_end(*one_last), across_end(*two_last))

    per_hidden = []
    for j in range(seqs):
        two = sum_projected[2 * j : 2 * j + 2].reshape(2, 2, heads // 2, DH).transpose(0, 2, 1, 3)
        per_hidden.append(jnp.concatenate((two.reshape(-1), sum_in[2 * j : 2 * j + 2].reshape(-1))))
    block = after(jnp.concatenate((sums_a, sums_b), axis=0), one_last[0])
    per_hidden = [after(v, one_last[0]) for v in per_hidden]
    for stage in by_seq + by_way:
        half = block.shape[1] // 2
        got = stage.trade(lax.dynamic_slice_in_dim(block, (1 - stage.bit) * half, half, 1))
        block = lax.dynamic_slice_in_dim(block, stage.bit * half, half, 1) + got
    for stage in reversed(by_seq):
        count = len(per_hidden) // 2
        per_hidden = [per_hidden[j] + stage.trade(per_hidden[count + j]) for j in range(count)]
    sums = jnp.concatenate((per_hidden[0], block.reshape(-1)))
    for stage in by_row:
        sums = sums + stage.trade(sums)
    nqv = bias_qv.shape[0]
    sum_qv, sum_in = sums[:nqv], sums[nqv : nqv + hid]
    rest = sums[nqv + hid :].reshape(6, width)
    split = 3 * lanes
    grad_qkv = jnp.stack([h[:, :split] for h in qkv_halves])
    grad_qkv = grad_qkv.reshape(2, own_rows, 3, heads // 2, DH).transpose(1, 0, 3, 2, 4)
    return (
        output,
        grad_tokens,
        grad_qkv.reshape(own_rows, -1),
        sum_qv,
        jnp.concatenate([h[:, split:] for h in qkv_halves], axis=1).T,
        rest[0],
        rest[1],
        rest[2],
        jnp.concatenate(in_halves, axis=1),
        sum_in,
        out_sum.reshape(own_rows, hid).astype(F32).T,
        rest[3],
        rest[4],
        rest[5],
    )


def solution(mesh):
    rows, cols = mesh.shape["row"], mesh.shape["col"]
    tile, across, down, flat_col = P("row", COL), P("row", None), P(COL, "row"), P(COL)
    in_specs = (
        tile, across, tile, flat_col, down, flat_col, flat_col, flat_col,
        tile, flat_col, down, flat_col, flat_col, flat_col, tile,
    )
    out_specs = (
        tile, tile, tile, flat_col, down, flat_col, flat_col, flat_col,
        tile, flat_col, down, flat_col, flat_col, flat_col,
    )

    def run(*args):
        seqs = args[1].shape[0] // rows
        fine = jax.sharding.Mesh(mesh.devices.reshape(rows, seqs, cols // seqs), ("row",) + COL)

        def layer(*local):
            return body(rows, cols, *local)

        return jax.shard_map(layer, mesh=fine, in_specs=in_specs, out_specs=out_specs, check_vma=False)(*args)

    return run
```

```python
import functools
import math

import jax
import jax.numpy as jnp
from jax import lax
from jax.experimental import pallas as pl
from jax.experimental.pallas import tpu as pltpu
from jax.sharding import PartitionSpec as P

DH = 64
NORM_EPS = 1e-06
MASKED = -1000000000.0
LONGEST = 256
COL = ("seq", "way")
SHARE = 1
F32 = jnp.float32
BF16 = jnp.bfloat16


def nn(left, right):
    return lax.dot_general(left, right, (((1,), (0,)), ((), ())), preferred_element_type=F32)


def nt(left, right):
    return lax.dot_general(left, right, (((1,), (1,)), ((), ())), preferred_element_type=F32)


def tn(left, right):
    return lax.dot_general(left, right, (((0,), (0,)), ((), ())), preferred_element_type=F32)


def after(block, *others):
    return lax.optimization_barrier((block,) + others)[0]


def pick(block, bit, dim):
    return lax.dynamic_slice_in_dim(block, bit, 1, dim)


def bits_of(count):
    return [1 << b for b in reversed(range(count.bit_length() - 1))]


class Stage:
    def __init__(self, axis, count, mask, index):
        self.axis, self.pairs = axis, [(i, i ^ mask) for i in range(count)]
        self.bit = (index // mask) % 2

    def trade(self, block):
        return lax.ppermute(block, self.axis, self.pairs)

    def join(self, mine, other, dim):
        low = self.bit == 0
        return jnp.concatenate(
            (jnp.where(low, mine, other), jnp.where(low, other, mine)), axis=dim
        )

    def gather(self, block, dim):
        return self.join(block, self.trade(block), dim)

    def swap(self, block, split, dim):
        keep = pick(block, self.bit, split)
        return self.join(keep, self.trade(pick(block, 1 - self.bit, split)), dim)

    def reduce(self, block, dim):
        got = self.trade(pick(block, 1 - self.bit, dim))
        return add(pick(block, self.bit, dim), got)


def add_three(mine, one, two):
    return (mine.astype(F32) + one.astype(F32) + two.astype(F32)).astype(mine.dtype)


def add(mine, other):
    return (mine.astype(F32) + other.astype(F32)).astype(mine.dtype)


def tiles_of(length):
    return min(256, length), min(128, length)


def key_windows(labels):
    rows, step = tiles_of(labels.shape[0])
    first, last = labels[::rows], labels[rows - 1 :: rows]
    start = jnp.sum(labels[None, :] < first[:, None], axis=1)
    stop = jnp.sum(labels[None, :] <= last[:, None], axis=1)
    block = start // step
    return jnp.stack((block, (stop - 1) // step + 1 - block)).astype(jnp.int32)


def for_each_block(windows, length, run):
    rows, step = tiles_of(length)
    reach = -(-(LONGEST - 1) // step)
    most = min(length // step, rows // step + 2 * reach)

    def one(i, carry):
        q0 = pl.multiple_of(i * rows, rows)
        k0 = pl.multiple_of(windows[0, i] * step, step)
        for n in range(1, most + 1):
            pl.when(windows[1, i] == n)(functools.partial(run, q0, k0, rows, n * step))
        return carry

    lax.fori_loop(0, length // rows, one, 0)


def attend_kernel(windows, q_ref, k_ref, v_ref, lab_col, lab_row, ctx_ref, lse_ref):
    length, lanes = q_ref.shape[1:]

    def run(q0, k0, rows, span):
        q = q_ref[0, pl.ds(q0, rows), :]
        k = k_ref[0, pl.ds(k0, span), :]
        v_t = v_ref[0, pl.ds(k0, span), :].T
        same = lab_col[pl.ds(k0, span), :] == lab_row[:, pl.ds(q0, rows)]
        head = lax.broadcasted_iota(jnp.int32, (span, lanes), 1) // DH
        outs = []
        for h in range(lanes // DH):
            scores = nt(jnp.where(head == h, k, jnp.zeros_like(k)), q)
            scores = jnp.where(same, scores, MASKED)
            top = jnp.max(scores, axis=0, keepdims=True)
            shifted = jnp.exp(scores - top)
            total = jnp.sum(shifted, axis=0, keepdims=True)
            outs.append(nn(v_t[h * DH : (h + 1) * DH, :], shifted.astype(BF16)) / total)
            lse_ref[0, h : h + 1, pl.ds(q0, rows)] = top + jnp.log(total)
        ctx_ref[0, pl.ds(q0, rows), :] = jnp.concatenate(outs, axis=0).T.astype(BF16)

    for_each_block(windows, length, run)


def attend_back_kernel(
    windows, q_ref, k_ref, v_ref, do_ref, lse_ref, lab_col, lab_row, gp_ref, sum_ref, dk_acc, dv_acc
):
    length, lanes = q_ref.shape[1:]
    scale = 1.0 / math.sqrt(DH)
    dk_acc[...] = jnp.zeros_like(dk_acc)
    dv_acc[...] = jnp.zeros_like(dv_acc)
    sum_ref[...] = jnp.zeros_like(sum_ref)

    def run(q0, k0, rows, span):
        q = q_ref[0, pl.ds(q0, rows), :]
        do = do_ref[0, pl.ds(q0, rows), :]
        k = k_ref[0, pl.ds(k0, span), :]
        v = v_ref[0, pl.ds(k0, span), :]
        k_t = k.T
        same = lab_col[pl.ds(k0, span), :] == lab_row[:, pl.ds(q0, rows)]
        head = lax.broadcasted_iota(jnp.int32, (span, lanes), 1) // DH
        head_q = lax.broadcasted_iota(jnp.int32, (rows, lanes), 1) // DH
        dqs = []
        dk = dv = None
        for h in range(lanes // DH):
            only = lambda a, own: jnp.where(own == h, a, jnp.zeros_like(a))
            scores = jnp.where(same, nt(only(k, head), q), MASKED)
            prob = jnp.exp(scores - lse_ref[0, h : h + 1, pl.ds(q0, rows)])
            weighted = prob * nt(only(v, head), do)
            row_dot = jnp.sum(weighted, axis=0, keepdims=True)
            dscore = (weighted - prob * row_dot).astype(BF16)
            dv_h = nn(prob.astype(BF16), only(do, head_q))
            dk_h = nn(dscore, only(q, head_q))
            dv = dv_h if dv is None else dv + dv_h
            dk = dk_h if dk is None else dk + dk_h
            dqs.append(nn(k_t[h * DH : (h + 1) * DH, :], dscore))
        dq = jnp.concatenate(dqs, axis=0).T * scale
        gp_ref[0, pl.ds(q0, rows), :lanes] = dq.astype(BF16)
        sum_ref[0, 0:1, :] += jnp.sum(dq, axis=0, keepdims=True)
        dk_acc[pl.ds(k0, span), :] += dk
        dv_acc[pl.ds(k0, span), :] += dv

    for_each_block(windows, length, run)
    gp_ref[0, :, lanes : 2 * lanes] = dk_acc[...].astype(BF16)
    gp_ref[0, :, 2 * lanes :] = dv_acc[...].astype(BF16)
    sum_ref[0, 1:2, :] = jnp.sum(dv_acc[...], axis=0, keepdims=True)


def struct(shape, dtype):
    return jax.ShapeDtypeStruct(shape, dtype)


def fixed(a):
    return pl.BlockSpec(a.shape, lambda i, *_: (0,) * len(a.shape))


def slab(a):
    return pl.BlockSpec((1,) + a.shape[1:], lambda i, *_: (i,) + (0,) * (len(a.shape) - 1))


def launch(kernel, grid, scalars, operands, specs, outs, out_specs, scratch, flops, name, aliases=None):
    moved = sum(math.prod(a.shape) * a.dtype.itemsize for a in list(operands) + list(outs))
    return pl.pallas_call(
        kernel,
        grid_spec=pltpu.PrefetchScalarGridSpec(
            num_scalar_prefetch=len(scalars),
            grid=(grid,),
            in_specs=specs,
            out_specs=out_specs,
            scratch_shapes=scratch,
        ),
        out_shape=outs,
        input_output_aliases=aliases or {},
        cost_estimate=pl.CostEstimate(flops=flops // SHARE, transcendentals=0, bytes_accessed=moved // SHARE),
        name=name,
    )(*scalars, *operands)


def slab_from(a, first):
    return pl.BlockSpec((1,) + a.shape[1:], lambda i, *_: (first + i,) + (0,) * (len(a.shape) - 1))


def attend(windows, q, k, v, lab_col, lab_row, first, slabs):
    _, length, lanes = q.shape
    operands = [q, k, v, lab_col, lab_row]
    specs = [slab_from(q, first)] * 3 + [fixed(lab_col), fixed(lab_row)]
    outs = [struct((slabs,) + q.shape[1:], BF16), struct((slabs, lanes // DH, length), F32)]
    return launch(
        attend_kernel, slabs, [windows], operands, specs, outs, [slab(a) for a in outs], [],
        40 * slabs * length * 640 * lanes, "attend",
    )


def attend_back(windows, q, k, v, do, lse, lab_col, lab_row, first, slabs):
    _, length, lanes = q.shape
    operands = [q, k, v, do, lse, lab_col, lab_row]
    specs = [slab_from(a, first) for a in operands[:4]] + [slab(lse), fixed(lab_col), fixed(lab_row)]
    outs = [struct((slabs, length, 3 * lanes), BF16), struct((slabs, 2, lanes), F32)]
    return launch(
        attend_back_kernel, slabs, [windows], operands, specs, outs, [slab(a) for a in outs],
        [pltpu.VMEM((length, lanes), F32)] * 2, 60 * slabs * length * 640 * lanes, "attend_back",
    )


def row_tile(length):
    return min(256, length)


def product_tile(length):
    return min(512, length)


def tall(a, tile):
    if len(a.shape) == 2:
        return pl.BlockSpec((tile, a.shape[1]), lambda i, *_: (i, 0))
    return pl.BlockSpec((a.shape[0], tile, a.shape[2]), lambda i, *_: (0, i, 0))


def tall_from(a, tile, per):
    if len(a.shape) == 2:
        return pl.BlockSpec((tile, a.shape[1]), lambda i, at: (at[0] * per + i, 0))
    return pl.BlockSpec((a.shape[0], tile, a.shape[2]), lambda i, at: (0, at[0] * per + i, 0))


class Slab:
    def __init__(self, array, width, block, order):
        self.array, self.width = array, width
        shape = (array.shape[0], 1, array.shape[2], width)
        self.spec = pl.BlockSpec(shape, lambda i, at: (0, at[1 + order], 0, block))


class Whole:
    def __init__(self, array, width, block):
        self.array, self.width = array, width
        self.spec = pl.BlockSpec((array.shape[0], width), lambda i, *_: (0, block))


def arrays(slabs):
    return [w.array for w in slabs]


def specs_of(slabs):
    return [w.spec for w in slabs]


def rows_of(slab):
    shape = slab.array.shape
    return shape[0] if len(shape) == 2 else shape[0] * shape[2]


def flat(ref):
    if len(ref.shape) == 2:
        return ref[...]
    return ref[:, 0].reshape(ref.shape[0] * ref.shape[2], ref.shape[3])


def project_kernel(x_ref, b_ref, *refs):
    count = b_ref.shape[0]
    weights, (q_ref, k_ref, v_ref) = refs[:count], refs[count:]
    lanes = q_ref.shape[2]
    scale = 1.0 / math.sqrt(DH)
    x = x_ref[...]
    for i in range(count):
        projected = nn(x, weights[i][...]) + b_ref[i]
        q_ref[i] = (projected[:, :lanes].astype(BF16).astype(F32) * scale).astype(BF16)
        k_ref[i] = projected[:, lanes : 2 * lanes].astype(BF16)
        v_ref[i] = projected[:, 2 * lanes :].astype(BF16)


def project(x, weights, bias):
    length, model = x.shape
    lanes = weights[0].shape[1] // 3
    tile = row_tile(length)
    outs = [struct((len(weights), length, lanes), BF16)] * 3
    return launch(
        project_kernel, length // tile, [], [x, bias] + weights,
        [tall(x, tile), fixed(bias)] + [fixed(w) for w in weights], outs,
        [tall(a, tile) for a in outs], [], 6 * length * model * lanes * len(weights), "project",
    )


def context_out(at, stacks, weights, part, dtype):
    tile = row_tile(part)
    model = rows_of(weights[0])
    per, _, lanes = stacks[0].shape
    out = struct((part, model), dtype)

    def kernel(at_ref, *refs):
        left = jnp.concatenate([ctx[i] for ctx in refs[: len(stacks)] for i in range(per)], axis=1)
        right = jnp.concatenate([flat(w)[:, w.shape[-1] - lanes :] for w in refs[len(stacks) : -1]], axis=1)
        refs[-1][...] = nt(left, right).astype(refs[-1].dtype)

    return launch(
        kernel, part // tile, [at], list(stacks) + arrays(weights),
        [tall_from(a, tile, part // tile) for a in stacks] + specs_of(weights), [out], [tall(out, tile)], [],
        2 * part * model * lanes * len(weights), "context_out",
    )[0]


def context_back_kernel(at, ga_ref, *refs):
    weights, out_ref = refs[:-1], refs[-1]
    lanes = out_ref.shape[2]
    right = jnp.concatenate([flat(w)[:, w.shape[-1] - lanes :] for w in weights], axis=1)
    grad = nn(ga_ref[...], right).astype(BF16)
    for i in range(out_ref.shape[0]):
        out_ref[i] = grad[:, i * lanes : (i + 1) * lanes]


def context_back(at, ga, weights, lanes):
    tile = product_tile(ga.shape[0])
    count = len(weights)
    out = struct((count, ga.shape[0], lanes), BF16)
    return launch(
        context_back_kernel, ga.shape[0] // tile, [at], [ga] + arrays(weights),
        [tall(ga, tile)] + specs_of(weights), [out], [tall(out, tile)], [],
        2 * math.prod(ga.shape) * lanes * count, "context_back",
    )[0]


def ffn_in_kernel(at, y_ref, b_ref, *refs):
    count = b_ref.shape[0]
    weights, (act_ref, slope_ref) = refs[:count], refs[-2:]
    y = y_ref[...]
    for i in range(count):
        inner = nn(y, flat(weights[i])) + b_ref[i]
        share = 0.5 + 0.5 * lax.erf(inner * math.sqrt(0.5))
        density = jnp.exp(-0.5 * inner * inner) * (1.0 / math.sqrt(2.0 * math.pi))
        act_ref[i] = (inner * share).astype(BF16)
        slope_ref[i] = (share + inner * density).astype(BF16)


def place(a, tile, first):
    return pl.BlockSpec((a.shape[0], tile, a.shape[2]), lambda i, *_: (0, first + i, 0))


def ffn_in(at, y, bias, weights, ways, place_at, earlier):
    part, model = y.shape
    tile = row_tile(part)
    first = place_at * (part // tile)
    wide = bias.shape[2]
    count = len(weights)
    out = struct((count, part * ways, wide), BF16)
    anywhere = [pl.BlockSpec(memory_space=pl.ANY)] * len(earlier)
    return launch(
        ffn_in_kernel, part // tile, [at], [y, bias] + arrays(weights) + earlier,
        [tall(y, tile), fixed(bias)] + specs_of(weights) + anywhere,
        [out, out], [place(out, tile, first)] * 2, [],
        6 * part * model * wide * count, "ffn_in",
        {3 + count + i: i for i in range(len(earlier))},
    )


def ffn_out_kernel(at, act_ref, *refs):
    weights, out_ref = refs[:-1], refs[-1]
    total = nt(act_ref[0], flat(weights[0]))
    for i in range(1, len(weights)):
        total += nt(act_ref[i], flat(weights[i]))
    out_ref[...] = total.astype(out_ref.dtype)


def ffn_out(at, act, weights, part, place_at, dtype):
    tile = row_tile(part)
    model = rows_of(weights[0])
    out = struct((part, model), dtype)
    return launch(
        ffn_out_kernel, part // tile, [at], [act] + arrays(weights),
        [place(act, tile, place_at * (part // tile))] + specs_of(weights),
        [out], [tall(out, tile)], [], 2 * part * model * act.shape[0] * act.shape[2], "ffn_out",
    )[0]


def ffn_back_kernel(at, gb_ref, slope_ref, *refs):
    count = slope_ref.shape[0]
    outs, ins = refs[:count], refs[count : 2 * count]
    gi_ref, sum_ref, out_ref = refs[-3:]
    gb = gb_ref[...]
    total = None
    sums = []
    for i in range(count):
        grad = nn(gb, flat(outs[i])) * slope_ref[i].astype(F32)
        low = grad.astype(BF16)
        gi_ref[i] = low
        sums.append(jnp.sum(grad, axis=0, keepdims=True))
        term = nt(low, flat(ins[i]))
        total = term if total is None else total + term
    out_ref[...] = total.astype(out_ref.dtype)

    @pl.when(pl.program_id(0) == 0)
    def _():
        sum_ref[...] = jnp.zeros_like(sum_ref)

    for i in range(count):
        sum_ref[i] += sums[i]


def ffn_back(at, gb, slope, outs_w, ins_w, place_at, earlier, dtype):
    part, model = gb.shape
    tile = row_tile(part)
    first = place_at * (part // tile)
    count, _, wide = slope.shape
    anywhere = [pl.BlockSpec(memory_space=pl.ANY)] * len(earlier)
    outs = [struct(slope.shape, BF16), struct((count, 1, wide), F32), struct((part, model), dtype)]
    return launch(
        ffn_back_kernel, part // tile, [at], [gb, slope] + arrays(outs_w + ins_w) + earlier,
        [tall(gb, tile), place(slope, tile, first)] + specs_of(outs_w + ins_w) + anywhere,
        outs, [place(outs[0], tile, first), fixed(outs[1]), tall(outs[2], tile)], [],
        4 * part * model * wide * count, "ffn_back",
        {3 + 2 * count + i: i for i in range(len(earlier))},
    )


def inputs_back(at, stacks, weights, part, dtype):
    tile = row_tile(part)
    model = weights[0].shape[0]
    out = struct((part, model), dtype)
    per = stacks[0].shape[0]

    def kernel(at_ref, *refs):
        grads, rest, out_ref = refs[: len(stacks)], refs[len(stacks) : -1], refs[-1]
        total = None
        for i, weight in enumerate(rest):
            term = nt(grads[i // per][i % per], weight[...])
            total = term if total is None else total + term
        out_ref[...] = total.astype(out_ref.dtype)

    return launch(
        kernel, part // tile, [at], list(stacks) + weights,
        [tall_from(a, tile, part // tile) for a in stacks] + [fixed(w) for w in weights], [out], [tall(out, tile)], [],
        2 * part * model * weights[0].shape[1] * len(weights), "inputs_back",
    )[0]


def transpose_into(left_t, lefts):
    first = 0
    for left in lefts:
        left_t[:, pl.ds(first, left.shape[0])] = left[...].T
        first += left.shape[0]


def weight_grad(pairs):
    count = pairs[0][1].shape[0]
    length, model = pairs[0][1].shape[1], pairs[0][0][0].shape[1]
    wides = [right.shape[2] for _, right, _ in pairs]
    out = struct((model, sum(wides)), BF16)
    lefts = [left for group, _, _ in pairs for left in group]
    rights = [right for _, right, _ in pairs]
    many = len(pairs)

    def kernel(*refs):
        left_refs, refs = refs[: len(lefts)], refs[len(lefts) :]
        right_refs, outs = refs[:many], refs[many : many + count]
        left_t, slots, sems = refs[many + count :]
        copies = [pltpu.make_async_copy(slots.at[k % 2], outs[k], sems.at[k % 2]) for k in range(count)]

        def step(k):
            if k == 0:
                first = 0
                for n, (group, _, _) in enumerate(pairs):
                    transpose_into(left_t.at[n], left_refs[first : first + len(group)])
                    first += len(group)
            if k > 1:
                copies[k - 2].wait()
            column = 0
            for n, wide in enumerate(wides):
                slots[k % 2, :, column : column + wide] = nn(left_t[n], right_refs[n][0]).astype(BF16)
                column += wide
            copies[k].start()
            if k == count - 1:
                for last in copies[max(k - 1, 0) :]:
                    last.wait()

        for k in range(count):
            pl.when(pl.program_id(0) == k)(functools.partial(step, k))

    return launch(
        kernel, count, [], lefts + rights, [fixed(a) for a in lefts] + [slab_from(a, f) for _, a, f in pairs],
        [out] * count, [pl.BlockSpec(memory_space=pl.ANY)] * count,
        [
            pltpu.VMEM((many, model, length), BF16),
            pltpu.VMEM((2,) + out.shape, BF16),
            pltpu.SemaphoreType.DMA((2,)),
        ],
        2 * length * model * sum(wides) * count, "weight_grad",
    )


def weight_grad_shards(at, lefts, right, ring, near, seqs):
    count, length, wide = right.shape
    model = lefts[0].shape[1]
    halves = count // seqs
    own = model // (ring * near)
    out = struct((near, seqs, own, wide * halves), BF16)
    parts = len(lefts)
    block = near * own

    def kernel(at_ref, *refs):
        right_ref, outs, left_t = refs[parts], refs[parts + 1 : -1], refs[-1]

        @pl.when(pl.program_id(0) == 0)
        def _():
            transpose_into(left_t, refs[:parts])

        for k in range(ring):
            first = pl.multiple_of(((at_ref[1 + seqs] + k + ring // 2) % ring) * block, block)
            made = nn(left_t[pl.ds(first, block), :], right_ref[0]).astype(BF16).reshape(near, own, wide)
            if k == 0:
                for n in range(near):
                    outs[n][0] = made[n]
            else:
                outs[near - 1 + k][:, 0] = made

    spec = pl.BlockSpec((near, 1, own, wide), lambda i, at: (0, at[1 + i // halves], 0, i % halves))
    lone = pl.BlockSpec((1, own, wide), lambda i, at: (at[1 + i // halves], 0, i % halves))
    shape = struct(out.shape[1:], BF16)
    made = launch(
        kernel, count, [at], list(lefts) + [right], [fixed(a) for a in lefts] + [slab(right)],
        [shape] * near + [out] * (ring - 1), [lone] * near + [spec] * (ring - 1), [pltpu.VMEM((model, length), BF16)], 2 * length * model * wide * count, "weight_grad_shards",
    )
    arrays_of = [list(made[:near])] + list(made[near:])
    return arrays_of[ring // 2 :] + arrays_of[: ring // 2]


def assemble(place, pieces):
    ring = len(pieces)
    each = [p if isinstance(p, list) else [p] for p in pieces]
    shape = pieces[0].shape[1:]
    out = struct((ring,) + shape, BF16)
    operands = [a for p in each for a in p]

    def kernel(place_ref, *refs):
        sources, outs, sems = list(refs[: len(operands)]), refs[len(operands) : -1], refs[-1]
        copies = []
        for k, p in enumerate(each):
            spot = (place_ref[0] + k) % ring
            own = [sources.pop(0) for _ in p]
            for h in range(2):
                source = own[h] if len(own) == 2 else own[0].at[h]
                copies.append(pltpu.make_async_copy(source, outs[h].at[spot], sems.at[2 * k + h]))
        for copy in copies:
            copy.start()
        for copy in copies:
            copy.wait()

    anywhere = pl.BlockSpec(memory_space=pl.ANY)
    return launch(
        kernel, 1, [place], operands, [anywhere] * len(operands), [out] * 2, [fixed(out)] * 2,
        [pltpu.SemaphoreType.DMA((2 * ring,))], 0, "assemble",
    )


def last_grads(halves, lanes):
    own = halves[0][0].shape[0]
    outs = [struct((own, 6 * lanes), F32), struct((2 * lanes, own), F32)]
    operands = [a for pair in halves for a in pair]

    def kernel(*refs):
        qkv_ref, wo_ref = refs[-2:]
        for h in range(2):
            total = (refs[2 * h][...].astype(F32) + refs[2 * h + 1][...].astype(F32)).astype(BF16).astype(F32)
            for n in range(lanes // DH):
                for kind in range(3):
                    to, start = (h * lanes // DH + n) * 3 * DH + kind * DH, kind * lanes + n * DH
                    qkv_ref[:, to : to + DH] = total[:, start : start + DH]
            wo_ref[h * lanes : (h + 1) * lanes, :] = total[:, 3 * lanes :].T

    return launch(
        kernel, 1, [], operands, [fixed(a) for a in operands], outs, [fixed(a) for a in outs], [], 0, "last_grads",
    )


def norm_rows(hidden):
    mean = jnp.mean(hidden, axis=1, keepdims=True)
    square = jnp.mean(hidden * hidden, axis=1, keepdims=True)
    inv_std = lax.rsqrt(square - mean * mean + NORM_EPS)
    return (hidden - mean) * inv_std, inv_std


def norm_rows_back(incoming, centred, inv_std, gain):
    scaled = incoming * gain
    first = jnp.mean(scaled, axis=1, keepdims=True)
    second = jnp.mean(scaled * centred, axis=1, keepdims=True)
    return inv_std * (scaled - first - centred * second)


def add_sums(sum_ref, terms):
    @pl.when(pl.program_id(0) == 0)
    def _():
        sum_ref[...] = jnp.zeros_like(sum_ref)

    for i, term in enumerate(terms):
        sum_ref[i : i + 1, :] += jnp.sum(term, axis=0, keepdims=True)


def norm_a_kernel(at, mine_ref, got_ref, x_ref, vec_ref, centred_ref, inv_ref, y_ref):
    hidden = mine_ref[...] + got_ref[...].astype(F32) + x_ref[...].astype(F32) + vec_ref[0]
    centred, inv_std = norm_rows(hidden)
    centred_ref[...] = centred
    inv_ref[...] = inv_std
    y_ref[...] = (centred * vec_ref[1] + vec_ref[2]).astype(BF16)


def norm_a(at, mine, got, x, vec):
    part, model = mine.shape
    tile = row_tile(part)
    outs = [struct((part, model), F32), struct((part, 1), F32), struct((part, model), BF16)]
    return launch(
        norm_a_kernel, part // tile, [at], [mine, got, x, vec],
        [tall(mine, tile), tall(got, tile), tall_from(x, tile, part // tile), fixed(vec)],
        outs, [tall(a, tile) for a in outs], [], 20 * part * model, "norm_a",
    )


def norm_b_kernel(mine_ref, got_ref, centred_a_ref, cot_ref, vec_ref, out_ref, grad_ref, low_ref, sum_ref):
    normed = centred_a_ref[...] * vec_ref[1] + vec_ref[2]
    hidden = mine_ref[...] + got_ref[...].astype(F32) + vec_ref[3] + normed
    centred, inv_std = norm_rows(hidden)
    out_ref[...] = (centred * vec_ref[4] + vec_ref[5]).astype(BF16)
    incoming = cot_ref[...].astype(F32)
    grad = norm_rows_back(incoming, centred, inv_std, vec_ref[4])
    grad_ref[...] = grad
    low_ref[...] = grad.astype(BF16)
    add_sums(sum_ref, (grad, incoming * centred, incoming))


def norm_b(mine, got, centred_a, cot, vec):
    part, model = mine.shape
    tile = row_tile(part)
    outs = [struct((part, model), BF16), struct((part, model), F32), struct((part, model), BF16), struct((3, model), F32)]
    return launch(
        norm_b_kernel, part // tile, [], [mine, got, centred_a, cot, vec],
        [tall(a, tile) for a in (mine, got, centred_a, cot)] + [fixed(vec)],
        outs, [tall(a, tile) for a in outs[:3]] + [fixed(outs[3])], [], 40 * part * model, "norm_b",
    )


def norm_a_back_kernel(mine_ref, got_ref, gb_ref, centred_ref, inv_ref, vec_ref, grad_ref, low_ref, sum_ref):
    incoming = mine_ref[...] + got_ref[...].astype(F32) + gb_ref[...]
    centred = centred_ref[...]
    grad = norm_rows_back(incoming, centred, inv_ref[...], vec_ref[1])
    grad_ref[...] = grad
    low_ref[...] = grad.astype(BF16)
    add_sums(sum_ref, (grad, incoming * centred, incoming))


def norm_a_back(mine, got, gb, centred, inv, vec):
    part, model = mine.shape
    tile = row_tile(part)
    outs = [struct((part, model), F32), struct((part, model), BF16), struct((3, model), F32)]
    return launch(
        norm_a_back_kernel, part // tile, [], [mine, got, gb, centred, inv, vec],
        [tall(a, tile) for a in (mine, got, gb, centred, inv)] + [fixed(vec)],
        outs, [tall(a, tile) for a in outs[:2]] + [fixed(outs[2])], [], 30 * part * model, "norm_a_back",
    )


def body(
    rows,
    cols,
    tokens,
    segments,
    wqkv,
    bias_qv,
    wo,
    bias_o,
    gain_a,
    shift_a,
    w_in,
    bias_in,
    w_out,
    bias_out,
    gain_b,
    shift_b,
    cotangent,
):
    seqs, length = segments.shape
    ways = cols // seqs
    width = tokens.shape[1]
    model = width * cols
    heads = wqkv.shape[1] // (3 * DH)
    lanes = heads * DH // 2
    hid = w_in.shape[1]
    part = length // ways
    own_rows = wqkv.shape[0]
    row, col = lax.axis_index("row"), lax.axis_index(COL)
    seq, way = col // ways, col % ways
    by_seq = [Stage(COL, cols, mask * ways, col) for mask in bits_of(seqs)]
    by_way = [Stage(COL, cols, mask, col) for mask in bits_of(ways)]
    by_row = [Stage("row", rows, mask, row) for mask in bits_of(rows)]
    ns, nw, nr = len(by_seq), len(by_way), len(by_row)
    outer, near = by_row[:-1], by_row[-1]
    parts = range(ways)
    orders = [0]
    for mask in bits_of(seqs):
        orders = orders + [o ^ mask for o in orders]
    ring = rows // 2
    place = row // 2
    at = [jnp.stack([way ^ p] + [seq ^ o for o in orders] + [place]).astype(jnp.int32) for p in parts]
    here = place.reshape(1).astype(jnp.int32)

    def turn(block, step):
        return lax.ppermute(block, "row", [(i, (i + 2 * step) % rows) for i in range(rows)])

    def turn_first(piece):
        return turn(piece, 1), turn(piece, -1)

    def turn_rest(piece, got):
        plus, minus = got
        pieces = {0: piece, ring - 1: plus, 1: minus}
        for k in range(2, ring // 2):
            plus, minus = turn(plus, 1), turn(minus, -1)
            pieces[ring - k], pieces[k] = plus, minus
        pieces[ring // 2] = [turn(plus[0], 1), turn(minus[1], -1)]
        return [pieces[k] for k in range(ring)]

    def held(block, mark):
        return after(block, *mark) if mark else block

    def spread(halves):
        one, two = [h[None, None] for h in halves]
        return one, two, near.trade(one), by_seq[0].trade(two)

    def spread_rest(one, two, one_got, two_got):
        one, two = near.join(one, one_got, 0), by_seq[0].join(two, two_got, 1)
        return one, two, by_seq[0].trade(one), near.trade(two)

    def spread_end(one, two, one_got, two_got):
        return jnp.stack((by_seq[0].join(one, one_got, 1), near.join(two, two_got, 0)))

    def whole_shards(pieces):
        return [g.reshape((rows,) + g.shape[2:]) for g in assemble(here, pieces)]

    def last_first(one, two):
        twos = [two]
        for stage in by_seq:
            twos = twos + [stage.trade(b) for b in twos]
        return near.trade(one), twos[1:]

    def last_rest(one, two, one_got, two_got):
        def whole(block, got):
            return near.join(block, got, nr - 1).reshape(model, -1)

        twos = [two] + two_got
        twos_got = [near.trade(b) for b in twos]
        ones = [whole(one, one_got)]
        for stage in by_seq:
            ones = ones + [stage.trade(b) for b in ones]
        return ones, twos, twos_got

    def last_end(ones, twos, twos_got):
        twos = [near.join(b, g, nr - 1).reshape(model, -1) for b, g in zip(twos, twos_got)]
        return [b for j in range(seqs) for b in (ones[j], twos[j])]

    def halves_of(weight):
        half = weight.shape[1] // 2
        return weight[:, :half], weight[:, half:]

    by_kind = wqkv.reshape(own_rows, 2, heads // 2, 3, DH).transpose(1, 0, 3, 2, 4)
    by_kind = by_kind.reshape(2, own_rows, -1)
    def by_bits(pieces):
        return [b.reshape((2,) * (nr - 1) + (1,) + b.shape[1:]) for b in assemble(here, pieces)]

    wo_t = halves_of(wo.T)
    qkv_got = turn_first(by_kind)
    in_piece = jnp.stack([jnp.concatenate((a, b), axis=1) for a, b in zip(halves_of(w_in), wo_t)])
    qkv_pieces = turn_rest(by_kind, qkv_got)
    in_got = turn_first(after(in_piece, *qkv_got))
    out_shards = spread(halves_of(w_out.T))
    out_first = out_shards[2:]
    out_shards = spread_rest(*out_shards)
    far_qkv = by_bits(qkv_pieces)

    labels = lax.dynamic_slice_in_dim(segments, seq, 1, 0)[0]
    windows = key_windows(labels)
    lab_col, lab_row = labels[:, None], labels[None, :]

    def exchange(array, split, whole, mark=()):
        blocks = [array]
        for stage in split + whole:
            both = blocks[0] if len(blocks) == 1 else jnp.concatenate(blocks, axis=1)
            if stage in split:
                both = both.reshape(2, both.shape[0] // 2, both.shape[1])
                mine, sent = pick(both, stage.bit, 0)[0], pick(both, 1 - stage.bit, 0)[0]
            else:
                mine = sent = both
            got = held(stage.trade(sent), mark)
            low = stage.bit == 0
            blocks = [
                half
                for i in range(len(blocks))
                for a, b in [(mine[:, i * width : (i + 1) * width], got[:, i * width : (i + 1) * width])]
                for half in (jnp.where(low, a, b), jnp.where(low, b, a))
            ]
        return jnp.concatenate(blocks, axis=1)

    def to_features(array):
        blocks = [array]
        for stage in by_seq + by_way:
            half = blocks[0].shape[1] // 2
            both = blocks[0] if len(blocks) == 1 else jnp.concatenate(blocks, axis=0)
            mine = lax.dynamic_slice_in_dim(both, stage.bit * half, half, 1)
            got = stage.trade(lax.dynamic_slice_in_dim(both, (1 - stage.bit) * half, half, 1))
            low = stage.bit == 0
            count = array.shape[0]
            blocks = [
                half_rows
                for i in range(len(blocks))
                for a, b in [(mine[i * count : (i + 1) * count], got[i * count : (i + 1) * count])]
                for half_rows in (jnp.where(low, a, b), jnp.where(low, b, a))
            ]
        return jnp.concatenate(blocks, axis=0)

    def widen(array, whole):
        for stage in whole:
            got = stage.trade(array)
            low = stage.bit == 0
            array = jnp.concatenate(
                [
                    half
                    for i in range(array.shape[1] // width)
                    for a, b in [(array[:, i * width : (i + 1) * width], got[:, i * width : (i + 1) * width])]
                    for half in (jnp.where(low, a, b), jnp.where(low, b, a))
                ],
                axis=1,
            )
        return array

    half_x = exchange(after(tokens, *out_first), by_seq, [])
    vectors = jnp.concatenate(
        [v.reshape(-1, width) for v in (bias_o, gain_a, shift_a, bias_out, gain_b, shift_b, bias_qv, bias_in)]
    )
    vectors = after(vectors, half_x)
    whole_x = widen(half_x, by_way)
    pairs = [vectors]
    for stage in by_seq:
        pairs = pairs + [stage.trade(v) for v in pairs]
    blocks = [vectors[:6]]
    for i, stage in enumerate(by_seq):
        got = jnp.concatenate([p[:6] for p in pairs[1 << i : 2 << i]], axis=1)
        low = stage.bit == 0
        both = jnp.concatenate(blocks, axis=1)
        blocks = [
            half
            for k in range(len(blocks))
            for a, b in [(both[:, k * width : (k + 1) * width], got[:, k * width : (k + 1) * width])]
            for half in (jnp.where(low, a, b), jnp.where(low, b, a))
        ]
    for stage in by_way:
        both = jnp.concatenate(blocks, axis=1)
        got = stage.trade(both)
        low = stage.bit == 0
        blocks = [
            half
            for k in range(len(blocks))
            for a, b in [(both[:, k * width : (k + 1) * width], got[:, k * width : (k + 1) * width])]
            for half in (jnp.where(low, a, b), jnp.where(low, b, a))
        ]
    vec = jnp.concatenate(blocks, axis=1).astype(F32)[:, None, :]
    nq = bias_qv.shape[0] // width
    q_biases, in_biases = [], []
    for j in range(seqs):
        both = pairs[j][6 : 6 + nq].astype(F32).reshape(2, heads // 2, 2, DH)
        both = both.transpose(0, 2, 1, 3).reshape(2, 2, lanes)
        q_biases.append(jnp.concatenate((both[:, :1], jnp.zeros_like(both[:, :1]), both[:, 1:]), axis=1))
        in_biases.append(pairs[j][6 + nq :].astype(F32).reshape(2, 1, hid // 2))
    q_bias = jnp.concatenate(q_biases, axis=0).reshape(2 * seqs, 1, 3 * lanes)
    in_bias = jnp.concatenate(in_biases, axis=0)

    qkv_first = last_first(*far_qkv)
    qkv_rest = last_rest(*far_qkv, *qkv_first)
    in_pieces = turn_rest(in_piece, [after(g, *far_qkv) for g in in_got])
    far_in = by_bits(in_pieces)
    in_first = last_first(*[after(b, qkv_rest[0][0], *qkv_first[1]) for b in far_in])
    qkv_all = last_end(*qkv_rest)
    out_piece = spread_end(*out_shards[:2], *[after(b, *far_qkv) for b in out_shards[2:]])
    out_got = turn_first(after(out_piece, *far_in))
    pairs_of = [(j, h) for j in range(seqs) for h in range(2)]

    def gather_parts(own):
        blocks = {0: own}
        for mask, stage in zip(bits_of(ways), by_way):
            for p in list(blocks):
                blocks[p ^ mask] = stage.trade(blocks[p])
        return [blocks[p] for p in parts]

    def scatter_parts(make):
        terms = {p: make(p, F32 if p == 0 else BF16) for p in reversed(parts)}
        for mask, stage in list(zip(bits_of(ways), by_way))[:-1]:
            for p in [q for q in terms if q & mask]:
                got = stage.trade(terms.pop(p))
                terms[p ^ mask] = add(terms[p ^ mask], got)
        return terms[0], by_way[-1].trade(terms[1])

    def whole_rows(blocks):
        blocks = list(blocks)
        for mask, stage in zip(reversed(bits_of(ways)), reversed(by_way)):
            low = stage.bit == 0
            for p in parts:
                if not p & mask:
                    a, b = blocks[p], blocks[p | mask]
                    blocks[p], blocks[p | mask] = jnp.where(low, a, b), jnp.where(low, b, a)
        return jnp.concatenate(blocks, axis=0)

    def fold_start(block):
        block = block.reshape((2,) * nr + (own_rows, -1))
        return block, near.trade(pick(block, 1 - near.bit, nr - 1))

    def fold_end(block, got):
        return add(pick(block, near.bit, nr - 1), got)

    def across_start(blocks):
        count = len(blocks) // 2
        return blocks[:count], [by_seq[-1].trade(b) for b in blocks[count:]]

    def across_end(mine, gots):
        blocks = [add(m, g) for m, g in zip(mine, gots)]
        for stage in list(reversed(by_seq))[1:]:
            count = len(blocks) // 2
            blocks = [add(blocks[j], stage.trade(blocks[count + j])) for j in range(count)]
        return blocks[0]

    def scatter_far(one, two, marks=(), split=False):
        for n, (i, stage) in enumerate(reversed(list(enumerate(outer)))):
            halves = (one, two)
            sent = jnp.stack([pick(b, 1 - stage.bit, i) for b in halves])
            got = held(stage.trade(sent), marks[n] if n < len(marks) else ())
            if split and n == len(outer) - 1:
                return [(pick(b, stage.bit, i).reshape(own_rows, -1), got[h].reshape(own_rows, -1)) for h, b in enumerate(halves)]
            one, two = [add(pick(b, stage.bit, i), got[h]) for h, b in enumerate(halves)]
        return one.reshape(own_rows, -1).astype(F32), two.reshape(own_rows, -1).astype(F32)

    q, k, v = project(whole_x, qkv_all, q_bias)
    contexts, lses, ready = [], [], [in_first[0], *in_first[1]]
    for j in range(seqs):
        context, lse = attend(windows, after(q, *contexts, *ready) if j else q, k, v, lab_col, lab_row, 2 * j, 2)
        contexts, lses = contexts + [context], lses + [lse]
        if j == 0:
            in_first = after(in_first[0], context), [after(b, context) for b in in_first[1]]
            in_rest = last_rest(*far_in, *in_first)
    contexts = [after(c, *contexts, *out_got) for c in contexts]
    out_pieces = turn_rest(out_piece, [after(g, contexts[-1]) for g in out_got])
    in_blocks = last_end(*in_rest)
    in_all = [Whole(b, hid // 2, 0) for b in in_blocks]
    aligned = lanes % 128 == 0
    wo_all = [Whole(b, lanes, hid // 2 // lanes) if aligned else Whole(b, b.shape[1], 0) for b in in_blocks]
    mine, got = scatter_parts(lambda p, dtype: context_out(at[p], contexts, wo_all, part, dtype))
    centred_a, inv_a, y = norm_a(at[0], mine, got, whole_x, vec)
    y_parts = gather_parts(y)
    earlier = []
    for p in parts:
        earlier = ffn_in(at[0], y_parts[p], in_bias, in_all, ways, p, list(earlier))
    active, slope = earlier
    whole_out = whole_shards([after(p, active) if not isinstance(p, list) else [after(b, active) for b in p] for p in out_pieces])
    out_all = [Slab(whole_out[h], hid // 2, 0, j) for j, h in pairs_of]
    cot = exchange(after(cotangent, contexts[-1]), by_seq + by_way, [], (active,))
    mine, got = scatter_parts(lambda p, dtype: ffn_out(at[0], active, out_all, part, p, dtype))
    output, grad_b, gb, sums_b = norm_b(mine, got, centred_a, cot, vec)

    gb_parts = gather_parts(gb)
    output = to_features(after(output, gb_parts[-1]))
    chunks = weight_grad_shards(at[0], gb_parts, active, ring, 2, seqs)
    plus, minus = turn(chunks[ring // 2][0], 1), turn(chunks[ring // 2][1], -1)
    tie = (chunks[0],)
    terms, sum_in, earlier = {}, 0.0, []
    for p in parts:
        grad_inner, sums, terms[p] = ffn_back(
            at[0], after(gb_parts[p], *tie), slope, out_all, in_all, p, earlier, F32 if p == 0 else BF16
        )
        earlier = [grad_inner]
        if p == parts[-1]:
            firsts = plus, minus
            plus, minus = after(plus, grad_inner), after(minus, grad_inner)
            for far in reversed(range(1, ring // 2)):
                up, down = chunks[far], chunks[ring - far]
                if far == ring // 2 - 1:
                    up = jnp.stack((add(up[0], plus), up[1]))
                    down = jnp.stack((down[0], add(down[1], minus)))
                else:
                    up, down = add(up, plus), add(down, minus)
                tie = (up, down)
                plus, minus = turn(up, 1), turn(down, -1)
        sum_in = sum_in + sums
    mine, got = scatter_parts(lambda p, dtype: terms[p])
    grad_w_in = weight_grad([(y_parts, after(grad_inner, *firsts), 0)])
    grad_a, ga, sums_a = norm_a_back(mine, got, after(grad_b, grad_w_in[0]), centred_a, inv_a, vec)
    whole_ga = whole_rows(gather_parts(ga))
    grad_context = context_back(at[0], whole_ga, wo_all, lanes)
    ones_mine, ones_got = across_start(grad_w_in[0::2])
    twos_in = [fold_start(b) for b in grad_w_in[1::2]]
    gots = ones_got + [g for _, g in twos_in] + [plus, minus]
    stacks, sums_p, made, later = {}, [], {}, []
    ready = grad_context
    for j in reversed(range(seqs)):
        projected, sums = attend_back(
            windows, q, k, v, after(grad_context, ready), lses[j], lab_col, lab_row, 2 * j, 2
        )
        if j == seqs - 1:
            projected = after(projected, *gots)
        made[j] = weight_grad([([whole_x], projected, 0), ([whole_ga], contexts[j], 0)])
        ready = made[j][0]
        stacks[j], sums_p = projected, [sums] + sums_p
        if j == seqs - 1:
            ones_got, twos_got = [held(g, (projected,)) for g in ones_got], [held(g, (projected,)) for _, g in twos_in]
            one_in = fold_start(across_end(ones_mine, ones_got))
            two_in = across_start([fold_end(b, g) for (b, _), g in zip(twos_in, twos_got)])
            later = [one_in[1]] + two_in[1]
            out_sum = add_three(chunks[0], after(plus, projected), after(minus, projected))
            out_sum = near.reduce(after(out_sum, ready), 0)
    sum_projected = jnp.concatenate(sums_p, axis=0)
    for stage in reversed(by_seq):
        out_sum = stage.reduce(after(out_sum, ready), 1)
    halves_in = fold_end(one_in[0], held(one_in[1], (ready,))), across_end(two_in[0], [held(g, (ready,)) for g in two_in[1]])

    per_hidden = []
    for j in range(seqs):
        two = sum_projected[2 * j : 2 * j + 2].reshape(2, 2, heads // 2, DH).transpose(0, 2, 1, 3)
        per_hidden += [two.reshape(-1), sum_in[2 * j : 2 * j + 2].reshape(-1)]
    small = jnp.concatenate([sums_a.reshape(-1), sums_b.reshape(-1)] + per_hidden)
    for stage in outer:
        small = small + stage.trade(small)

    ones_mine, ones_got = across_start([made[j][0] for j in range(seqs)])
    twos_last = [fold_start(made[j][1]) for j in range(seqs)]
    ones_got = [held(g, (ready,)) for g in ones_got]
    one_last = fold_start(across_end(ones_mine, ones_got))
    stacks = [after(stacks[j], ready, *later, one_last[0], small) for j in range(seqs)]
    term = {1: inputs_back(at[1], stacks, qkv_all, part, BF16)} if ways == 2 else {}
    small = held(small, tuple(term.values()))
    small_got = near.trade(small)
    twos_got = [held(g, tuple(term.values())) for _, g in twos_last]
    two_last = across_start([fold_end(b, g) for (b, _), g in zip(twos_last, twos_got)])
    tied = [after(a, *twos_got, *term.values()) for a in stacks]
    mine, got = scatter_parts(
        lambda p, dtype: term[p] if p in term else inputs_back(at[p], tied, qkv_all, part, dtype)
    )
    in_halves = scatter_far(*halves_in, [tuple(term.values())])
    mine = after(mine, one_last[1], *two_last[1], *in_halves, small_got)
    grad_tokens = to_features((mine + got.astype(F32) + grad_a).astype(BF16)).astype(F32)
    halves_last = fold_end(*one_last), across_end(*two_last)
    finals = scatter_far(*halves_last, split=True)
    grad_qkv, grad_wo = last_grads(finals, lanes)
    small = after(small, *halves_last) + small_got
    block = small[: 6 * model].reshape(6, model)
    per_hidden = list(small[6 * model :].reshape(seqs, -1))
    for stage in by_seq + by_way:
        half = block.shape[1] // 2
        got = stage.trade(lax.dynamic_slice_in_dim(block, (1 - stage.bit) * half, half, 1))
        block = lax.dynamic_slice_in_dim(block, stage.bit * half, half, 1) + got
    for stage in reversed(by_seq):
        count = len(per_hidden) // 2
        per_hidden = [per_hidden[j] + stage.trade(per_hidden[count + j]) for j in range(count)]
    sums = jnp.concatenate((per_hidden[0], block.reshape(-1)))

    nqv = bias_qv.shape[0]
    sum_qv, sum_in = sums[:nqv], sums[nqv : nqv + hid]
    rest = sums[nqv + hid :].reshape(6, width)
    return (
        output,
        grad_tokens,
        grad_qkv,
        sum_qv,
        grad_wo,
        rest[0],
        rest[1],
        rest[2],
        jnp.concatenate(in_halves, axis=1),
        sum_in,
        out_sum.reshape(own_rows, hid).astype(F32).T,
        rest[3],
        rest[4],
        rest[5],
    )


def solution(mesh):
    rows, cols = mesh.shape["row"], mesh.shape["col"]
    tile, across, down, flat_col = P("row", COL), P("row", None), P(COL, "row"), P(COL)
    in_specs = (
        tile, across, tile, flat_col, down, flat_col, flat_col, flat_col,
        tile, flat_col, down, flat_col, flat_col, flat_col, tile,
    )
    out_specs = (
        tile, tile, tile, flat_col, down, flat_col, flat_col, flat_col,
        tile, flat_col, down, flat_col, flat_col, flat_col,
    )

    def run(*args):
        seqs = args[1].shape[0] // rows
        fine = jax.sharding.Mesh(mesh.devices.reshape(rows, seqs, cols // seqs), ("row",) + COL)

        def layer(*local):
            return body(rows, cols, *local)

        return jax.shard_map(layer, mesh=fine, in_specs=in_specs, out_specs=out_specs, check_vma=False)(*args)

    return run
```

```python
import functools
import math

import jax
import jax.numpy as jnp
from jax import lax
from jax.experimental import pallas as pl
from jax.experimental.pallas import tpu as pltpu
from jax.sharding import PartitionSpec as P

DH = 64
NORM_EPS = 1e-06
MASKED = -1000000000.0
LONGEST = 256
COL = ("seq", "way")
SHARE = 1
F32 = jnp.float32
BF16 = jnp.bfloat16


def nn(left, right):
    return lax.dot_general(left, right, (((1,), (0,)), ((), ())), preferred_element_type=F32)


def nt(left, right):
    return lax.dot_general(left, right, (((1,), (1,)), ((), ())), preferred_element_type=F32)


def tn(left, right):
    return lax.dot_general(left, right, (((0,), (0,)), ((), ())), preferred_element_type=F32)


def after(block, *others):
    return lax.optimization_barrier((block,) + others)[0]


def pick(block, bit, dim):
    return lax.dynamic_slice_in_dim(block, bit, 1, dim)


def bits_of(count):
    return [1 << b for b in reversed(range(count.bit_length() - 1))]


class Stage:
    def __init__(self, axis, count, mask, index):
        self.axis, self.pairs = axis, [(i, i ^ mask) for i in range(count)]
        self.bit = (index // mask) % 2

    def trade(self, block):
        return lax.ppermute(block, self.axis, self.pairs)

    def join(self, mine, other, dim):
        low = self.bit == 0
        return jnp.concatenate(
            (jnp.where(low, mine, other), jnp.where(low, other, mine)), axis=dim
        )

    def gather(self, block, dim):
        return self.join(block, self.trade(block), dim)

    def swap(self, block, split, dim):
        keep = pick(block, self.bit, split)
        return self.join(keep, self.trade(pick(block, 1 - self.bit, split)), dim)

    def reduce(self, block, dim):
        got = self.trade(pick(block, 1 - self.bit, dim))
        return add(pick(block, self.bit, dim), got)


def add_three(mine, one, two):
    return (mine.astype(F32) + one.astype(F32) + two.astype(F32)).astype(mine.dtype)


def add(mine, other):
    return (mine.astype(F32) + other.astype(F32)).astype(mine.dtype)


def tiles_of(length):
    return min(256, length), min(128, length)


def key_windows(labels):
    rows, step = tiles_of(labels.shape[0])
    first, last = labels[::rows], labels[rows - 1 :: rows]
    start = jnp.sum(labels[None, :] < first[:, None], axis=1)
    stop = jnp.sum(labels[None, :] <= last[:, None], axis=1)
    block = start // step
    return jnp.stack((block, (stop - 1) // step + 1 - block)).astype(jnp.int32)


def for_each_block(windows, length, run):
    rows, step = tiles_of(length)
    reach = -(-(LONGEST - 1) // step)
    most = min(length // step, rows // step + 2 * reach)

    def one(i, carry):
        q0 = pl.multiple_of(i * rows, rows)
        k0 = pl.multiple_of(windows[0, i] * step, step)
        for n in range(1, most + 1):
            pl.when(windows[1, i] == n)(functools.partial(run, q0, k0, rows, n * step))
        return carry

    lax.fori_loop(0, length // rows, one, 0)


def attend_kernel(windows, q_ref, k_ref, v_ref, lab_col, lab_row, ctx_ref, lse_ref):
    length, lanes = q_ref.shape[1:]

    def run(q0, k0, rows, span):
        q = q_ref[0, pl.ds(q0, rows), :]
        k = k_ref[0, pl.ds(k0, span), :]
        v_t = v_ref[0, pl.ds(k0, span), :].T
        same = lab_col[pl.ds(k0, span), :] == lab_row[:, pl.ds(q0, rows)]
        head = lax.broadcasted_iota(jnp.int32, (span, lanes), 1) // DH
        outs = []
        for h in range(lanes // DH):
            scores = nt(jnp.where(head == h, k, jnp.zeros_like(k)), q)
            scores = jnp.where(same, scores, MASKED)
            top = jnp.max(scores, axis=0, keepdims=True)
            shifted = jnp.exp(scores - top)
            total = jnp.sum(shifted, axis=0, keepdims=True)
            outs.append(nn(v_t[h * DH : (h + 1) * DH, :], shifted.astype(BF16)) / total)
            lse_ref[0, h : h + 1, pl.ds(q0, rows)] = top + jnp.log(total)
        ctx_ref[0, pl.ds(q0, rows), :] = jnp.concatenate(outs, axis=0).T.astype(BF16)

    for_each_block(windows, length, run)


def attend_back_kernel(
    windows, q_ref, k_ref, v_ref, do_ref, lse_ref, lab_col, lab_row, gp_ref, sum_ref, dk_acc, dv_acc
):
    length, lanes = q_ref.shape[1:]
    scale = 1.0 / math.sqrt(DH)
    dk_acc[...] = jnp.zeros_like(dk_acc)
    dv_acc[...] = jnp.zeros_like(dv_acc)
    sum_ref[...] = jnp.zeros_like(sum_ref)

    def run(q0, k0, rows, span):
        q = q_ref[0, pl.ds(q0, rows), :]
        do = do_ref[0, pl.ds(q0, rows), :]
        k = k_ref[0, pl.ds(k0, span), :]
        v = v_ref[0, pl.ds(k0, span), :]
        k_t = k.T
        same = lab_col[pl.ds(k0, span), :] == lab_row[:, pl.ds(q0, rows)]
        head = lax.broadcasted_iota(jnp.int32, (span, lanes), 1) // DH
        head_q = lax.broadcasted_iota(jnp.int32, (rows, lanes), 1) // DH
        dqs = []
        dk = dv = None
        for h in range(lanes // DH):
            only = lambda a, own: jnp.where(own == h, a, jnp.zeros_like(a))
            scores = jnp.where(same, nt(only(k, head), q), MASKED)
            prob = jnp.exp(scores - lse_ref[0, h : h + 1, pl.ds(q0, rows)])
            weighted = prob * nt(only(v, head), do)
            row_dot = jnp.sum(weighted, axis=0, keepdims=True)
            dscore = (weighted - prob * row_dot).astype(BF16)
            dv_h = nn(prob.astype(BF16), only(do, head_q))
            dk_h = nn(dscore, only(q, head_q))
            dv = dv_h if dv is None else dv + dv_h
            dk = dk_h if dk is None else dk + dk_h
            dqs.append(nn(k_t[h * DH : (h + 1) * DH, :], dscore))
        dq = jnp.concatenate(dqs, axis=0).T * scale
        gp_ref[0, pl.ds(q0, rows), :lanes] = dq.astype(BF16)
        sum_ref[0, 0:1, :] += jnp.sum(dq, axis=0, keepdims=True)
        dk_acc[pl.ds(k0, span), :] += dk
        dv_acc[pl.ds(k0, span), :] += dv

    for_each_block(windows, length, run)
    gp_ref[0, :, lanes : 2 * lanes] = dk_acc[...].astype(BF16)
    gp_ref[0, :, 2 * lanes :] = dv_acc[...].astype(BF16)
    sum_ref[0, 1:2, :] = jnp.sum(dv_acc[...], axis=0, keepdims=True)


def struct(shape, dtype):
    return jax.ShapeDtypeStruct(shape, dtype)


def fixed(a):
    return pl.BlockSpec(a.shape, lambda i, *_: (0,) * len(a.shape))


def slab(a):
    return pl.BlockSpec((1,) + a.shape[1:], lambda i, *_: (i,) + (0,) * (len(a.shape) - 1))


def launch(kernel, grid, scalars, operands, specs, outs, out_specs, scratch, flops, name, aliases=None):
    moved = sum(math.prod(a.shape) * a.dtype.itemsize for a in list(operands) + list(outs))
    return pl.pallas_call(
        kernel,
        grid_spec=pltpu.PrefetchScalarGridSpec(
            num_scalar_prefetch=len(scalars),
            grid=(grid,),
            in_specs=specs,
            out_specs=out_specs,
            scratch_shapes=scratch,
        ),
        out_shape=outs,
        input_output_aliases=aliases or {},
        cost_estimate=pl.CostEstimate(flops=flops // SHARE, transcendentals=0, bytes_accessed=moved // SHARE),
        name=name,
    )(*scalars, *operands)


def slab_from(a, first):
    return pl.BlockSpec((1,) + a.shape[1:], lambda i, *_: (first + i,) + (0,) * (len(a.shape) - 1))


def attend(windows, q, k, v, lab_col, lab_row, first, slabs):
    _, length, lanes = q.shape
    operands = [q, k, v, lab_col, lab_row]
    specs = [slab_from(q, first)] * 3 + [fixed(lab_col), fixed(lab_row)]
    outs = [struct((slabs,) + q.shape[1:], BF16), struct((slabs, lanes // DH, length), F32)]
    return launch(
        attend_kernel, slabs, [windows], operands, specs, outs, [slab(a) for a in outs], [],
        40 * slabs * length * 640 * lanes, "attend",
    )


def attend_back(windows, q, k, v, do, lse, lab_col, lab_row, first, slabs):
    _, length, lanes = q.shape
    operands = [q, k, v, do, lse, lab_col, lab_row]
    specs = [slab_from(a, first) for a in operands[:4]] + [slab(lse), fixed(lab_col), fixed(lab_row)]
    outs = [struct((slabs, length, 3 * lanes), BF16), struct((slabs, 2, lanes), F32)]
    return launch(
        attend_back_kernel, slabs, [windows], operands, specs, outs, [slab(a) for a in outs],
        [pltpu.VMEM((length, lanes), F32)] * 2, 6 * slabs * length * 640 * lanes, "attend_back",
    )


def row_tile(length):
    return min(256, length)


def product_tile(length):
    return min(512, length)


def tall(a, tile):
    if len(a.shape) == 2:
        return pl.BlockSpec((tile, a.shape[1]), lambda i, *_: (i, 0))
    return pl.BlockSpec((a.shape[0], tile, a.shape[2]), lambda i, *_: (0, i, 0))


def tall_from(a, tile, per):
    if len(a.shape) == 2:
        return pl.BlockSpec((tile, a.shape[1]), lambda i, at: (at[0] * per + i, 0))
    return pl.BlockSpec((a.shape[0], tile, a.shape[2]), lambda i, at: (0, at[0] * per + i, 0))


class Slab:
    def __init__(self, array, width, block, order):
        self.array, self.width = array, width
        shape = (array.shape[0], 1, array.shape[2], width)
        self.spec = pl.BlockSpec(shape, lambda i, at: (0, at[1 + order], 0, block))


class Whole:
    def __init__(self, array, width, block):
        self.array, self.width = array, width
        self.spec = pl.BlockSpec((array.shape[0], width), lambda i, *_: (0, block))


def arrays(slabs):
    return [w.array for w in slabs]


def specs_of(slabs):
    return [w.spec for w in slabs]


def rows_of(slab):
    shape = slab.array.shape
    return shape[0] if len(shape) == 2 else shape[0] * shape[2]


def flat(ref):
    if len(ref.shape) == 2:
        return ref[...]
    return ref[:, 0].reshape(ref.shape[0] * ref.shape[2], ref.shape[3])


def project_kernel(x_ref, b_ref, *refs):
    count = b_ref.shape[0]
    weights, (q_ref, k_ref, v_ref) = refs[:count], refs[count:]
    lanes = q_ref.shape[2]
    scale = 1.0 / math.sqrt(DH)
    x = x_ref[...]
    for i in range(count):
        projected = nn(x, weights[i][...]) + b_ref[i]
        q_ref[i] = (projected[:, :lanes].astype(BF16).astype(F32) * scale).astype(BF16)
        k_ref[i] = projected[:, lanes : 2 * lanes].astype(BF16)
        v_ref[i] = projected[:, 2 * lanes :].astype(BF16)


def project(x, weights, bias):
    length, model = x.shape
    lanes = weights[0].shape[1] // 3
    tile = row_tile(length)
    outs = [struct((len(weights), length, lanes), BF16)] * 3
    return launch(
        project_kernel, length // tile, [], [x, bias] + weights,
        [tall(x, tile), fixed(bias)] + [fixed(w) for w in weights], outs,
        [tall(a, tile) for a in outs], [], 6 * length * model * lanes * len(weights), "project",
    )


def context_out(at, stacks, weights, part, dtype):
    tile = row_tile(part)
    model = rows_of(weights[0])
    per, _, lanes = stacks[0].shape
    out = struct((part, model), dtype)

    def kernel(at_ref, *refs):
        left = jnp.concatenate([ctx[i] for ctx in refs[: len(stacks)] for i in range(per)], axis=1)
        right = jnp.concatenate([flat(w)[:, w.shape[-1] - lanes :] for w in refs[len(stacks) : -1]], axis=1)
        refs[-1][...] = nt(left, right).astype(refs[-1].dtype)

    return launch(
        kernel, part // tile, [at], list(stacks) + arrays(weights),
        [tall_from(a, tile, part // tile) for a in stacks] + specs_of(weights), [out], [tall(out, tile)], [],
        2 * part * model * lanes * len(weights), "context_out",
    )[0]


def context_back_kernel(at, ga_ref, *refs):
    weights, out_ref = refs[:-1], refs[-1]
    lanes = out_ref.shape[2]
    right = jnp.concatenate([flat(w)[:, w.shape[-1] - lanes :] for w in weights], axis=1)
    grad = nn(ga_ref[...], right).astype(BF16)
    for i in range(out_ref.shape[0]):
        out_ref[i] = grad[:, i * lanes : (i + 1) * lanes]


def context_back(at, ga, weights, lanes):
    tile = product_tile(ga.shape[0])
    count = len(weights)
    out = struct((count, ga.shape[0], lanes), BF16)
    return launch(
        context_back_kernel, ga.shape[0] // tile, [at], [ga] + arrays(weights),
        [tall(ga, tile)] + specs_of(weights), [out], [tall(out, tile)], [],
        2 * math.prod(ga.shape) * lanes * count, "context_back",
    )[0]


def ffn_in_kernel(at, y_ref, b_ref, *refs):
    count = b_ref.shape[0]
    weights, (act_ref, slope_ref) = refs[:count], refs[-2:]
    y = y_ref[...]
    for i in range(count):
        inner = nn(y, flat(weights[i])) + b_ref[i]
        share = 0.5 + 0.5 * lax.erf(inner * math.sqrt(0.5))
        density = jnp.exp(-0.5 * inner * inner) * (1.0 / math.sqrt(2.0 * math.pi))
        act_ref[i] = (inner * share).astype(BF16)
        slope_ref[i] = (share + inner * density).astype(BF16)


def place(a, tile, first):
    return pl.BlockSpec((a.shape[0], tile, a.shape[2]), lambda i, *_: (0, first + i, 0))


def ffn_in(at, y, bias, weights, ways, place_at, earlier):
    part, model = y.shape
    tile = row_tile(part)
    first = place_at * (part // tile)
    wide = bias.shape[2]
    count = len(weights)
    out = struct((count, part * ways, wide), BF16)
    anywhere = [pl.BlockSpec(memory_space=pl.ANY)] * len(earlier)
    return launch(
        ffn_in_kernel, part // tile, [at], [y, bias] + arrays(weights) + earlier,
        [tall(y, tile), fixed(bias)] + specs_of(weights) + anywhere,
        [out, out], [place(out, tile, first)] * 2, [],
        6 * part * model * wide * count, "ffn_in",
        {3 + count + i: i for i in range(len(earlier))},
    )


def ffn_out_kernel(at, act_ref, *refs):
    weights, out_ref = refs[:-1], refs[-1]
    total = nt(act_ref[0], flat(weights[0]))
    for i in range(1, len(weights)):
        total += nt(act_ref[i], flat(weights[i]))
    out_ref[...] = total.astype(out_ref.dtype)


def ffn_out(at, act, weights, part, place_at, dtype):
    tile = row_tile(part)
    model = rows_of(weights[0])
    out = struct((part, model), dtype)
    return launch(
        ffn_out_kernel, part // tile, [at], [act] + arrays(weights),
        [place(act, tile, place_at * (part // tile))] + specs_of(weights),
        [out], [tall(out, tile)], [], 2 * part * model * act.shape[0] * act.shape[2], "ffn_out",
    )[0]


def ffn_back_kernel(at, gb_ref, slope_ref, *refs):
    count = slope_ref.shape[0]
    outs, ins = refs[:count], refs[count : 2 * count]
    gi_ref, sum_ref, out_ref = refs[-3:]
    gb = gb_ref[...]
    total = None
    sums = []
    for i in range(count):
        grad = nn(gb, flat(outs[i])) * slope_ref[i].astype(F32)
        low = grad.astype(BF16)
        gi_ref[i] = low
        sums.append(jnp.sum(grad, axis=0, keepdims=True))
        term = nt(low, flat(ins[i]))
        total = term if total is None else total + term
    out_ref[...] = total.astype(out_ref.dtype)

    @pl.when(pl.program_id(0) == 0)
    def _():
        sum_ref[...] = jnp.zeros_like(sum_ref)

    for i in range(count):
        sum_ref[i] += sums[i]


def ffn_back(at, gb, slope, outs_w, ins_w, place_at, earlier, dtype):
    part, model = gb.shape
    tile = row_tile(part)
    first = place_at * (part // tile)
    count, _, wide = slope.shape
    anywhere = [pl.BlockSpec(memory_space=pl.ANY)] * len(earlier)
    outs = [struct(slope.shape, BF16), struct((count, 1, wide), F32), struct((part, model), dtype)]
    return launch(
        ffn_back_kernel, part // tile, [at], [gb, slope] + arrays(outs_w + ins_w) + earlier,
        [tall(gb, tile), place(slope, tile, first)] + specs_of(outs_w + ins_w) + anywhere,
        outs, [place(outs[0], tile, first), fixed(outs[1]), tall(outs[2], tile)], [],
        4 * part * model * wide * count, "ffn_back",
        {3 + 2 * count + i: i for i in range(len(earlier))},
    )


def inputs_back(at, stacks, weights, part, dtype):
    tile = row_tile(part)
    model = weights[0].shape[0]
    out = struct((part, model), dtype)
    per = stacks[0].shape[0]

    def kernel(at_ref, *refs):
        grads, rest, out_ref = refs[: len(stacks)], refs[len(stacks) : -1], refs[-1]
        total = None
        for i, weight in enumerate(rest):
            term = nt(grads[i // per][i % per], weight[...])
            total = term if total is None else total + term
        out_ref[...] = total.astype(out_ref.dtype)

    return launch(
        kernel, part // tile, [at], list(stacks) + weights,
        [tall_from(a, tile, part // tile) for a in stacks] + [fixed(w) for w in weights], [out], [tall(out, tile)], [],
        2 * part * model * weights[0].shape[1] * len(weights), "inputs_back",
    )[0]


def transpose_into(left_t, lefts):
    first = 0
    for left in lefts:
        left_t[:, pl.ds(first, left.shape[0])] = left[...].T
        first += left.shape[0]


def weight_grad(pairs):
    count = pairs[0][1].shape[0]
    length, model = pairs[0][1].shape[1], pairs[0][0][0].shape[1]
    wides = [right.shape[2] for _, right, _ in pairs]
    out = struct((model, sum(wides)), BF16)
    lefts = [left for group, _, _ in pairs for left in group]
    rights = [right for _, right, _ in pairs]
    many = len(pairs)

    def kernel(*refs):
        left_refs, refs = refs[: len(lefts)], refs[len(lefts) :]
        right_refs, outs = refs[:many], refs[many : many + count]
        left_t, slots, sems = refs[many + count :]
        copies = [pltpu.make_async_copy(slots.at[k % 2], outs[k], sems.at[k % 2]) for k in range(count)]

        def step(k):
            if k == 0:
                first = 0
                for n, (group, _, _) in enumerate(pairs):
                    transpose_into(left_t.at[n], left_refs[first : first + len(group)])
                    first += len(group)
            if k > 1:
                copies[k - 2].wait()
            column = 0
            for n, wide in enumerate(wides):
                slots[k % 2, :, column : column + wide] = nn(left_t[n], right_refs[n][0]).astype(BF16)
                column += wide
            copies[k].start()
            if k == count - 1:
                for last in copies[max(k - 1, 0) :]:
                    last.wait()

        for k in range(count):
            pl.when(pl.program_id(0) == k)(functools.partial(step, k))

    return launch(
        kernel, count, [], lefts + rights, [fixed(a) for a in lefts] + [slab_from(a, f) for _, a, f in pairs],
        [out] * count, [pl.BlockSpec(memory_space=pl.ANY)] * count,
        [
            pltpu.VMEM((many, model, length), BF16),
            pltpu.VMEM((2,) + out.shape, BF16),
            pltpu.SemaphoreType.DMA((2,)),
        ],
        2 * length * model * sum(wides) * count, "weight_grad",
    )


def weight_grad_shards(at, lefts, right, ring, near, seqs):
    count, length, wide = right.shape
    model = lefts[0].shape[1]
    halves = count // seqs
    own = model // (ring * near)
    out = struct((near, seqs, own, wide * halves), BF16)
    parts = len(lefts)
    block = near * own

    def kernel(at_ref, *refs):
        right_ref, outs, left_t = refs[parts], refs[parts + 1 : -1], refs[-1]

        @pl.when(pl.program_id(0) == 0)
        def _():
            transpose_into(left_t, refs[:parts])

        for k in range(ring):
            first = pl.multiple_of(((at_ref[1 + seqs] + k + ring // 2) % ring) * block, block)
            made = nn(left_t[pl.ds(first, block), :], right_ref[0]).astype(BF16).reshape(near, own, wide)
            if k == 0:
                for n in range(near):
                    outs[n][0] = made[n]
            else:
                outs[near - 1 + k][:, 0] = made

    spec = pl.BlockSpec((near, 1, own, wide), lambda i, at: (0, at[1 + i // halves], 0, i % halves))
    lone = pl.BlockSpec((1, own, wide), lambda i, at: (at[1 + i // halves], 0, i % halves))
    shape = struct(out.shape[1:], BF16)
    made = launch(
        kernel, count, [at], list(lefts) + [right], [fixed(a) for a in lefts] + [slab(right)],
        [shape] * near + [out] * (ring - 1), [lone] * near + [spec] * (ring - 1), [pltpu.VMEM((model, length), BF16)], 2 * length * model * wide * count, "weight_grad_shards",
    )
    arrays_of = [list(made[:near])] + list(made[near:])
    return arrays_of[ring // 2 :] + arrays_of[: ring // 2]


def assemble(place, pieces):
    ring = len(pieces)
    each = [p if isinstance(p, list) else [p] for p in pieces]
    shape = pieces[0].shape[1:]
    out = struct((ring,) + shape, BF16)
    operands = [a for p in each for a in p]

    def kernel(place_ref, *refs):
        sources, outs, sems = list(refs[: len(operands)]), refs[len(operands) : -1], refs[-1]
        copies = []
        for k, p in enumerate(each):
            spot = (place_ref[0] + k) % ring
            own = [sources.pop(0) for _ in p]
            for h in range(2):
                source = own[h] if len(own) == 2 else own[0].at[h]
                copies.append(pltpu.make_async_copy(source, outs[h].at[spot], sems.at[2 * k + h]))
        for copy in copies:
            copy.start()
        for copy in copies:
            copy.wait()

    anywhere = pl.BlockSpec(memory_space=pl.ANY)
    return launch(
        kernel, 1, [place], operands, [anywhere] * len(operands), [out] * 2, [fixed(out)] * 2,
        [pltpu.SemaphoreType.DMA((2 * ring,))], 0, "assemble",
    )


def last_grads(halves, lanes):
    own = halves[0][0].shape[0]
    outs = [struct((own, 6 * lanes), F32), struct((2 * lanes, own), F32)]
    operands = [a for pair in halves for a in pair]

    def kernel(*refs):
        qkv_ref, wo_ref = refs[-2:]
        for h in range(2):
            total = (refs[2 * h][...].astype(F32) + refs[2 * h + 1][...].astype(F32)).astype(BF16).astype(F32)
            for n in range(lanes // DH):
                for kind in range(3):
                    to, start = (h * lanes // DH + n) * 3 * DH + kind * DH, kind * lanes + n * DH
                    qkv_ref[:, to : to + DH] = total[:, start : start + DH]
            wo_ref[h * lanes : (h + 1) * lanes, :] = total[:, 3 * lanes :].T

    return launch(
        kernel, 1, [], operands, [fixed(a) for a in operands], outs, [fixed(a) for a in outs], [], 0, "last_grads",
    )


def norm_rows(hidden):
    mean = jnp.mean(hidden, axis=1, keepdims=True)
    square = jnp.mean(hidden * hidden, axis=1, keepdims=True)
    inv_std = lax.rsqrt(square - mean * mean + NORM_EPS)
    return (hidden - mean) * inv_std, inv_std


def norm_rows_back(incoming, centred, inv_std, gain):
    scaled = incoming * gain
    first = jnp.mean(scaled, axis=1, keepdims=True)
    second = jnp.mean(scaled * centred, axis=1, keepdims=True)
    return inv_std * (scaled - first - centred * second)


def add_sums(sum_ref, terms):
    @pl.when(pl.program_id(0) == 0)
    def _():
        sum_ref[...] = jnp.zeros_like(sum_ref)

    for i, term in enumerate(terms):
        sum_ref[i : i + 1, :] += jnp.sum(term, axis=0, keepdims=True)


def norm_a_kernel(at, mine_ref, got_ref, x_ref, vec_ref, centred_ref, inv_ref, y_ref):
    hidden = mine_ref[...] + got_ref[...].astype(F32) + x_ref[...].astype(F32) + vec_ref[0]
    centred, inv_std = norm_rows(hidden)
    centred_ref[...] = centred
    inv_ref[...] = inv_std
    y_ref[...] = (centred * vec_ref[1] + vec_ref[2]).astype(BF16)


def norm_a(at, mine, got, x, vec):
    part, model = mine.shape
    tile = row_tile(part)
    outs = [struct((part, model), F32), struct((part, 1), F32), struct((part, model), BF16)]
    return launch(
        norm_a_kernel, part // tile, [at], [mine, got, x, vec],
        [tall(mine, tile), tall(got, tile), tall_from(x, tile, part // tile), fixed(vec)],
        outs, [tall(a, tile) for a in outs], [], 20 * part * model, "norm_a",
    )


def norm_b_kernel(mine_ref, got_ref, centred_a_ref, cot_ref, vec_ref, out_ref, grad_ref, low_ref, sum_ref):
    normed = centred_a_ref[...] * vec_ref[1] + vec_ref[2]
    hidden = mine_ref[...] + got_ref[...].astype(F32) + vec_ref[3] + normed
    centred, inv_std = norm_rows(hidden)
    out_ref[...] = (centred * vec_ref[4] + vec_ref[5]).astype(BF16)
    incoming = cot_ref[...].astype(F32)
    grad = norm_rows_back(incoming, centred, inv_std, vec_ref[4])
    grad_ref[...] = grad
    low_ref[...] = grad.astype(BF16)
    add_sums(sum_ref, (grad, incoming * centred, incoming))


def norm_b(mine, got, centred_a, cot, vec):
    part, model = mine.shape
    tile = row_tile(part)
    outs = [struct((part, model), BF16), struct((part, model), F32), struct((part, model), BF16), struct((3, model), F32)]
    return launch(
        norm_b_kernel, part // tile, [], [mine, got, centred_a, cot, vec],
        [tall(a, tile) for a in (mine, got, centred_a, cot)] + [fixed(vec)],
        outs, [tall(a, tile) for a in outs[:3]] + [fixed(outs[3])], [], 40 * part * model, "norm_b",
    )


def norm_a_back_kernel(mine_ref, got_ref, gb_ref, centred_ref, inv_ref, vec_ref, grad_ref, low_ref, sum_ref):
    incoming = mine_ref[...] + got_ref[...].astype(F32) + gb_ref[...]
    centred = centred_ref[...]
    grad = norm_rows_back(incoming, centred, inv_ref[...], vec_ref[1])
    grad_ref[...] = grad
    low_ref[...] = grad.astype(BF16)
    add_sums(sum_ref, (grad, incoming * centred, incoming))


def norm_a_back(mine, got, gb, centred, inv, vec):
    part, model = mine.shape
    tile = row_tile(part)
    outs = [struct((part, model), F32), struct((part, model), BF16), struct((3, model), F32)]
    return launch(
        norm_a_back_kernel, part // tile, [], [mine, got, gb, centred, inv, vec],
        [tall(a, tile) for a in (mine, got, gb, centred, inv)] + [fixed(vec)],
        outs, [tall(a, tile) for a in outs[:2]] + [fixed(outs[2])], [], 30 * part * model, "norm_a_back",
    )


def body(
    rows,
    cols,
    tokens,
    segments,
    wqkv,
    bias_qv,
    wo,
    bias_o,
    gain_a,
    shift_a,
    w_in,
    bias_in,
    w_out,
    bias_out,
    gain_b,
    shift_b,
    cotangent,
):
    seqs, length = segments.shape
    ways = cols // seqs
    width = tokens.shape[1]
    model = width * cols
    heads = wqkv.shape[1] // (3 * DH)
    lanes = heads * DH // 2
    hid = w_in.shape[1]
    part = length // ways
    own_rows = wqkv.shape[0]
    row, col = lax.axis_index("row"), lax.axis_index(COL)
    seq, way = col // ways, col % ways
    by_seq = [Stage(COL, cols, mask * ways, col) for mask in bits_of(seqs)]
    by_way = [Stage(COL, cols, mask, col) for mask in bits_of(ways)]
    by_row = [Stage("row", rows, mask, row) for mask in bits_of(rows)]
    ns, nw, nr = len(by_seq), len(by_way), len(by_row)
    outer, near = by_row[:-1], by_row[-1]
    parts = range(ways)
    orders = [0]
    for mask in bits_of(seqs):
        orders = orders + [o ^ mask for o in orders]
    ring = rows // 2
    place = row // 2
    at = [jnp.stack([way ^ p] + [seq ^ o for o in orders] + [place]).astype(jnp.int32) for p in parts]
    here = place.reshape(1).astype(jnp.int32)

    def turn(block, step):
        return lax.ppermute(block, "row", [(i, (i + 2 * step) % rows) for i in range(rows)])

    def turn_first(piece):
        return turn(piece, 1), turn(piece, -1)

    def turn_rest(piece, got):
        plus, minus = got
        pieces = {0: piece, ring - 1: plus, 1: minus}
        for k in range(2, ring // 2):
            plus, minus = turn(plus, 1), turn(minus, -1)
            pieces[ring - k], pieces[k] = plus, minus
        pieces[ring // 2] = [turn(plus[0], 1), turn(minus[1], -1)]
        return [pieces[k] for k in range(ring)]

    def held(block, mark):
        return after(block, *mark) if mark else block

    def spread(halves):
        one, two = [h[None, None] for h in halves]
        return one, two, near.trade(one), by_seq[0].trade(two)

    def spread_rest(one, two, one_got, two_got):
        one, two = near.join(one, one_got, 0), by_seq[0].join(two, two_got, 1)
        return one, two, by_seq[0].trade(one), near.trade(two)

    def spread_end(one, two, one_got, two_got):
        return jnp.stack((by_seq[0].join(one, one_got, 1), near.join(two, two_got, 0)))

    def whole_shards(pieces):
        return [g.reshape((rows,) + g.shape[2:]) for g in assemble(here, pieces)]

    def last_first(one, two):
        twos = [two]
        for stage in by_seq:
            twos = twos + [stage.trade(b) for b in twos]
        return near.trade(one), twos[1:]

    def last_rest(one, two, one_got, two_got):
        def whole(block, got):
            return near.join(block, got, nr - 1).reshape(model, -1)

        twos = [two] + two_got
        twos_got = [near.trade(b) for b in twos]
        ones = [whole(one, one_got)]
        for stage in by_seq:
            ones = ones + [stage.trade(b) for b in ones]
        return ones, twos, twos_got

    def last_end(ones, twos, twos_got):
        twos = [near.join(b, g, nr - 1).reshape(model, -1) for b, g in zip(twos, twos_got)]
        return [b for j in range(seqs) for b in (ones[j], twos[j])]

    def halves_of(weight):
        half = weight.shape[1] // 2
        return weight[:, :half], weight[:, half:]

    by_kind = wqkv.reshape(own_rows, 2, heads // 2, 3, DH).transpose(1, 0, 3, 2, 4)
    by_kind = by_kind.reshape(2, own_rows, -1)
    def by_bits(pieces):
        return [b.reshape((2,) * (nr - 1) + (1,) + b.shape[1:]) for b in assemble(here, pieces)]

    wo_t = halves_of(wo.T)
    qkv_got = turn_first(by_kind)
    in_piece = jnp.stack([jnp.concatenate((a, b), axis=1) for a, b in zip(halves_of(w_in), wo_t)])
    qkv_pieces = turn_rest(by_kind, qkv_got)
    in_got = turn_first(after(in_piece, *qkv_got))
    out_shards = spread(halves_of(w_out.T))
    out_first = out_shards[2:]
    out_shards = spread_rest(*out_shards)
    far_qkv = by_bits(qkv_pieces)

    labels = lax.dynamic_slice_in_dim(segments, seq, 1, 0)[0]
    windows = key_windows(labels)
    lab_col, lab_row = labels[:, None], labels[None, :]

    def exchange(array, split, whole, mark=()):
        blocks = [array]
        for stage in split + whole:
            both = blocks[0] if len(blocks) == 1 else jnp.concatenate(blocks, axis=1)
            if stage in split:
                both = both.reshape(2, both.shape[0] // 2, both.shape[1])
                mine, sent = pick(both, stage.bit, 0)[0], pick(both, 1 - stage.bit, 0)[0]
            else:
                mine = sent = both
            got = held(stage.trade(sent), mark)
            low = stage.bit == 0
            blocks = [
                half
                for i in range(len(blocks))
                for a, b in [(mine[:, i * width : (i + 1) * width], got[:, i * width : (i + 1) * width])]
                for half in (jnp.where(low, a, b), jnp.where(low, b, a))
            ]
        return jnp.concatenate(blocks, axis=1)

    def to_features(array):
        blocks = [array]
        for stage in by_seq + by_way:
            half = blocks[0].shape[1] // 2
            both = blocks[0] if len(blocks) == 1 else jnp.concatenate(blocks, axis=0)
            mine = lax.dynamic_slice_in_dim(both, stage.bit * half, half, 1)
            got = stage.trade(lax.dynamic_slice_in_dim(both, (1 - stage.bit) * half, half, 1))
            low = stage.bit == 0
            count = array.shape[0]
            blocks = [
                half_rows
                for i in range(len(blocks))
                for a, b in [(mine[i * count : (i + 1) * count], got[i * count : (i + 1) * count])]
                for half_rows in (jnp.where(low, a, b), jnp.where(low, b, a))
            ]
        return jnp.concatenate(blocks, axis=0)

    def widen(array, whole):
        for stage in whole:
            got = stage.trade(array)
            low = stage.bit == 0
            array = jnp.concatenate(
                [
                    half
                    for i in range(array.shape[1] // width)
                    for a, b in [(array[:, i * width : (i + 1) * width], got[:, i * width : (i + 1) * width])]
                    for half in (jnp.where(low, a, b), jnp.where(low, b, a))
                ],
                axis=1,
            )
        return array

    half_x = exchange(after(tokens, *out_first), by_seq, [])
    vectors = jnp.concatenate(
        [v.reshape(-1, width) for v in (bias_o, gain_a, shift_a, bias_out, gain_b, shift_b, bias_qv, bias_in)]
    )
    vectors = after(vectors, half_x)
    whole_x = widen(half_x, by_way)
    pairs = [vectors]
    for stage in by_seq:
        pairs = pairs + [stage.trade(v) for v in pairs]
    blocks = [vectors[:6]]
    for i, stage in enumerate(by_seq):
        got = jnp.concatenate([p[:6] for p in pairs[1 << i : 2 << i]], axis=1)
        low = stage.bit == 0
        both = jnp.concatenate(blocks, axis=1)
        blocks = [
            half
            for k in range(len(blocks))
            for a, b in [(both[:, k * width : (k + 1) * width], got[:, k * width : (k + 1) * width])]
            for half in (jnp.where(low, a, b), jnp.where(low, b, a))
        ]
    for stage in by_way:
        both = jnp.concatenate(blocks, axis=1)
        got = stage.trade(both)
        low = stage.bit == 0
        blocks = [
            half
            for k in range(len(blocks))
            for a, b in [(both[:, k * width : (k + 1) * width], got[:, k * width : (k + 1) * width])]
            for half in (jnp.where(low, a, b), jnp.where(low, b, a))
        ]
    vec = jnp.concatenate(blocks, axis=1).astype(F32)[:, None, :]
    nq = bias_qv.shape[0] // width
    q_biases, in_biases = [], []
    for j in range(seqs):
        both = pairs[j][6 : 6 + nq].astype(F32).reshape(2, heads // 2, 2, DH)
        both = both.transpose(0, 2, 1, 3).reshape(2, 2, lanes)
        q_biases.append(jnp.concatenate((both[:, :1], jnp.zeros_like(both[:, :1]), both[:, 1:]), axis=1))
        in_biases.append(pairs[j][6 + nq :].astype(F32).reshape(2, 1, hid // 2))
    q_bias = jnp.concatenate(q_biases, axis=0).reshape(2 * seqs, 1, 3 * lanes)
    in_bias = jnp.concatenate(in_biases, axis=0)

    qkv_first = last_first(*far_qkv)
    qkv_rest = last_rest(*far_qkv, *qkv_first)
    in_pieces = turn_rest(in_piece, [after(g, *far_qkv) for g in in_got])
    far_in = by_bits(in_pieces)
    in_first = last_first(*[after(b, qkv_rest[0][0], *qkv_first[1]) for b in far_in])
    qkv_all = last_end(*qkv_rest)
    out_piece = spread_end(*out_shards[:2], *[after(b, *far_qkv) for b in out_shards[2:]])
    out_got = turn_first(after(out_piece, *far_in))
    pairs_of = [(j, h) for j in range(seqs) for h in range(2)]

    def gather_parts(own):
        blocks = {0: own}
        for mask, stage in zip(bits_of(ways), by_way):
            for p in list(blocks):
                blocks[p ^ mask] = stage.trade(blocks[p])
        return [blocks[p] for p in parts]

    def scatter_parts(make):
        terms = {p: make(p, F32 if p == 0 else BF16) for p in reversed(parts)}
        for mask, stage in list(zip(bits_of(ways), by_way))[:-1]:
            for p in [q for q in terms if q & mask]:
                got = stage.trade(terms.pop(p))
                terms[p ^ mask] = add(terms[p ^ mask], got)
        return terms[0], by_way[-1].trade(terms[1])

    def whole_rows(blocks):
        blocks = list(blocks)
        for mask, stage in zip(reversed(bits_of(ways)), reversed(by_way)):
            low = stage.bit == 0
            for p in parts:
                if not p & mask:
                    a, b = blocks[p], blocks[p | mask]
                    blocks[p], blocks[p | mask] = jnp.where(low, a, b), jnp.where(low, b, a)
        return jnp.concatenate(blocks, axis=0)

    def fold_start(block):
        block = block.reshape((2,) * nr + (own_rows, -1))
        return block, near.trade(pick(block, 1 - near.bit, nr - 1))

    def fold_end(block, got):
        return add(pick(block, near.bit, nr - 1), got)

    def across_start(blocks):
        count = len(blocks) // 2
        return blocks[:count], [by_seq[-1].trade(b) for b in blocks[count:]]

    def across_end(mine, gots):
        blocks = [add(m, g) for m, g in zip(mine, gots)]
        for stage in list(reversed(by_seq))[1:]:
            count = len(blocks) // 2
            blocks = [add(blocks[j], stage.trade(blocks[count + j])) for j in range(count)]
        return blocks[0]

    def scatter_far(one, two, marks=(), split=False):
        for n, (i, stage) in enumerate(reversed(list(enumerate(outer)))):
            halves = (one, two)
            sent = jnp.stack([pick(b, 1 - stage.bit, i) for b in halves])
            got = held(stage.trade(sent), marks[n] if n < len(marks) else ())
            if split and n == len(outer) - 1:
                return [(pick(b, stage.bit, i).reshape(own_rows, -1), got[h].reshape(own_rows, -1)) for h, b in enumerate(halves)]
            one, two = [add(pick(b, stage.bit, i), got[h]) for h, b in enumerate(halves)]
        return one.reshape(own_rows, -1).astype(F32), two.reshape(own_rows, -1).astype(F32)

    q, k, v = project(whole_x, qkv_all, q_bias)
    contexts, lses, ready = [], [], [in_first[0], *in_first[1]]
    for j in range(seqs):
        context, lse = attend(windows, after(q, *contexts, *ready) if j else q, k, v, lab_col, lab_row, 2 * j, 2)
        contexts, lses = contexts + [context], lses + [lse]
        if j == 0:
            in_first = after(in_first[0], context), [after(b, context) for b in in_first[1]]
            in_rest = last_rest(*far_in, *in_first)
    contexts = [after(c, *contexts, *out_got) for c in contexts]
    out_pieces = turn_rest(out_piece, [after(g, contexts[-1]) for g in out_got])
    in_blocks = last_end(*in_rest)
    in_all = [Whole(b, hid // 2, 0) for b in in_blocks]
    aligned = lanes % 128 == 0
    wo_all = [Whole(b, lanes, hid // 2 // lanes) if aligned else Whole(b, b.shape[1], 0) for b in in_blocks]
    mine, got = scatter_parts(lambda p, dtype: context_out(at[p], contexts, wo_all, part, dtype))
    centred_a, inv_a, y = norm_a(at[0], mine, got, whole_x, vec)
    y_parts = gather_parts(y)
    earlier = []
    for p in parts:
        earlier = ffn_in(at[0], y_parts[p], in_bias, in_all, ways, p, list(earlier))
    active, slope = earlier
    whole_out = whole_shards([after(p, active) if not isinstance(p, list) else [after(b, active) for b in p] for p in out_pieces])
    out_all = [Slab(whole_out[h], hid // 2, 0, j) for j, h in pairs_of]
    cot = exchange(after(cotangent, contexts[-1]), by_seq + by_way, [], (active,))
    mine, got = scatter_parts(lambda p, dtype: ffn_out(at[0], active, out_all, part, p, dtype))
    output, grad_b, gb, sums_b = norm_b(mine, got, centred_a, cot, vec)

    gb_parts = gather_parts(gb)
    output = to_features(after(output, gb_parts[-1]))
    chunks = weight_grad_shards(at[0], gb_parts, active, ring, 2, seqs)
    plus, minus = turn(chunks[ring // 2][0], 1), turn(chunks[ring // 2][1], -1)
    tie = (chunks[0],)
    terms, sum_in, earlier = {}, 0.0, []
    for p in parts:
        grad_inner, sums, terms[p] = ffn_back(
            at[0], after(gb_parts[p], *tie), slope, out_all, in_all, p, earlier, F32 if p == 0 else BF16
        )
        earlier = [grad_inner]
        if p == parts[-1]:
            firsts = plus, minus
            plus, minus = after(plus, grad_inner), after(minus, grad_inner)
            for far in reversed(range(1, ring // 2)):
                up, down = chunks[far], chunks[ring - far]
                if far == ring // 2 - 1:
                    up = jnp.stack((add(up[0], plus), up[1]))
                    down = jnp.stack((down[0], add(down[1], minus)))
                else:
                    up, down = add(up, plus), add(down, minus)
                tie = (up, down)
                plus, minus = turn(up, 1), turn(down, -1)
        sum_in = sum_in + sums
    mine, got = scatter_parts(lambda p, dtype: terms[p])
    grad_w_in = weight_grad([(y_parts, after(grad_inner, *firsts), 0)])
    grad_a, ga, sums_a = norm_a_back(mine, got, after(grad_b, grad_w_in[0]), centred_a, inv_a, vec)
    whole_ga = whole_rows(gather_parts(ga))
    grad_context = context_back(at[0], whole_ga, wo_all, lanes)
    ones_mine, ones_got = across_start(grad_w_in[0::2])
    twos_in = [fold_start(b) for b in grad_w_in[1::2]]
    gots = ones_got + [g for _, g in twos_in] + [plus, minus]
    stacks, sums_p, made, later = {}, [], {}, []
    ready = grad_context
    for j in reversed(range(seqs)):
        projected, sums = attend_back(
            windows, q, k, v, after(grad_context, ready), lses[j], lab_col, lab_row, 2 * j, 2
        )
        if j == seqs - 1:
            projected = after(projected, *gots)
        made[j] = weight_grad([([whole_x], projected, 0), ([whole_ga], contexts[j], 0)])
        ready = made[j][0]
        stacks[j], sums_p = projected, [sums] + sums_p
        if j == seqs - 1:
            ones_got, twos_got = [held(g, (projected,)) for g in ones_got], [held(g, (projected,)) for _, g in twos_in]
            one_in = fold_start(across_end(ones_mine, ones_got))
            two_in = across_start([fold_end(b, g) for (b, _), g in zip(twos_in, twos_got)])
            later = [one_in[1]] + two_in[1]
            out_sum = add_three(chunks[0], after(plus, projected), after(minus, projected))
            out_sum = near.reduce(after(out_sum, ready), 0)
    sum_projected = jnp.concatenate(sums_p, axis=0)
    for stage in reversed(by_seq):
        out_sum = stage.reduce(after(out_sum, ready), 1)
    halves_in = fold_end(one_in[0], held(one_in[1], (ready,))), across_end(two_in[0], [held(g, (ready,)) for g in two_in[1]])

    per_hidden = []
    for j in range(seqs):
        two = sum_projected[2 * j : 2 * j + 2].reshape(2, 2, heads // 2, DH).transpose(0, 2, 1, 3)
        per_hidden += [two.reshape(-1), sum_in[2 * j : 2 * j + 2].reshape(-1)]
    small = jnp.concatenate([sums_a.reshape(-1), sums_b.reshape(-1)] + per_hidden)
    for stage in outer:
        small = small + stage.trade(small)

    ones_mine, ones_got = across_start([made[j][0] for j in range(seqs)])
    twos_last = [fold_start(made[j][1]) for j in range(seqs)]
    ones_got = [held(g, (ready,)) for g in ones_got]
    one_last = fold_start(across_end(ones_mine, ones_got))
    stacks = [after(stacks[j], ready, *later, one_last[0], small) for j in range(seqs)]
    term = {1: inputs_back(at[1], stacks, qkv_all, part, BF16)} if ways == 2 else {}
    small = held(small, tuple(term.values()))
    small_got = near.trade(small)
    twos_got = [held(g, tuple(term.values())) for _, g in twos_last]
    two_last = across_start([fold_end(b, g) for (b, _), g in zip(twos_last, twos_got)])
    tied = [after(a, *twos_got, *term.values()) for a in stacks]
    mine, got = scatter_parts(
        lambda p, dtype: term[p] if p in term else inputs_back(at[p], tied, qkv_all, part, dtype)
    )
    in_halves = scatter_far(*halves_in, [tuple(term.values())])
    mine = after(mine, one_last[1], *two_last[1], *in_halves, small_got)
    grad_tokens = to_features((mine + got.astype(F32) + grad_a).astype(BF16)).astype(F32)
    halves_last = fold_end(*one_last), across_end(*two_last)
    finals = scatter_far(*halves_last, split=True)
    grad_qkv, grad_wo = last_grads(finals, lanes)
    small = after(small, *halves_last) + small_got
    block = small[: 6 * model].reshape(6, model)
    per_hidden = list(small[6 * model :].reshape(seqs, -1))
    for stage in by_seq + by_way:
        half = block.shape[1] // 2
        got = stage.trade(lax.dynamic_slice_in_dim(block, (1 - stage.bit) * half, half, 1))
        block = lax.dynamic_slice_in_dim(block, stage.bit * half, half, 1) + got
    for stage in reversed(by_seq):
        count = len(per_hidden) // 2
        per_hidden = [per_hidden[j] + stage.trade(per_hidden[count + j]) for j in range(count)]
    sums = jnp.concatenate((per_hidden[0], block.reshape(-1)))

    nqv = bias_qv.shape[0]
    sum_qv, sum_in = sums[:nqv], sums[nqv : nqv + hid]
    rest = sums[nqv + hid :].reshape(6, width)
    return (
        output,
        grad_tokens,
        grad_qkv,
        sum_qv,
        grad_wo,
        rest[0],
        rest[1],
        rest[2],
        jnp.concatenate(in_halves, axis=1),
        sum_in,
        out_sum.reshape(own_rows, hid).astype(F32).T,
        rest[3],
        rest[4],
        rest[5],
    )


def solution(mesh):
    rows, cols = mesh.shape["row"], mesh.shape["col"]
    tile, across, down, flat_col = P("row", COL), P("row", None), P(COL, "row"), P(COL)
    in_specs = (
        tile, across, tile, flat_col, down, flat_col, flat_col, flat_col,
        tile, flat_col, down, flat_col, flat_col, flat_col, tile,
    )
    out_specs = (
        tile, tile, tile, flat_col, down, flat_col, flat_col, flat_col,
        tile, flat_col, down, flat_col, flat_col, flat_col,
    )

    def run(*args):
        seqs = args[1].shape[0] // rows
        fine = jax.sharding.Mesh(mesh.devices.reshape(rows, seqs, cols // seqs), ("row",) + COL)

        def layer(*local):
            return body(rows, cols, *local)

        return jax.shard_map(layer, mesh=fine, in_specs=in_specs, out_specs=out_specs, check_vma=False)(*args)

    return run
```
